128 devices in a mesh: wide: 16 (over z, y), narrow: 8 (over x, core).
Axes of the slice: x: 4, y: 4, z: 4, core: 2. Of those that a mesh axis runs over, the one named last changes fastest.
Arguments:
- features: bfloat16 [512, 65536], P('narrow', 'wide'), may hold values from -36 to 36
- edge_tiles: bfloat16 [512, 12, 128, 128], P('wide'), may hold values from 0 to 22, as said below
- block_lists: int32 [512, 12], P('wide'), may hold values from 0 to 63, as said below
- send_lists: int32 [16, 16, 2], P('wide'), may hold values from 0 to 31
- train_ids: int32 [8192], P('wide'), may hold values from 0 to 4095, as said below
- owners: int32 [8192, 1], P('wide'), may hold values from 0 to 127; in each aligned block of 512 rows (0 to 511, 512 to 1023, ...) at most 8 rows name the same one
- cotangent: bfloat16 [4, 512, 8192], P(None, 'narrow', 'wide'), may hold values from -6 to 6
- query_weight: bfloat16 [512, 512], replicated, may hold values from -8 to 8
- key_weight: bfloat16 [512, 512], replicated, may hold values from -8 to 8
- value_weight: bfloat16 [512, 512], replicated, may hold values from -0.25 to 0.25
- out_weight: bfloat16 [512, 512], replicated, may hold values from -0.25 to 0.25
- up_weight: bfloat16 [2048, 512], replicated, may hold values from -0.25 to 0.25
- down_weight: bfloat16 [2048, 512], replicated, may hold values from -0.125 to 0.125
Outputs:
- hop_tokens: bfloat16 [3, 512, 65536], P(None, 'narrow', 'wide')
- grad_attn: float32 [2048, 512], P(('wide', 'narrow'))
- grad_up: float32 [2048, 512], P(('wide', 'narrow'))
- grad_down: float32 [2048, 512], P(('wide', 'narrow'))
The draws below stay inside these ranges and needn't reach their ends.
Inputs may be any that keep to these rules, and one draw needn't show every extreme that they name: edge_tiles[b, k, s, t] weighs the edge from node s of block source[b, k] to node t of block b; the diagonal of every edge_tiles[b, 0] is positive. block_lists[b, 0] = b mod 32; within every part each position 32 to 63 appears. `train_ids`: distinct within a part. `owners`: at most 8 of the 512 training nodes of one part name the same owner; every owner is named by some node.
All inputs are finite; a program needn't handle non-finite values.
Results may differ from the reference program's by a relative error of at most 0.025.
Values may be sent and summed in bfloat16 or wider, within the bound.
No kernel may reach another device: no remote copies, remote signals or barrier semaphores. Data moves between devices by JAX's collectives and lax.ppermute only.
A program may use at most 128 MiB of HBM per device.

```python
import math
import jax
import jax.numpy as jnp
import numpy as np
from jax import lax

D = 512
FF = 2048
HEADS = 8
HOPS = 3
TOKS = 4
BLK = 128
K = 12
SEND = 2
NB = 32
MB = 128
PARTS_SIZE = 16
NODES_PART = 4096
NODES = 65536
TRAIN_PART = 512
TRAINS = 8192
DEVICES = 128


def draw_features(key, part):
    key_rows, key_cols, key_base = jax.random.split(key, 3)
    row_scale = jnp.exp(jax.random.uniform(key_rows, (D, 1), jnp.float32, math.log(0.3), math.log(3.0)))
    col_scale = jnp.exp(jax.random.uniform(key_cols, (1, NODES), jnp.float32, math.log(0.3), math.log(3.0)))
    base_draw = jnp.clip(jax.random.normal(key_base, (D, NODES), jnp.float32), -4.0, 4.0)
    return (base_draw * row_scale * col_scale).astype(jnp.bfloat16)


def draw_edge_tiles(key, part):
    key_mask, key_weight, key_self = jax.random.split(key, 3)
    tile_shape = (PARTS_SIZE * NB, K, BLK, BLK)
    present = jax.random.uniform(key_mask, tile_shape, jnp.float32) < 0.125
    weight = jnp.exp(jax.random.uniform(key_weight, tile_shape, jnp.float32, math.log(0.05), math.log(20.0)))
    self_loops = jnp.exp(jax.random.uniform(key_self, (PARTS_SIZE * NB, BLK), jnp.float32, math.log(0.5), math.log(2.0)))
    diagonal = jnp.eye(BLK, dtype=jnp.float32)[None] * self_loops[:, None, :]
    tiles_all = jnp.where(present, weight, 0.0)
    tiles_all = tiles_all.at[:, 0].add(diagonal)
    return tiles_all.astype(jnp.bfloat16)


def draw_block_lists(key, part):
    part_keys = jax.random.split(key, PARTS_SIZE)
    ref_count = NB * (K - 1)

    def single_part(sub_key):
        key_refs, key_shuffle = jax.random.split(sub_key, 2)
        random_refs = jax.random.randint(key_refs, (ref_count,), 0, NB + PARTS_SIZE * SEND)
        positions = jnp.arange(ref_count, dtype=jnp.int32)
        forced_refs = NB + positions % (PARTS_SIZE * SEND)
        all_refs = jnp.where(positions < PARTS_SIZE * SEND, forced_refs, random_refs)
        shuffle = jax.random.permutation(key_shuffle, ref_count)
        all_refs = all_refs[shuffle].reshape(NB, K - 1)
        own_refs = jnp.arange(NB, dtype=jnp.int32)[:, None]
        return jnp.concatenate([own_refs, all_refs.astype(jnp.int32)], axis=1)
    return jax.vmap(single_part)(part_keys).reshape(PARTS_SIZE * NB, K).astype(jnp.int32)


def draw_train_ids(key, part):
    part_keys = jax.random.split(key, PARTS_SIZE)

    def single_part(sub_key):
        return jax.random.permutation(sub_key, NODES_PART)[:TRAIN_PART]
    return jax.vmap(single_part)(part_keys).reshape(-1).astype(jnp.int32)


def attention_weight(key, salt_value):
    base_draw = jnp.clip(jax.random.normal(jax.random.fold_in(key, salt_value), (D, D), jnp.float32), -4.0, 4.0) / math.sqrt(D)
    return base_draw.astype(jnp.bfloat16)


def draw_query_weight(key, part):
    return attention_weight(key, 1)


def draw_key_weight(key, part):
    return attention_weight(key, 2)


def touch_ends(entries, rng, low, top_value):
    longest = entries.shape.index(max(entries.shape))
    spots = []
    for shift in (0, 1):
        where = [jax.random.randint(jax.random.fold_in(rng, axis), (), 0, length) for axis, length in enumerate(entries.shape)]
        where[longest] = (where[longest] + shift) % entries.shape[longest]
        spots.append(tuple(where))
    return entries.at[spots[0]].set(low).at[spots[1]].set(top_value)


def steps_of(stream_key, extent, cuts, least, largest):
    gain = 1.0
    for dim, parts in cuts:
        heights = jax.random.uniform(jax.random.fold_in(jax.random.fold_in(stream_key, 6), dim), (parts,), jnp.float32, least / len(cuts), largest / len(cuts))
        gain = gain * jnp.repeat(jnp.exp(heights), extent[dim] // parts).reshape((-1,) + (1,) * (len(extent) - 1 - dim))
    return gain


def shared_out(key, own, number, rows, amount, top, bound, slope):
    order = jax.random.permutation(key, amount)
    packed, common = load_shares(amount, rows * top, bound, slope, True), load_shares(amount, rows * top, bound, slope, False)
    places = jnp.arange(amount)

    def named(sizes, rotation):
        used = int((sizes > 0).sum())
        fixed = max(1, used // 4)
        moved = fixed + (places - fixed + rotation * (used - fixed)) % max(1, amount - fixed)
        return jnp.zeros((amount,), jnp.int32).at[order[jnp.where(places < fixed, places, moved)]].set(jnp.asarray(sizes, jnp.int32))

    sizes = jnp.where(number % 4 == 0, named(packed, number // 4), named(common, number - number // 4 - 1))
    mixed = jax.random.permutation(jax.random.fold_in(own, 3), amount)
    donor, taker = mixed[0:amount // 2 * 2:2], mixed[1:amount // 2 * 2:2]
    room = jnp.minimum(sizes[donor] - 1, bound - sizes[taker]) // 2
    room = jnp.where((donor == order[0]) | (taker == order[0]) | (sizes[taker] == 0), 0, jnp.maximum(room, 0))
    moved = jax.random.randint(jax.random.fold_in(own, 4), (amount // 2,), 0, 1 << 20) % (room + 1)
    sizes = sizes.at[donor].add(-moved).at[taker].add(moved)
    items = jnp.searchsorted(jnp.cumsum(sizes), jnp.arange(rows * top), side="right").astype(jnp.int32)
    table = items.reshape(top, rows).T
    table = table[jax.random.permutation(jax.random.fold_in(own, 1), rows)]
    rotation = jax.random.randint(jax.random.fold_in(own, 2), (rows, 1), 0, top)
    return jnp.take_along_axis(table, (jnp.arange(top)[None, :] + rotation) % top, axis=1)


def load_shares(number_of, total, bound, skew, full):
    weights = [(1 << 20) // math.isqrt(rank ** skew) + 1 for rank in range(1, number_of + 1)]
    largest = bound if full else min(bound, max(-(-total // number_of), total * weights[0] // sum(weights)))
    least = 1 if total - largest >= number_of - 1 else 0
    given, spare = [largest] + [least] * (number_of - 1), total - largest - least * (number_of - 1)
    while spare > 0:
        candidates = [i for i in range(1, number_of) if given[i] < largest] or [i for i in range(1, number_of) if given[i] < bound]
        pool, left = sum([weights[i] for i in candidates]), spare
        for i in candidates:
            extra = min(bound - given[i], max(1, left * weights[i] // pool), spare)
            given[i] = given[i] + extra
            spare = spare - extra
    return np.array(given)


def centred(own_key, dims, spread, limit, pieces=(), held_as=jnp.bfloat16):
    values = jax.random.normal(own_key, dims, jnp.float32) * spread
    if len(pieces) > 0:
        values = steps_of(own_key, dims, pieces, -0.22, 0.18) * values
    return jnp.clip(values, min=-limit, max=limit).astype(held_as)


def setup_inputs(seed: int = 0) -> dict:
    key_of = jax.random.split(jax.random.key(seed), 14)
    features = draw_features(jax.random.fold_in(key_of[13], 71), 0)
    edge_tiles = draw_edge_tiles(jax.random.fold_in(key_of[13], 71), 0)
    block_lists = draw_block_lists(jax.random.fold_in(key_of[13], 71), 0)
    send_lists = touch_ends(jax.random.randint(key_of[3], (PARTS_SIZE, PARTS_SIZE, SEND), 0, NB), jax.random.fold_in(key_of[3], 1), 0, NB - 1).astype(jnp.int32)
    train_ids = draw_train_ids(jax.random.fold_in(key_of[13], 71), 0)
    owners_keys = jax.random.split(jax.random.fold_in(key_of[5], 1), TRAINS // TRAIN_PART)
    owners_turns = jax.random.permutation(jax.random.fold_in(key_of[5], 3), TRAINS // TRAIN_PART)
    owners = jax.vmap(lambda own, number: shared_out(jax.random.fold_in(key_of[5], 2), own, number, TRAIN_PART, DEVICES, 1, MB // PARTS_SIZE, 2))(owners_keys, owners_turns).reshape((TRAINS, 1))
    cotangent = centred(key_of[6], (TOKS, D, TRAINS), 1.0, 6.0, ((1, 8), (2, 16)))
    query_weight = draw_query_weight(jax.random.fold_in(key_of[13], 71), 0)
    key_weight = draw_key_weight(jax.random.fold_in(key_of[13], 71), 0)
    value_weight = centred(key_of[9], (D, D), D ** -0.5, 0.25)
    out_weight = centred(key_of[10], (D, D), D ** -0.5, 0.25)
    up_weight = centred(key_of[11], (FF, D), D ** -0.5, 0.25)
    down_weight = centred(key_of[12], (FF, D), FF ** -0.5, 0.125)
    return {"features": features, "edge_tiles": edge_tiles, "block_lists": block_lists, "send_lists": send_lists, "train_ids": train_ids, "owners": owners, "cotangent": cotangent, "query_weight": query_weight, "key_weight": key_weight, "value_weight": value_weight, "out_weight": out_weight, "up_weight": up_weight, "down_weight": down_weight}


epsilon = 1e-05

def product_of(pattern, first_arg, second_arg):
    return jnp.einsum(pattern, first_arg.astype(jnp.float32), second_arg.astype(jnp.float32))

def normalize(hidden):
    center = hidden - lax.optimization_barrier(jnp.mean(hidden, axis=1, keepdims=True))
    inverse = lax.rsqrt(lax.optimization_barrier(jnp.mean(center * center, axis=1, keepdims=True)) + epsilon)
    return (center * inverse, inverse)

def norm_back(upstream, normed, inverse):
    return inverse * (upstream - lax.optimization_barrier(jnp.mean(upstream, axis=1, keepdims=True)) - normed * lax.optimization_barrier(jnp.mean(upstream * normed, axis=1, keepdims=True)))

def gelu_tanh(values):
    return jax.nn.gelu(values, approximate=True)

def layer_grads(tokens, cotangent, query_weight, key_weight, value_weight, out_weight, up_weight, down_weight):
    tok_count, feat_width, row_count = tokens.shape
    head_dim = feat_width // HEADS
    score_scale = 1.0 / math.sqrt(head_dim)
    split_heads = (tok_count, HEADS, head_dim, row_count)
    first_norm, _ = normalize(tokens.astype(jnp.float32))
    normed_a = first_norm.astype(jnp.bfloat16)
    query_heads = product_of('od,tdr->tor', query_weight, normed_a).astype(jnp.bfloat16).reshape(split_heads)
    key_heads = product_of('od,tdr->tor', key_weight, normed_a).astype(jnp.bfloat16).reshape(split_heads)
    value_heads = product_of('od,tdr->tor', value_weight, normed_a).astype(jnp.bfloat16).reshape(split_heads)
    scores = product_of('thdr,uhdr->htur', query_heads, key_heads) * score_scale
    attn_probs = jax.nn.softmax(scores, axis=2)
    attn_low = attn_probs.astype(jnp.bfloat16)
    mixed_heads = product_of('htur,uhdr->thdr', attn_low, value_heads).astype(jnp.bfloat16).reshape(tok_count, feat_width, row_count)
    residual = (tokens.astype(jnp.float32) + product_of('od,tdr->tor', out_weight, mixed_heads)).astype(jnp.bfloat16)
    second_norm, second_inv = normalize(residual.astype(jnp.float32))
    normed_b = second_norm.astype(jnp.bfloat16)
    pre_act = product_of('fd,tdr->tfr', up_weight, normed_b)
    activated = gelu_tanh(pre_act).astype(jnp.bfloat16)
    sum_down = product_of('tfr,tdr->fd', activated, cotangent)
    grad_act = product_of('fd,tdr->tfr', down_weight, cotangent)
    _, gelu_back = jax.vjp(gelu_tanh, pre_act)
    grad_pre = gelu_back(grad_act)[0].astype(jnp.bfloat16)
    sum_up = product_of('tfr,tdr->fd', grad_pre, normed_b)
    grad_normed = product_of('fd,tfr->tdr', up_weight, grad_pre)
    grad_resid = (cotangent.astype(jnp.float32) + norm_back(grad_normed, second_norm, second_inv)).astype(jnp.bfloat16)
    sum_out = product_of('tor,tdr->od', grad_resid, mixed_heads)
    grad_mixed = product_of('od,tor->tdr', out_weight, grad_resid).astype(jnp.bfloat16).reshape(split_heads)
    grad_probs = product_of('thdr,uhdr->htur', grad_mixed, value_heads)
    grad_value = product_of('htur,thdr->uhdr', attn_low, grad_mixed).astype(jnp.bfloat16)
    grad_scores = (attn_probs * (grad_probs - lax.optimization_barrier(jnp.sum(attn_probs * grad_probs, axis=2, keepdims=True))) * score_scale).astype(jnp.bfloat16)
    grad_query = product_of('htur,uhdr->thdr', grad_scores, key_heads).astype(jnp.bfloat16)
    grad_key = product_of('htur,thdr->uhdr', grad_scores, query_heads).astype(jnp.bfloat16)
    flat_shape = (tok_count, feat_width, row_count)
    sum_query = product_of('tor,tdr->od', grad_query.reshape(flat_shape), normed_a)
    sum_key = product_of('tor,tdr->od', grad_key.reshape(flat_shape), normed_a)
    sum_value = product_of('tor,tdr->od', grad_value.reshape(flat_shape), normed_a)
    return (jnp.concatenate([sum_query, sum_key, sum_value, sum_out], axis=0), sum_up, sum_down)

def global_sources(block_lists, send_lists):
    block_count = block_lists.shape[0]
    home_part = (jnp.arange(block_count, dtype=jnp.int32) // NB)[:, None]
    is_local = block_lists < NB
    halo_slot = jnp.maximum(block_lists - NB, 0)
    peer_part = halo_slot // SEND
    peer_slot = halo_slot % SEND
    remote = peer_part * NB + send_lists[peer_part, home_part, peer_slot]
    return jnp.where(is_local, home_part * NB + block_lists, remote).astype(jnp.int32)

def smooth_step(field, edge_tiles, sources, degree):
    feat_width = field.shape[0]
    blocks = field.reshape(feat_width, -1, BLK).astype(jnp.float32)

    def single_block(inputs):
        tile_block, src_block, deg_block = inputs
        picked = blocks[:, src_block, :]
        return jnp.einsum('dks,kst->dt', picked, tile_block.astype(jnp.float32)) / deg_block[None]
    result = lax.map(single_block, (edge_tiles, sources, degree))
    return jnp.transpose(result, (1, 0, 2)).reshape(feat_width, -1).astype(jnp.bfloat16)

def reference(features, edge_tiles, block_lists, send_lists, train_ids, owners, cotangent, query_weight, key_weight, value_weight, out_weight, up_weight, down_weight):
    sources = global_sources(block_lists, send_lists)
    degree = lax.optimization_barrier(jnp.sum(edge_tiles.astype(jnp.float32), axis=(1, 2)))
    current = features
    hop_list = []
    for hop_index in range(HOPS):
        applied_once = smooth_step(current, edge_tiles, sources, degree)
        applied_twice = smooth_step(applied_once, edge_tiles, sources, degree)
        current = (0.5 * current.astype(jnp.float32) + applied_once.astype(jnp.float32) + applied_twice.astype(jnp.float32)).astype(jnp.bfloat16)
        hop_list.append(current)
    hop_tokens = jnp.stack(hop_list)
    everything = jnp.concatenate([features[None], hop_tokens], axis=0)
    part_of = jnp.arange(TRAINS, dtype=jnp.int32) // TRAIN_PART
    picked = everything[:, :, part_of * NODES_PART + train_ids]
    onehot = (owners[:, 0:1] == jnp.arange(DEVICES, dtype=jnp.int32)[None]).astype(jnp.float32)
    counts = lax.optimization_barrier(jnp.sum(onehot, axis=0))
    row_scale = lax.optimization_barrier(jnp.sum(onehot * (1.0 / counts)[None], axis=1))
    scaled = (cotangent.astype(jnp.float32) * row_scale[None, None]).astype(jnp.bfloat16)
    token_parts = picked.reshape(TOKS, D, PARTS_SIZE, TRAIN_PART).transpose(2, 0, 1, 3)
    grad_parts = scaled.reshape(TOKS, D, PARTS_SIZE, TRAIN_PART).transpose(2, 0, 1, 3)

    def accumulate(totals, inputs):
        part_terms = layer_grads(inputs[0], inputs[1], query_weight, key_weight, value_weight, out_weight, up_weight, down_weight)
        return (tuple((old_sum + new_term for old_sum, new_term in zip(totals, part_terms))), None)
    zero_sums = (jnp.zeros((4 * D, D), jnp.float32), jnp.zeros((FF, D), jnp.float32), jnp.zeros((FF, D), jnp.float32))
    totals, _ = lax.scan(accumulate, zero_sums, (token_parts, grad_parts))
    return (hop_tokens, totals[0], totals[1], totals[2])
```

```python
import functools
import math

import jax
import jax.numpy as jnp
from jax import lax
from jax.experimental import pallas as pl
from jax.experimental.pallas import tpu as pltpu
from jax.sharding import Mesh, PartitionSpec as P

D = 512
FF = 2048
HEADS = 8
HEAD_DIM = 64
HOPS = 3
TOKS = 4
BLK = 128
K = 12
SEND = 2
NB = 32
PARTS = 16
FEATS = 64
NODES = NB * BLK
TRAIN = 512
CHIP_NODES = 128
NARROW = 8
CHIPS = 64
GROUP = 16
STEP_BLOCKS = 4
FF_CHUNK = 256
EPSILON = 1e-05

BF = jnp.bfloat16
F32 = jnp.float32
WIDE = ("z", "y")
NARROW_AXES = ("x", "c")
ALL_CHIPS = ("z", "y", "x")


def params(limit_mib):
    return pltpu.CompilerParams(vmem_limit_bytes=limit_mib * 1024 * 1024)


def dot(left, right):
    return jnp.dot(left, right, preferred_element_type=F32)


def dot_rows(left, right):
    return lax.dot_general(left, right, (((1,), (1,)), ((), ())), preferred_element_type=F32)


def pack_kernel(sends, field, outgoing):
    for slot in range(PARTS * SEND):
        start = pl.multiple_of(sends[slot] * BLK, BLK)
        rows = (slot % SEND) * FEATS
        outgoing[slot // SEND, rows : rows + FEATS, :] = field[:, pl.ds(start, BLK)]


def pack(sends, field):
    return pl.pallas_call(
        pack_kernel,
        out_shape=jax.ShapeDtypeStruct((PARTS, SEND * FEATS, BLK), BF),
        in_specs=[
            pl.BlockSpec(memory_space=pltpu.SMEM),
            pl.BlockSpec((FEATS, NODES), lambda: (0, 0)),
        ],
        compiler_params=params(16),
        name="pack",
    )(sends, field)


def apply_kernel(*refs, second, last, counted):
    refs = list(refs)
    lists, sends, tiles, field, incoming, degree = refs[:6]
    refs = refs[6:]
    previous = refs.pop(0) if second else None
    counts = refs.pop(0) if counted else None
    if second:
        refs.pop(0)
    result = refs.pop(0)
    hops = refs.pop(0) if second else None
    outgoing = None if last else refs.pop(0)
    pool, fresh = refs
    step = pl.program_id(0)

    @pl.when(step == 0)
    def _():
        for j in range(NB):
            pool[j] = field[:, j * BLK : (j + 1) * BLK]
        for j in range(PARTS * SEND):
            rows = (j % SEND) * FEATS
            pool[NB + j] = incoming[j // SEND, rows : rows + FEATS, :]

    for g in range(STEP_BLOCKS):
        b = step * STEP_BLOCKS + g
        picked = jnp.concatenate([pool[lists[b, k]] for k in range(K)], axis=1)
        summed = dot(picked, tiles[g].reshape(K * BLK, BLK))
        value = (summed / degree[pl.ds(b, 1), :]).astype(BF)
        cols = pl.ds(pl.multiple_of(b * BLK, BLK), BLK)
        if second:
            value = (
                0.5 * previous[:, cols].astype(F32) + pool[b].astype(F32) + value.astype(F32)
            ).astype(BF)
            hops[0, :, cols] = value
        result[:, cols] = value
        fresh[b] = value

    if not last:

        @pl.when(step == NB // STEP_BLOCKS - 1)
        def _():
            for slot in range(PARTS * SEND):
                rows = (slot % SEND) * FEATS
                outgoing[slot // SEND, rows : rows + FEATS, :] = fresh[sends[slot]]
            if counted:
                for p in range(PARTS):
                    outgoing[p, SEND * FEATS :, :] = jnp.broadcast_to(
                        counts[...], (GROUP, BLK)
                    ).astype(BF)


def apply(lists, sends, tiles, field, incoming, degree, previous=None, hops=None, hop=0, counts=None):
    second = previous is not None
    last = second and hop == HOPS - 1
    counted = counts is not None
    whole = lambda *shape: pl.BlockSpec(shape, lambda i: (0,) * len(shape))
    smem = pl.BlockSpec(memory_space=pltpu.SMEM)
    operands = [lists, sends, tiles, field, incoming, degree]
    in_specs = [
        smem,
        smem,
        pl.BlockSpec((STEP_BLOCKS, K, BLK, BLK), lambda i: (i, 0, 0, 0)),
        whole(FEATS, NODES),
        whole(*incoming.shape),
        whole(NB, BLK),
    ]
    out_shape = [jax.ShapeDtypeStruct((FEATS, NODES), BF)]
    out_specs = [whole(FEATS, NODES)]
    aliases = {}
    if second:
        operands.append(previous)
        in_specs.append(whole(FEATS, NODES))
    if counted:
        operands.append(counts)
        in_specs.append(whole(1, BLK))
    if second:
        if hops is None:
            operands.append(counts_stub(sends))
            in_specs.append(smem)
        else:
            aliases = {len(operands): 1}
            operands.append(hops)
            in_specs.append(pl.BlockSpec(memory_space=pl.ANY))
        out_shape.append(jax.ShapeDtypeStruct((HOPS, FEATS, NODES), BF))
        out_specs.append(pl.BlockSpec((1, FEATS, NODES), lambda i: (hop, 0, 0)))
    if not last:
        rows = SEND * FEATS + (GROUP if counted else 0)
        out_shape.append(jax.ShapeDtypeStruct((PARTS, rows, BLK), BF))
        out_specs.append(whole(PARTS, rows, BLK))
    return pl.pallas_call(
        functools.partial(apply_kernel, second=second, last=last, counted=counted),
        grid=(NB // STEP_BLOCKS,),
        out_shape=out_shape,
        in_specs=in_specs,
        out_specs=out_specs,
        scratch_shapes=[
            pltpu.VMEM((2 * NB, FEATS, BLK), BF),
            pltpu.VMEM((NB, FEATS, BLK), BF),
        ],
        input_output_aliases=aliases,
        compiler_params=params(32),
        name=f"apply_{'second' if second else 'first'}_{hop}",
    )(*operands)


def counts_stub(sends):
    return sends


def pick_field(field, ids):
    total = None
    for b in range(NB):
        rows = lax.broadcasted_iota(jnp.int32, (BLK, TRAIN), 0) + b * BLK
        chosen = jnp.where(rows == ids, 1.0, 0.0).astype(BF)
        term = dot(field[:, b * BLK : (b + 1) * BLK], chosen)
        total = term if total is None else total + term
    return total.astype(BF)


def pick_kernel(ids, *refs, with_grads):
    refs = list(refs)
    out = refs.pop()
    grads = refs.pop() if with_grads else None
    id_row = ids[...]
    for index, field in enumerate(refs):
        picked = pick_field(field, id_row)
        for n in range(NARROW):
            x = n // 2
            out[n, index * FEATS : (index + 1) * FEATS, :] = picked[
                :, x * CHIP_NODES : (x + 1) * CHIP_NODES
            ]
    if with_grads:
        base = len(refs) * FEATS
        for n in range(NARROW):
            x = n // 2
            out[n, base:, :] = grads[:, x * CHIP_NODES : (x + 1) * CHIP_NODES]


def pick(ids, fields, grads=None):
    rows = FEATS * len(fields) + (0 if grads is None else TOKS * FEATS)
    operands = [ids, *fields] + ([] if grads is None else [grads])
    return pl.pallas_call(
        functools.partial(pick_kernel, with_grads=grads is not None),
        out_shape=jax.ShapeDtypeStruct((NARROW, rows, CHIP_NODES), BF),
        compiler_params=params(32),
        name=f"pick_{len(fields)}_{rows}",
    )(*operands)


def layer_kernel(
    core, first, middle, final, scale, query_w, key_w, value_w, out_w, out_t, up_w, up_t, down_w,
    result, query_s, key_s, value_s, mixed_s, probs_s, act_s, pre_s, gmix_s, gq_s, gk_s, gv_s, gr_s,
):
    own = core[0]
    width = TOKS * CHIP_NODES
    tokens = jnp.concatenate(
        [
            first[:, 0:FEATS, :].reshape(D, CHIP_NODES),
            middle[:, 0:FEATS, :].reshape(D, CHIP_NODES),
            middle[:, FEATS : 2 * FEATS, :].reshape(D, CHIP_NODES),
            final[...].reshape(D, CHIP_NODES),
        ],
        axis=1,
    )
    row_scale = scale[...]
    scaled = jnp.concatenate(
        [
            (
                first[:, (t + 1) * FEATS : (t + 2) * FEATS, :].reshape(D, CHIP_NODES).astype(F32)
                * row_scale
            ).astype(BF)
            for t in range(TOKS)
        ],
        axis=1,
    )

    def normalize(hidden):
        center = hidden - jnp.mean(hidden, axis=0, keepdims=True)
        inverse = lax.rsqrt(jnp.mean(center * center, axis=0, keepdims=True) + EPSILON)
        return center * inverse, inverse

    normed_a = normalize(tokens.astype(F32))[0].astype(BF)
    query_s[...] = dot(query_w[...], normed_a).astype(BF)
    key_s[...] = dot(key_w[...], normed_a).astype(BF)
    value_s[...] = dot(value_w[...], normed_a).astype(BF)
    score_scale = 1.0 / math.sqrt(HEAD_DIM)

    def parts(ref, rows):
        block = ref[rows, :].astype(F32)
        return [block[:, t * CHIP_NODES : (t + 1) * CHIP_NODES] for t in range(TOKS)]

    def forward_head(h, carry):
        rows = pl.ds(pl.multiple_of(h * HEAD_DIM, HEAD_DIM), HEAD_DIM)
        query, key, value = parts(query_s, rows), parts(key_s, rows), parts(value_s, rows)
        all_probs = []
        mixed = []
        for t in range(TOKS):
            scores = [
                jnp.sum(query[t] * key[u], axis=0, keepdims=True) * score_scale
                for u in range(TOKS)
            ]
            top = jnp.maximum(
                jnp.maximum(scores[0], scores[1]), jnp.maximum(scores[2], scores[3])
            )
            raised = [jnp.exp(s - top) for s in scores]
            total = raised[0] + raised[1] + raised[2] + raised[3]
            probs = [r / total for r in raised]
            all_probs += probs
            low = [p.astype(BF).astype(F32) for p in probs]
            mixed.append(
                low[0] * value[0] + low[1] * value[1] + low[2] * value[2] + low[3] * value[3]
            )
        probs_s[h] = jnp.concatenate(all_probs, axis=0)
        mixed_s[rows, :] = jnp.concatenate(mixed, axis=1).astype(BF)
        return carry

    lax.fori_loop(0, HEADS, forward_head, 0)
    residual = (tokens.astype(F32) + dot(out_w[...], mixed_s[...])).astype(BF)
    second_norm, second_inv = normalize(residual.astype(F32))
    normed_b = second_norm.astype(BF)

    root = math.sqrt(2.0 / math.pi)
    groups = FF_CHUNK // (2 * GROUP)

    def ffn_chunk(i, carry):
        rows = pl.ds(pl.multiple_of(i * FF_CHUNK, FF_CHUNK), FF_CHUNK)
        pre = dot(up_w[rows, :], normed_b)
        grad_act = dot(down_w[rows, :], scaled)
        square = pre * pre
        gate = 0.5 + 0.5 * jnp.tanh(pre * (root + (root * 0.044715) * square))
        activated = pre * gate
        slope = gate + activated * (1.0 - gate) * (
            2.0 * root + (6.0 * root * 0.044715) * square
        )
        at = pl.ds(i * groups, groups)
        act_s[at] = activated.astype(BF).reshape(groups, 2, GROUP, width)
        pre_s[at] = (grad_act * slope).astype(BF).reshape(groups, 2, GROUP, width)
        return carry

    lax.fori_loop(0, FF // FF_CHUNK, ffn_chunk, 0)

    half = FF // 2
    grad_down = dot_rows(act_s[:, own].reshape(half, width), scaled)
    result[:, 2 * GROUP : 3 * GROUP, :] = grad_down.astype(BF).reshape(CHIPS, GROUP, D)
    grad_up = dot_rows(pre_s[:, own].reshape(half, width), normed_b)
    result[:, GROUP : 2 * GROUP, :] = grad_up.astype(BF).reshape(CHIPS, GROUP, D)

    grad_normed = dot(up_t[...], pre_s[...].reshape(FF, width))
    grad_resid = (
        scaled.astype(F32)
        + second_inv
        * (
            grad_normed
            - jnp.mean(grad_normed, axis=0, keepdims=True)
            - second_norm * jnp.mean(grad_normed * second_norm, axis=0, keepdims=True)
        )
    ).astype(BF)
    gr_s[...] = grad_resid.reshape(GROUP, 2, GROUP, width)
    gmix_s[...] = dot(out_t[...], grad_resid).astype(BF)

    def backward_head(h, carry):
        rows = pl.ds(pl.multiple_of(h * HEAD_DIM, HEAD_DIM), HEAD_DIM)
        query, key, value = parts(query_s, rows), parts(key_s, rows), parts(value_s, rows)
        grad_mixed = parts(gmix_s, rows)
        saved = probs_s[h]
        prob = lambda t, u: saved[t * TOKS + u : t * TOKS + u + 1, :]
        weights = []
        grad_query = []
        for t in range(TOKS):
            grad_probs = [
                jnp.sum(grad_mixed[t] * value[u], axis=0, keepdims=True) for u in range(TOKS)
            ]
            inner = sum(prob(t, u) * grad_probs[u] for u in range(TOKS))
            weight = [
                (prob(t, u) * (grad_probs[u] - inner) * score_scale).astype(BF).astype(F32)
                for u in range(TOKS)
            ]
            weights.append(weight)
            grad_query.append(sum(weight[u] * key[u] for u in range(TOKS)))
        grad_key = [sum(weights[t][u] * query[t] for t in range(TOKS)) for u in range(TOKS)]
        grad_value = [
            sum(prob(t, u).astype(BF).astype(F32) * grad_mixed[t] for t in range(TOKS))
            for u in range(TOKS)
        ]
        at = pl.ds(h * 2, 2)
        for ref, pieces in ((gq_s, grad_query), (gk_s, grad_key), (gv_s, grad_value)):
            ref[at] = jnp.concatenate(pieces, axis=1).astype(BF).reshape(2, 2, GROUP, width)
        return carry

    lax.fori_loop(0, HEADS, backward_head, 0)
    quarter = D // 2
    stacked = jnp.concatenate(
        [ref[:, own].reshape(quarter, width) for ref in (gq_s, gk_s, gv_s)], axis=0
    )
    count = GROUP * 3
    result[:count, 0:GROUP, :] = dot_rows(stacked, normed_a).astype(BF).reshape(count, GROUP, D)
    sum_out = dot_rows(gr_s[:, own].reshape(quarter, width), mixed_s[...])
    result[count:, 0:GROUP, :] = sum_out.astype(BF).reshape(GROUP, GROUP, D)


def layer(core, first, middle, final, scale, *weights):
    width = TOKS * CHIP_NODES
    square = pltpu.VMEM((D, width), BF)
    grouped = pltpu.VMEM((GROUP, 2, GROUP, width), BF)
    wide = pltpu.VMEM((CHIPS, 2, GROUP, width), BF)
    vmem = pl.BlockSpec(memory_space=pltpu.VMEM)
    return pl.pallas_call(
        layer_kernel,
        out_shape=jax.ShapeDtypeStruct((CHIPS, 3 * GROUP, D), BF),
        in_specs=[pl.BlockSpec(memory_space=pltpu.SMEM)] + [vmem] * 12,
        scratch_shapes=[
            square, square, square, square,
            pltpu.VMEM((HEADS, TOKS * TOKS, CHIP_NODES), F32),
            wide, wide, square, grouped, grouped, grouped, grouped,
        ],
        compiler_params=params(56),
        name="layer",
    )(core, first, middle, final, scale, *weights)


def exchange(array, axes):
    return lax.all_to_all(array, axes, split_axis=0, concat_axis=0, tiled=True)


def on_device(
    features, edge_tiles, block_lists, send_lists, train_ids, owners, cotangent,
    query_weight, key_weight, value_weight, out_weight, up_weight, down_weight,
):
    sends = send_lists.reshape(-1)
    ids = train_ids.reshape(1, TRAIN)
    degree = jnp.sum(edge_tiles, axis=(1, 2), dtype=F32)
    named = (owners == jnp.arange(CHIPS * 2, dtype=jnp.int32)[None]).astype(F32)
    counts = jnp.sum(named, axis=0, keepdims=True)

    incoming = exchange(pack(sends, features), WIDE)
    first_rows = exchange(pick(ids, [features], cotangent.reshape(TOKS * FEATS, TRAIN)), NARROW_AXES)
    current = features
    hops = None
    fields = []
    for hop in range(HOPS):
        once, outgoing = apply(
            block_lists, sends, edge_tiles, current, incoming, degree,
            hop=hop, counts=counts if hop == 0 else None,
        )
        incoming = exchange(outgoing, WIDE)
        if hop == 0:
            total_counts = jnp.sum(incoming[:, SEND * FEATS, :].astype(F32), axis=0)
        results = apply(
            block_lists, sends, edge_tiles, once, incoming, degree,
            previous=current, hops=hops, hop=hop,
        )
        current, hops = results[0], results[1]
        fields.append(current)
        if hop < HOPS - 1:
            incoming = exchange(results[2], WIDE)
        if hop == 1:
            middle_rows = exchange(pick(ids, fields), NARROW_AXES)
    final_rows = exchange(pick(ids, [current]), NARROW_AXES)

    mine = lax.dynamic_slice(owners.reshape(-1), (lax.axis_index("x") * CHIP_NODES,), (CHIP_NODES,))
    owner_of = jnp.arange(CHIPS * 2, dtype=jnp.int32)[:, None] == mine[None, :]
    scale = jnp.sum(
        jnp.where(owner_of, (1.0 / total_counts)[:, None], 0.0), axis=0, keepdims=True
    )
    core = lax.axis_index("c").astype(jnp.int32).reshape(1)
    partial = layer(
        core, first_rows, middle_rows, final_rows, scale,
        query_weight, key_weight, value_weight, out_weight, out_weight.T,
        up_weight, up_weight.T, down_weight,
    )
    gathered = exchange(partial, ALL_CHIPS)
    sums = jnp.sum(gathered.astype(F32), axis=0)
    return (hops, sums[:GROUP], sums[GROUP : 2 * GROUP], sums[2 * GROUP :])


def solution(mesh):
    split = Mesh(mesh.devices.reshape(4, 4, 4, 2), ("z", "y", "x", "c"))
    rows = P(WIDE + NARROW_AXES, None)
    in_specs = (
        P(NARROW_AXES, WIDE),
        P(WIDE, None, None, None),
        P(WIDE, None),
        P(WIDE, None, None),
        P(WIDE),
        P(WIDE, None),
        P(None, NARROW_AXES, WIDE),
        P(), P(), P(), P(), P(), P(),
    )
    out_specs = (P(None, NARROW_AXES, WIDE), rows, rows, rows)
    return jax.shard_map(
        on_device, mesh=split, in_specs=in_specs, out_specs=out_specs, check_vma=False
    )
```

```python
import functools
import math

import jax
import jax.numpy as jnp
from jax import lax
from jax.experimental import pallas as pl
from jax.experimental.pallas import tpu as pltpu
from jax.sharding import Mesh, PartitionSpec as P

D = 512
FF = 2048
HEADS = 8
HEAD_DIM = 64
HOPS = 3
TOKS = 4
BLK = 128
K = 12
SEND = 2
NB = 32
PARTS = 16
FEATS = 64
NODES = NB * BLK
TRAIN = 512
CHIP_NODES = 128
NARROW = 8
CHIPS = 64
GROUP = 16
UNROLL = 4
FF_CHUNK = 256
EPSILON = 1e-05

BF = jnp.bfloat16
F32 = jnp.float32
WIDE = ("z", "y")
NARROW_AXES = ("x", "c")
ALL_CHIPS = ("z", "y", "x")


def params(limit_mib):
    return pltpu.CompilerParams(vmem_limit_bytes=limit_mib * 1024 * 1024)


def dot(left, right):
    return jnp.dot(left, right, preferred_element_type=F32)


def dot_rows(left, right):
    return lax.dot_general(left, right, (((1,), (1,)), ((), ())), preferred_element_type=F32)


def pack_kernel(sends, field, outgoing, sems):
    copies = []
    for slot in range(PARTS * SEND):
        start = pl.multiple_of(sends[0, slot // SEND, slot % SEND] * BLK, BLK)
        rows = (slot % SEND) * FEATS
        copies.append(
            pltpu.make_async_copy(
                field.at[:, pl.ds(start, BLK)],
                outgoing.at[slot // SEND, rows : rows + FEATS, :],
                sems.at[slot],
            )
        )
    for copy in copies:
        copy.start()
    for copy in copies:
        copy.wait()


def pack(sends, field):
    return pl.pallas_call(
        pack_kernel,
        out_shape=jax.ShapeDtypeStruct((PARTS, SEND * FEATS, BLK), BF),
        in_specs=[
            pl.BlockSpec(memory_space=pltpu.SMEM),
            pl.BlockSpec(memory_space=pltpu.HBM),
        ],
        scratch_shapes=[pltpu.SemaphoreType.DMA((PARTS * SEND,))],
        compiler_params=params(4),
        name="pack",
    )(sends, in_hbm(field))


def apply_kernel(*refs, second, first, last):
    refs = list(refs)
    lists, sends, tiles, field, incoming = refs[:5]
    refs = refs[5:]
    degree = None if first else refs.pop(0)
    counts = refs.pop(0) if first else None
    previous = refs.pop(0) if second else None
    aliased = second and refs.pop(0)
    result = refs.pop(0)
    hops = refs.pop(0) if second else None
    outgoing = None if last else refs.pop(0)
    degree_out = refs.pop(0) if first else None
    pool, fresh = refs[:2]

    for j in range(NB):
        pool[j] = field[:, j * BLK : (j + 1) * BLK]
    for j in range(PARTS * SEND):
        rows = (j % SEND) * FEATS
        pool[NB + j] = incoming[j // SEND, rows : rows + FEATS, :]

    def one_block(b, carry):
        picked = jnp.concatenate([pool[lists[b, k]] for k in range(K)], axis=1)
        if first:
            picked = jnp.concatenate([picked, jnp.ones((GROUP, K * BLK), BF)], axis=0)
        summed = dot(picked, tiles[b].reshape(K * BLK, BLK))
        if first:
            share = summed[FEATS : FEATS + 1, :]
            degree_out[pl.ds(b, 1), :] = share
            summed = summed[:FEATS, :]
        else:
            share = degree[pl.ds(b, 1), :]
        value = (summed / share).astype(BF)
        cols = pl.ds(pl.multiple_of(b * BLK, BLK), BLK)
        if second:
            value = (
                0.5 * previous[:, cols].astype(F32) + pool[b].astype(F32) + value.astype(F32)
            ).astype(BF)
        result[:, cols] = value
        fresh[b] = value
        return carry

    lax.fori_loop(0, NB, one_block, 0, unroll=UNROLL)
    if second:
        store = pltpu.make_async_copy(result, hops.at[second - 1], refs[2])
        store.start()
    if not last:
        for slot in range(PARTS * SEND):
            rows = (slot % SEND) * FEATS
            outgoing[slot // SEND, rows : rows + FEATS, :] = fresh[
                sends[0, slot // SEND, slot % SEND]
            ]
        if first:
            for p in range(PARTS):
                outgoing[p, SEND * FEATS :, :] = jnp.broadcast_to(
                    counts[...], (GROUP, BLK)
                ).astype(BF)
    if second:
        store.wait()


def apply(lists, sends, tiles, field, incoming, extra, previous=None, hops=None, hop=0):
    second = previous is not None
    last = second and hop == HOPS - 1
    first = hop == 0 and not second
    smem = pl.BlockSpec(memory_space=pltpu.SMEM)
    vmem = pl.BlockSpec(memory_space=pltpu.VMEM)
    hbm = pl.BlockSpec(memory_space=pltpu.HBM)
    operands = [lists, sends, tiles, field, incoming, extra]
    in_specs = [smem, smem, vmem, vmem, vmem, vmem]
    out_shape = [jax.ShapeDtypeStruct((FEATS, NODES), BF)]
    out_specs = [vmem]
    aliases = {}
    if second:
        operands.append(previous)
        in_specs.append(vmem)
        if hops is None:
            operands.append(sends)
            in_specs.append(smem)
        else:
            aliases = {len(operands): 1}
            operands.append(hops)
            in_specs.append(hbm)
        out_shape.append(jax.ShapeDtypeStruct((HOPS, FEATS, NODES), BF))
        out_specs.append(hbm)
    if not last:
        rows = SEND * FEATS + (GROUP if first else 0)
        out_shape.append(jax.ShapeDtypeStruct((PARTS, rows, BLK), BF))
        out_specs.append(vmem)
    if first:
        out_shape.append(jax.ShapeDtypeStruct((NB, BLK), F32))
        out_specs.append(vmem)
    scratch = [pltpu.VMEM((2 * NB, FEATS, BLK), BF), pltpu.VMEM((NB, FEATS, BLK), BF)]
    if second:
        scratch.append(pltpu.SemaphoreType.DMA)
    return pl.pallas_call(
        functools.partial(apply_kernel, second=second and hop + 1, first=first, last=last),
        out_shape=out_shape,
        in_specs=in_specs,
        out_specs=out_specs,
        scratch_shapes=scratch,
        input_output_aliases=aliases,
        compiler_params=params(20),
        name=f"apply_{'second' if second else 'first'}_{hop}",
    )(*operands)


def pick_kernel(ids, *refs, with_grads):
    refs = list(refs)
    out = refs.pop()
    grads = refs.pop() if with_grads else None
    id_row = ids[...]
    total = None
    for b in range(NB):
        rows = lax.broadcasted_iota(jnp.int32, (BLK, TRAIN), 0) + b * BLK
        chosen = jnp.where(rows == id_row, 1.0, 0.0).astype(BF)
        fields = jnp.concatenate([field[:, b * BLK : (b + 1) * BLK] for field in refs], axis=0)
        term = dot(fields, chosen)
        total = term if total is None else total + term
    picked = total.astype(BF)
    base = len(refs) * FEATS
    for n in range(NARROW):
        cols = slice((n // 2) * CHIP_NODES, (n // 2 + 1) * CHIP_NODES)
        out[n, :base, :] = picked[:, cols]
        if with_grads:
            for t in range(TOKS):
                out[n, base + t * FEATS : base + (t + 1) * FEATS, :] = grads[t, :, cols]


def pick(ids, fields, grads=None):
    rows = FEATS * len(fields) + (0 if grads is None else TOKS * FEATS)
    operands = [ids, *fields] + ([] if grads is None else [grads])
    return pl.pallas_call(
        functools.partial(pick_kernel, with_grads=grads is not None),
        out_shape=jax.ShapeDtypeStruct((NARROW, rows, CHIP_NODES), BF),
        compiler_params=params(8),
        name=f"pick_{len(fields)}_{rows}",
    )(*operands)


def layer_kernel(
    place, first, later, counted, owners, query_h, key_h, value_h, out_h, out_th, up_h, up_th, down_h,
    result, query_s, key_s, value_s, mixed_s, probs_s, act_s, pre_s, gmix_s, gq_s, gk_s, gv_s, gr_s,
    query_w, key_w, value_w, out_w, out_t, up_w, up_t, down_w, sems,
):
    loads = {}
    pairs = (
        (query_h, query_w), (key_h, key_w), (value_h, value_w), (out_h, out_w),
        (up_h, up_w), (down_h, down_w), (up_th, up_t), (out_th, out_t),
    )
    for index, (source, target) in enumerate(pairs):
        loads[index] = pltpu.make_async_copy(source, target, sems.at[index])
        loads[index].start()
    own = place[0]
    width = TOKS * CHIP_NODES
    tokens = jnp.concatenate(
        [
            first[:, 0:FEATS, :].reshape(D, CHIP_NODES),
        ]
        + [later[:, t * FEATS : (t + 1) * FEATS, :].reshape(D, CHIP_NODES) for t in range(HOPS)],
        axis=1,
    )
    totals = counted[0, SEND * FEATS : SEND * FEATS + 1, :].astype(F32)
    for p in range(1, PARTS):
        totals = totals + counted[p, SEND * FEATS : SEND * FEATS + 1, :].astype(F32)
    by_owner = jnp.transpose(jnp.broadcast_to(1.0 / totals, (BLK, BLK)))
    named = lax.broadcasted_iota(jnp.int32, (BLK, BLK), 0) == owners[pl.ds(place[1], 1), :]
    row_scale = jnp.sum(jnp.where(named, by_owner, 0.0), axis=0, keepdims=True)
    scaled = jnp.concatenate(
        [
            (
                first[:, (t + 1) * FEATS : (t + 2) * FEATS, :].reshape(D, CHIP_NODES).astype(F32)
                * row_scale
            ).astype(BF)
            for t in range(TOKS)
        ],
        axis=1,
    )

    def normalize(hidden):
        center = hidden - jnp.mean(hidden, axis=0, keepdims=True)
        inverse = lax.rsqrt(jnp.mean(center * center, axis=0, keepdims=True) + EPSILON)
        return center * inverse, inverse

    normed_a = normalize(tokens.astype(F32))[0].astype(BF)
    loads[0].wait()
    query_s[...] = dot(query_w[...], normed_a).astype(BF)
    loads[1].wait()
    key_s[...] = dot(key_w[...], normed_a).astype(BF)
    loads[2].wait()
    value_s[...] = dot(value_w[...], normed_a).astype(BF)
    score_scale = 1.0 / math.sqrt(HEAD_DIM)

    def parts(ref, rows):
        block = ref[rows, :].astype(F32)
        return [block[:, t * CHIP_NODES : (t + 1) * CHIP_NODES] for t in range(TOKS)]

    def forward_head(h, carry):
        rows = pl.ds(pl.multiple_of(h * HEAD_DIM, HEAD_DIM), HEAD_DIM)
        query, key, value = parts(query_s, rows), parts(key_s, rows), parts(value_s, rows)
        all_probs = []
        mixed = []
        for t in range(TOKS):
            scores = [
                jnp.sum(query[t] * key[u], axis=0, keepdims=True) * score_scale
                for u in range(TOKS)
            ]
            top = jnp.maximum(
                jnp.maximum(scores[0], scores[1]), jnp.maximum(scores[2], scores[3])
            )
            raised = [jnp.exp(s - top) for s in scores]
            total = raised[0] + raised[1] + raised[2] + raised[3]
            probs = [r / total for r in raised]
            all_probs += probs
            low = [p.astype(BF).astype(F32) for p in probs]
            mixed.append(
                low[0] * value[0] + low[1] * value[1] + low[2] * value[2] + low[3] * value[3]
            )
        probs_s[h] = jnp.concatenate(all_probs, axis=0)
        mixed_s[rows, :] = jnp.concatenate(mixed, axis=1).astype(BF)
        return carry

    lax.fori_loop(0, HEADS, forward_head, 0)
    loads[3].wait()
    residual = (tokens.astype(F32) + dot(out_w[...], mixed_s[...])).astype(BF)
    second_norm, second_inv = normalize(residual.astype(F32))
    normed_b = second_norm.astype(BF)

    root = math.sqrt(2.0 / math.pi)
    groups = FF_CHUNK // (2 * GROUP)

    def ffn_chunk(i, carry):
        rows = pl.ds(pl.multiple_of(i * FF_CHUNK, FF_CHUNK), FF_CHUNK)
        pre = dot(up_w[rows, :], normed_b)
        grad_act = dot(down_w[rows, :], scaled)
        square = pre * pre
        gate = 0.5 + 0.5 * jnp.tanh(pre * (root + (root * 0.044715) * square))
        activated = pre * gate
        slope = gate + activated * (1.0 - gate) * (
            2.0 * root + (6.0 * root * 0.044715) * square
        )
        at = pl.ds(i * groups, groups)
        act_s[at] = activated.astype(BF).reshape(groups, 2, GROUP, width)
        pre_s[at] = (grad_act * slope).astype(BF).reshape(groups, 2, GROUP, width)
        return carry

    loads[4].wait()
    loads[5].wait()
    lax.fori_loop(0, FF // FF_CHUNK, ffn_chunk, 0)

    half = FF // 2
    grad_down = dot_rows(act_s[:, own].reshape(half, width), scaled)
    result[:, 2 * GROUP : 3 * GROUP, :] = grad_down.astype(BF).reshape(CHIPS, GROUP, D)
    grad_up = dot_rows(pre_s[:, own].reshape(half, width), normed_b)
    result[:, GROUP : 2 * GROUP, :] = grad_up.astype(BF).reshape(CHIPS, GROUP, D)

    loads[6].wait()
    grad_normed = dot(up_t[...], pre_s[...].reshape(FF, width))
    grad_resid = (
        scaled.astype(F32)
        + second_inv
        * (
            grad_normed
            - jnp.mean(grad_normed, axis=0, keepdims=True)
            - second_norm * jnp.mean(grad_normed * second_norm, axis=0, keepdims=True)
        )
    ).astype(BF)
    gr_s[...] = grad_resid.reshape(GROUP, 2, GROUP, width)
    loads[7].wait()
    gmix_s[...] = dot(out_t[...], grad_resid).astype(BF)

    def backward_head(h, carry):
        rows = pl.ds(pl.multiple_of(h * HEAD_DIM, HEAD_DIM), HEAD_DIM)
        query, key, value = parts(query_s, rows), parts(key_s, rows), parts(value_s, rows)
        grad_mixed = parts(gmix_s, rows)
        saved = probs_s[h]
        prob = lambda t, u: saved[t * TOKS + u : t * TOKS + u + 1, :]
        weights = []
        grad_query = []
        for t in range(TOKS):
            grad_probs = [
                jnp.sum(grad_mixed[t] * value[u], axis=0, keepdims=True) for u in range(TOKS)
            ]
            inner = sum(prob(t, u) * grad_probs[u] for u in range(TOKS))
            weight = [
                (prob(t, u) * (grad_probs[u] - inner) * score_scale).astype(BF).astype(F32)
                for u in range(TOKS)
            ]
            weights.append(weight)
            grad_query.append(sum(weight[u] * key[u] for u in range(TOKS)))
        grad_key = [sum(weights[t][u] * query[t] for t in range(TOKS)) for u in range(TOKS)]
        grad_value = [
            sum(prob(t, u).astype(BF).astype(F32) * grad_mixed[t] for t in range(TOKS))
            for u in range(TOKS)
        ]
        at = pl.ds(h * 2, 2)
        for ref, pieces in ((gq_s, grad_query), (gk_s, grad_key), (gv_s, grad_value)):
            ref[at] = jnp.concatenate(pieces, axis=1).astype(BF).reshape(2, 2, GROUP, width)
        return carry

    lax.fori_loop(0, HEADS, backward_head, 0)
    quarter = D // 2
    stacked = jnp.concatenate(
        [ref[:, own].reshape(quarter, width) for ref in (gq_s, gk_s, gv_s)], axis=0
    )
    count = GROUP * 3
    result[:count, 0:GROUP, :] = dot_rows(stacked, normed_a).astype(BF).reshape(count, GROUP, D)
    sum_out = dot_rows(gr_s[:, own].reshape(quarter, width), mixed_s[...])
    result[count:, 0:GROUP, :] = sum_out.astype(BF).reshape(GROUP, GROUP, D)


def layer(place, first, later, counted, owners, *weights):
    width = TOKS * CHIP_NODES
    square = pltpu.VMEM((D, width), BF)
    grouped = pltpu.VMEM((GROUP, 2, GROUP, width), BF)
    wide = pltpu.VMEM((CHIPS, 2, GROUP, width), BF)
    vmem = pl.BlockSpec(memory_space=pltpu.VMEM)
    hbm = pl.BlockSpec(memory_space=pltpu.HBM)
    return pl.pallas_call(
        layer_kernel,
        out_shape=jax.ShapeDtypeStruct((CHIPS, 3 * GROUP, D), BF),
        in_specs=[pl.BlockSpec(memory_space=pltpu.SMEM)] + [vmem] * 4 + [hbm] * 8,
        out_specs=vmem,
        scratch_shapes=[
            square, square, square, square,
            pltpu.VMEM((HEADS, TOKS * TOKS, CHIP_NODES), F32),
            wide, wide, square, grouped, grouped, grouped, grouped,
            *[pltpu.VMEM(w.shape, BF) for w in weights],
            pltpu.SemaphoreType.DMA((len(weights),)),
        ],
        compiler_params=params(36),
        name="layer",
    )(place, first, later, counted, owners, *[in_hbm(w) for w in weights])


def in_hbm(array):
    return pltpu.with_memory_space_constraint(array, pltpu.HBM)


def exchange(array, axes):
    return lax.all_to_all(array, axes, split_axis=0, concat_axis=0, tiled=True)


def on_device(
    features, edge_tiles, block_lists, send_lists, train_ids, owners, cotangent,
    query_weight, key_weight, value_weight, out_weight, up_weight, down_weight,
):
    ids = train_ids.reshape(1, TRAIN)
    named = (owners == jnp.arange(CHIPS * 2, dtype=jnp.int32)[None]).astype(F32)
    counts = jnp.sum(named, axis=0, keepdims=True)
    incoming = exchange(pack(send_lists, features), WIDE)
    first_rows = exchange(pick(ids, [features], cotangent), NARROW_AXES)
    incoming, first_rows, counts, up_t, out_t = lax.optimization_barrier(
        (incoming, first_rows, counts, up_weight.T, out_weight.T)
    )
    step = functools.partial(apply, block_lists, send_lists, edge_tiles)
    current = features
    hops = None
    fields = []
    for hop in range(HOPS):
        if hop == 0:
            once, outgoing, degree = step(current, incoming, counts)
        else:
            once, outgoing = step(current, incoming, degree, hop=hop)
        incoming = exchange(outgoing, WIDE)
        if hop == 0:
            counted = incoming
        results = step(once, incoming, degree, previous=current, hops=hops, hop=hop)
        current, hops = results[0], results[1]
        fields.append(current)
        if hop < HOPS - 1:
            incoming = exchange(results[2], WIDE)
    later_rows = exchange(pick(ids, fields), NARROW_AXES)

    place = jnp.stack([lax.axis_index("c"), lax.axis_index("x")]).astype(jnp.int32)
    partial = layer(
        place, first_rows, later_rows, counted, owners.reshape(TOKS, CHIP_NODES),
        query_weight, key_weight, value_weight, out_weight, out_t, up_weight, up_t, down_weight,
    )
    gathered = exchange(partial, ALL_CHIPS)
    sums = jnp.sum(gathered.astype(F32), axis=0)
    return (hops, sums[:GROUP], sums[GROUP : 2 * GROUP], sums[2 * GROUP :])


def solution(mesh):
    split = Mesh(mesh.devices.reshape(4, 4, 4, 2), ("z", "y", "x", "c"))
    rows = P(WIDE + NARROW_AXES, None)
    in_specs = (
        P(NARROW_AXES, WIDE),
        P(WIDE, None, None, None),
        P(WIDE, None),
        P(WIDE, None, None),
        P(WIDE),
        P(WIDE, None),
        P(None, NARROW_AXES, WIDE),
        P(), P(), P(), P(), P(), P(),
    )
    out_specs = (P(None, NARROW_AXES, WIDE), rows, rows, rows)
    return jax.shard_map(
        on_device, mesh=split, in_specs=in_specs, out_specs=out_specs, check_vma=False
    )
```

```python
import functools
import math

import jax
import jax.numpy as jnp
from jax import lax
from jax.experimental import pallas as pl
from jax.experimental.pallas import tpu as pltpu
from jax.sharding import Mesh, PartitionSpec as P

D = 512
FF = 2048
HEADS = 8
HEAD_DIM = 64
HOPS = 3
TOKS = 4
BLK = 128
K = 12
SEND = 2
NB = 32
PARTS = 16
FEATS = 64
NODES = NB * BLK
TRAIN = 512
OWNERS = 128
QUAD = 4
QUAD_NODES = 256
NARROW = 8
DESTS = 32
GROUP = 16
UNROLL = 4
FF_CHUNK = 256
EPSILON = 1e-05

BF = jnp.bfloat16
F32 = jnp.float32
WIDE = ("z", "y")
NARROW_AXES = ("xh", "xl", "c")
QUADS = ("z", "y", "xh")
CHUNK = 4


def params(limit_mib):
    return pltpu.CompilerParams(vmem_limit_bytes=limit_mib * 1024 * 1024)


def dot(left, right):
    return jnp.dot(left, right, preferred_element_type=F32)


def dot_rows(left, right):
    return lax.dot_general(left, right, (((1,), (1,)), ((), ())), preferred_element_type=F32)


def pack_kernel(sends, field, outgoing, sems):
    copies = []
    for slot in range(PARTS * SEND):
        start = pl.multiple_of(sends[0, slot // SEND, slot % SEND] * BLK, BLK)
        rows = (slot % SEND) * FEATS
        copies.append(
            pltpu.make_async_copy(
                field.at[:, pl.ds(start, BLK)],
                outgoing.at[slot // SEND, rows : rows + FEATS, :],
                sems.at[slot],
            )
        )
    for copy in copies:
        copy.start()
    for copy in copies:
        copy.wait()


def pack(sends, field):
    return pl.pallas_call(
        pack_kernel,
        out_shape=jax.ShapeDtypeStruct((PARTS, SEND * FEATS, BLK), BF),
        in_specs=[
            pl.BlockSpec(memory_space=pltpu.SMEM),
            pl.BlockSpec(memory_space=pltpu.HBM),
        ],
        scratch_shapes=[pltpu.SemaphoreType.DMA((PARTS * SEND,))],
        compiler_params=params(4),
        name="pack",
    )(sends, in_hbm(field))


def picked_columns(ids, fields):
    id_row = ids[...]
    total = None
    for b in range(NB):
        rows = lax.broadcasted_iota(jnp.int32, (BLK, TRAIN), 0) + b * BLK
        chosen = jnp.where(rows == id_row, 1.0, 0.0).astype(BF)
        block = jnp.concatenate([field[:, b * BLK : (b + 1) * BLK] for field in fields], axis=0)
        term = dot(block, chosen)
        total = term if total is None else total + term
    return total.astype(BF)


def apply_kernel(*refs, second, first, last, picking):
    refs = list(refs)
    lists, sends, tiles_h, field, incoming = refs[:5]
    refs = refs[5:]
    degree = None if first else refs.pop(0)
    previous = refs.pop(0) if second else None
    aliased = second and refs.pop(0)
    ids = refs.pop(0) if picking else None
    others = [refs.pop(0) for _ in range(picking - 1)] if picking else []
    result = refs.pop(0)
    hops = refs.pop(0) if second else None
    outgoing = None if last else refs.pop(0)
    rows_out = refs.pop(0) if picking else None
    degree_out = refs.pop(0) if first else None
    pool, fresh, tiles, sems = refs
    loads = [
        pltpu.make_async_copy(
            tiles_h.at[pl.ds(i * CHUNK, CHUNK)], tiles.at[pl.ds(i * CHUNK, CHUNK)], sems.at[i]
        )
        for i in range(NB // CHUNK)
    ]
    for load in loads:
        load.start()

    for j in range(NB):
        pool[j] = field[:, j * BLK : (j + 1) * BLK]
    for j in range(PARTS * SEND):
        rows = (j % SEND) * FEATS
        pool[NB + j] = incoming[j // SEND, rows : rows + FEATS, :]

    def one_block(b, carry):
        picked = jnp.concatenate([pool[lists[b, k]] for k in range(K)], axis=1)
        if first:
            picked = jnp.concatenate([picked, jnp.ones((GROUP, K * BLK), BF)], axis=0)
        summed = dot(picked, tiles[b].reshape(K * BLK, BLK))
        if first:
            share = summed[FEATS : FEATS + 1, :]
            degree_out[pl.ds(b, 1), :] = share
            summed = summed[:FEATS, :]
        else:
            share = degree[pl.ds(b, 1), :]
        value = (summed / share).astype(BF)
        cols = pl.ds(pl.multiple_of(b * BLK, BLK), BLK)
        if second:
            value = (
                0.5 * previous[:, cols].astype(F32) + pool[b].astype(F32) + value.astype(F32)
            ).astype(BF)
        result[:, cols] = value
        fresh[b] = value
        return carry

    for i, load in enumerate(loads):
        load.wait()
        lax.fori_loop(i * CHUNK, (i + 1) * CHUNK, one_block, 0, unroll=UNROLL)
    if second:
        store = pltpu.make_async_copy(result, hops.at[second - 1], sems.at[NB // CHUNK])
        store.start()
    if not last:
        for slot in range(PARTS * SEND):
            rows = (slot % SEND) * FEATS
            outgoing[slot // SEND, rows : rows + FEATS, :] = fresh[
                sends[0, slot // SEND, slot % SEND]
            ]
    if picking:
        picked = picked_columns(ids, [*others, result])
        if last:
            for n in range(NARROW):
                half = n // QUAD
                rows_out[n] = picked[:, half * QUAD_NODES : (half + 1) * QUAD_NODES]
        else:
            rows_out[...] = picked
    if second:
        store.wait()


def apply(lists, sends, tiles, field, incoming, degree=None, previous=None, hops=None, hop=0, ids=None, others=()):
    second = previous is not None
    last = second and hop == HOPS - 1
    first = hop == 0 and not second
    smem = pl.BlockSpec(memory_space=pltpu.SMEM)
    vmem = pl.BlockSpec(memory_space=pltpu.VMEM)
    hbm = pl.BlockSpec(memory_space=pltpu.HBM)
    operands = [lists, sends, in_hbm(tiles), field, incoming]
    in_specs = [smem, smem, hbm, vmem, vmem]
    if not first:
        operands.append(degree)
        in_specs.append(vmem)
    out_shape = [jax.ShapeDtypeStruct((FEATS, NODES), BF)]
    out_specs = [vmem]
    aliases = {}
    if second:
        operands.append(previous)
        in_specs.append(vmem)
        if hops is None:
            operands.append(sends)
            in_specs.append(smem)
        else:
            aliases = {len(operands): 1}
            operands.append(hops)
            in_specs.append(hbm)
        out_shape.append(jax.ShapeDtypeStruct((HOPS, FEATS, NODES), BF))
        out_specs.append(hbm)
    if ids is not None:
        operands += [ids, *others]
        in_specs += [vmem] * (1 + len(others))
    if not last:
        out_shape.append(jax.ShapeDtypeStruct((PARTS, SEND * FEATS, BLK), BF))
        out_specs.append(vmem)
    if ids is not None:
        rows = FEATS * (1 + len(others))
        shape = (NARROW, rows, QUAD_NODES) if last else (rows, TRAIN)
        out_shape.append(jax.ShapeDtypeStruct(shape, BF))
        out_specs.append(vmem)
    if first:
        out_shape.append(jax.ShapeDtypeStruct((NB, BLK), F32))
        out_specs.append(vmem)
    scratch = [
        pltpu.VMEM((2 * NB, FEATS, BLK), BF),
        pltpu.VMEM((NB, FEATS, BLK), BF),
        pltpu.VMEM(tiles.shape, BF),
        pltpu.SemaphoreType.DMA((NB // CHUNK + 1,)),
    ]
    return pl.pallas_call(
        functools.partial(
            apply_kernel, second=second and hop + 1, first=first, last=last,
            picking=0 if ids is None else 1 + len(others),
        ),
        out_shape=out_shape,
        in_specs=in_specs,
        out_specs=out_specs,
        scratch_shapes=scratch,
        input_output_aliases=aliases,
        compiler_params=params(28),
        name=f"apply_{'second' if second else 'first'}_{hop}",
    )(*operands)


def layer_kernel(
    place, early_h, grads_h, final, counts, owners,
    query_h, key_h, value_h, out_h, out_th, up_h, up_th, down_h,
    result, query_s, key_s, value_s, mixed_s, probs_s, act_s, pre_s, gmix_s, gq_s, gk_s, gv_s, gr_s,
    query_w, key_w, value_w, out_w, out_t, up_w, up_t, down_w, early, grads, sems,
):
    own = place[0]
    mine = pl.ds(pl.multiple_of(place[1] * QUAD_NODES, QUAD_NODES), QUAD_NODES)
    pairs = (
        (query_h, query_w), (key_h, key_w), (value_h, value_w), (out_h, out_w),
        (up_h, up_w), (down_h, down_w), (up_th, up_t), (out_th, out_t),
        (early_h.at[:, :, mine], early), (grads_h.at[:, :, mine], grads),
    )
    loads = [
        pltpu.make_async_copy(source, target, sems.at[index])
        for index, (source, target) in enumerate(pairs)
    ]
    for index in (8, 0, 1, 2, 9, 3, 4, 5, 6, 7):
        loads[index].start()
    width = TOKS * QUAD_NODES
    loads[8].wait()
    tokens = jnp.concatenate(
        [early[:, t * FEATS : (t + 1) * FEATS, :].reshape(D, QUAD_NODES) for t in range(HOPS)]
        + [final[...].reshape(D, QUAD_NODES)],
        axis=1,
    )

    def normalize(hidden):
        center = hidden - jnp.mean(hidden, axis=0, keepdims=True)
        inverse = lax.rsqrt(jnp.mean(center * center, axis=0, keepdims=True) + EPSILON)
        return center * inverse, inverse

    normed_a = normalize(tokens.astype(F32))[0].astype(BF)
    loads[0].wait()
    query_s[...] = dot(query_w[...], normed_a).astype(BF)
    loads[1].wait()
    key_s[...] = dot(key_w[...], normed_a).astype(BF)
    loads[2].wait()
    value_s[...] = dot(value_w[...], normed_a).astype(BF)
    score_scale = 1.0 / math.sqrt(HEAD_DIM)

    def columns(half):
        return [
            pl.ds(pl.multiple_of(t * QUAD_NODES + half * BLK, BLK), BLK) for t in range(TOKS)
        ]

    def parts(ref, rows, cols):
        return [ref[rows, c].astype(F32) for c in cols]

    def forward_head(step, carry):
        h = step // 2
        cols = columns(step % 2)
        rows = pl.ds(pl.multiple_of(h * HEAD_DIM, HEAD_DIM), HEAD_DIM)
        query, key, value = [parts(ref, rows, cols) for ref in (query_s, key_s, value_s)]
        all_probs = []
        for t in range(TOKS):
            scores = [
                jnp.sum(query[t] * key[u], axis=0, keepdims=True) * score_scale
                for u in range(TOKS)
            ]
            top = jnp.maximum(
                jnp.maximum(scores[0], scores[1]), jnp.maximum(scores[2], scores[3])
            )
            raised = [jnp.exp(s - top) for s in scores]
            total = raised[0] + raised[1] + raised[2] + raised[3]
            probs = [r / total for r in raised]
            all_probs += probs
            low = [p.astype(BF).astype(F32) for p in probs]
            mixed_s[rows, cols[t]] = (
                low[0] * value[0] + low[1] * value[1] + low[2] * value[2] + low[3] * value[3]
            ).astype(BF)
        probs_s[step] = jnp.concatenate(all_probs, axis=0)
        return carry

    lax.fori_loop(0, 2 * HEADS, forward_head, 0)
    loads[3].wait()
    residual = (tokens.astype(F32) + dot(out_w[...], mixed_s[...])).astype(BF)
    second_norm, second_inv = normalize(residual.astype(F32))
    normed_b = second_norm.astype(BF)

    root = math.sqrt(2.0 / math.pi)
    groups = FF_CHUNK // (QUAD * GROUP)

    loads[9].wait()
    named = lax.broadcasted_iota(jnp.int32, (OWNERS, QUAD_NODES), 0) == owners[:, mine]
    by_owner = jnp.concatenate([1.0 / counts[...]] * (QUAD_NODES // OWNERS), axis=1)
    row_scale = jnp.sum(jnp.where(named, by_owner, 0.0), axis=0, keepdims=True)
    scaled = jnp.concatenate(
        [
            (
                grads[:, t * FEATS : (t + 1) * FEATS, :].reshape(D, QUAD_NODES).astype(F32)
                * row_scale
            ).astype(BF)
            for t in range(TOKS)
        ],
        axis=1,
    )

    def ffn_chunk(i, carry):
        rows = pl.ds(pl.multiple_of(i * FF_CHUNK, FF_CHUNK), FF_CHUNK)
        pre = dot(up_w[rows, :], normed_b)
        grad_act = dot(down_w[rows, :], scaled)
        square = pre * pre
        gate = 0.5 + 0.5 * jnp.tanh(pre * (root + (root * 0.044715) * square))
        activated = pre * gate
        slope = gate + activated * (1.0 - gate) * (
            2.0 * root + (6.0 * root * 0.044715) * square
        )
        at = pl.ds(i * groups, groups)
        act_s[at] = activated.astype(BF).reshape(groups, QUAD, GROUP, width)
        pre_s[at] = (grad_act * slope).astype(BF).reshape(groups, QUAD, GROUP, width)
        return carry

    loads[4].wait()
    loads[5].wait()
    lax.fori_loop(0, FF // FF_CHUNK, ffn_chunk, 0)

    share = FF // QUAD
    grad_down = dot_rows(act_s[:, own].reshape(share, width), scaled)
    result[:, 2 * GROUP : 3 * GROUP, :] = grad_down.astype(BF).reshape(DESTS, GROUP, D)
    grad_up = dot_rows(pre_s[:, own].reshape(share, width), normed_b)
    result[:, GROUP : 2 * GROUP, :] = grad_up.astype(BF).reshape(DESTS, GROUP, D)

    loads[6].wait()
    grad_normed = dot(up_t[...], pre_s[...].reshape(FF, width))
    grad_resid = (
        scaled.astype(F32)
        + second_inv
        * (
            grad_normed
            - jnp.mean(grad_normed, axis=0, keepdims=True)
            - second_norm * jnp.mean(grad_normed * second_norm, axis=0, keepdims=True)
        )
    ).astype(BF)
    gr_s[...] = grad_resid.reshape(HEADS, QUAD, GROUP, width)
    loads[7].wait()
    gmix_s[...] = dot(out_t[...], grad_resid).astype(BF)

    def backward_head(step, carry):
        h = step // 2
        cols = columns(step % 2)
        rows = pl.ds(pl.multiple_of(h * HEAD_DIM, HEAD_DIM), HEAD_DIM)
        query, key, value, grad_mixed = [
            parts(ref, rows, cols) for ref in (query_s, key_s, value_s, gmix_s)
        ]
        saved = probs_s[step]
        prob = lambda t, u: saved[t * TOKS + u : t * TOKS + u + 1, :]
        weights = []
        grad_query = []
        for t in range(TOKS):
            grad_probs = [
                jnp.sum(grad_mixed[t] * value[u], axis=0, keepdims=True) for u in range(TOKS)
            ]
            inner = sum(prob(t, u) * grad_probs[u] for u in range(TOKS))
            weight = [
                (prob(t, u) * (grad_probs[u] - inner) * score_scale).astype(BF).astype(F32)
                for u in range(TOKS)
            ]
            weights.append(weight)
            grad_query.append(sum(weight[u] * key[u] for u in range(TOKS)))
        grad_key = [sum(weights[t][u] * query[t] for t in range(TOKS)) for u in range(TOKS)]
        grad_value = [
            sum(prob(t, u).astype(BF).astype(F32) * grad_mixed[t] for t in range(TOKS))
            for u in range(TOKS)
        ]
        for ref, pieces in ((gq_s, grad_query), (gk_s, grad_key), (gv_s, grad_value)):
            for t in range(TOKS):
                ref[h, :, :, cols[t]] = pieces[t].astype(BF).reshape(QUAD, GROUP, BLK)
        return carry

    lax.fori_loop(0, 2 * HEADS, backward_head, 0)
    share = D // QUAD
    stacked = jnp.concatenate(
        [ref[:, own].reshape(share, width) for ref in (gq_s, gk_s, gv_s)], axis=0
    )
    count = HEADS * 3
    result[:count, 0:GROUP, :] = dot_rows(stacked, normed_a).astype(BF).reshape(count, GROUP, D)
    sum_out = dot_rows(gr_s[:, own].reshape(share, width), mixed_s[...])
    result[count:, 0:GROUP, :] = sum_out.astype(BF).reshape(HEADS, GROUP, D)


def in_hbm(array):
    return pltpu.with_memory_space_constraint(array, pltpu.HBM)


def layer(place, early, grads, final, counts, owners, *weights):
    width = TOKS * QUAD_NODES
    square = pltpu.VMEM((D, width), BF)
    grouped = pltpu.VMEM((HEADS, QUAD, GROUP, width), BF)
    wide = pltpu.VMEM((DESTS, QUAD, GROUP, width), BF)
    vmem = pl.BlockSpec(memory_space=pltpu.VMEM)
    hbm = pl.BlockSpec(memory_space=pltpu.HBM)
    smem = pl.BlockSpec(memory_space=pltpu.SMEM)
    return pl.pallas_call(
        layer_kernel,
        out_shape=jax.ShapeDtypeStruct((DESTS, 3 * GROUP, D), BF),
        in_specs=[smem, hbm, hbm, vmem, vmem, vmem] + [hbm] * 8,
        out_specs=vmem,
        scratch_shapes=[
            square, square, square, square,
            pltpu.VMEM((2 * HEADS, TOKS * TOKS, BLK), F32),
            wide, wide, square, grouped, grouped, grouped, grouped,
            *[pltpu.VMEM(w.shape, BF) for w in weights],
            pltpu.VMEM((NARROW, HOPS * FEATS, QUAD_NODES), BF),
            pltpu.VMEM((NARROW, TOKS * FEATS, QUAD_NODES), BF),
            pltpu.SemaphoreType.DMA((len(weights) + 2,)),
        ],
        compiler_params=params(58),
        name="layer",
    )(
        place, in_hbm(early), in_hbm(grads), final, counts, owners,
        *[in_hbm(w) for w in weights],
    )


def exchange(array, axes):
    return lax.all_to_all(array, axes, split_axis=0, concat_axis=0, tiled=True)


def on_device(
    features, edge_tiles, block_lists, send_lists, train_ids, owners, cotangent,
    query_weight, key_weight, value_weight, out_weight, up_weight, down_weight,
):
    ids = train_ids.reshape(1, TRAIN)
    grads = lax.all_gather(cotangent.reshape(TOKS * FEATS, TRAIN), NARROW_AXES)
    named = (owners == jnp.arange(OWNERS, dtype=jnp.int32)[None]).astype(F32)
    counts = lax.psum(
        jnp.broadcast_to(jnp.sum(named, axis=0)[:, None], (OWNERS, OWNERS)), WIDE
    )
    incoming = exchange(pack(send_lists, features), WIDE)
    incoming, up_t, out_t = lax.optimization_barrier((incoming, up_weight.T, out_weight.T))
    step = functools.partial(apply, block_lists, send_lists, edge_tiles)
    current = features
    hops = None
    fields = [features]
    for hop in range(HOPS):
        if hop == 0:
            once, outgoing, degree = step(current, incoming)
        else:
            once, outgoing = step(current, incoming, degree, hop=hop)
        incoming = exchange(outgoing, WIDE)
        results = step(
            once, incoming, degree, previous=current, hops=hops, hop=hop,
            ids=None if hop == 0 else ids,
            others=tuple(fields) if hop == HOPS - 2 else (),
        )
        current, hops = results[0], results[1]
        fields.append(current)
        if hop == HOPS - 2:
            early = lax.all_gather(results[3], NARROW_AXES)
        if hop < HOPS - 1:
            incoming = exchange(results[2], WIDE)
    final = exchange(results[2], NARROW_AXES)

    place = jnp.stack(
        [2 * lax.axis_index("xl") + lax.axis_index("c"), lax.axis_index("xh")]
    ).astype(jnp.int32)
    partial = layer(
        place, early, grads, final, counts, owners.reshape(1, TRAIN),
        query_weight, key_weight, value_weight, out_weight, out_t, up_weight, up_t, down_weight,
    )
    gathered = exchange(partial, QUADS)
    sums = jnp.sum(gathered.astype(F32), axis=0)
    return (hops, sums[:GROUP], sums[GROUP : 2 * GROUP], sums[2 * GROUP :])


def solution(mesh):
    split = Mesh(mesh.devices.reshape(4, 4, 2, 2, 2), ("z", "y", "xh", "xl", "c"))
    rows = P(WIDE + NARROW_AXES, None)
    in_specs = (
        P(NARROW_AXES, WIDE),
        P(WIDE, None, None, None),
        P(WIDE, None),
        P(WIDE, None, None),
        P(WIDE),
        P(WIDE, None),
        P(None, NARROW_AXES, WIDE),
        P(), P(), P(), P(), P(), P(),
    )
    out_specs = (P(None, NARROW_AXES, WIDE), rows, rows, rows)
    return jax.shard_map(
        on_device, mesh=split, in_specs=in_specs, out_specs=out_specs, check_vma=False
    )
```

```python
import functools
import math

import jax
import jax.numpy as jnp
from jax import lax
from jax.experimental import pallas as pl
from jax.experimental.pallas import tpu as pltpu
from jax.sharding import Mesh, PartitionSpec as P

D = 512
FF = 2048
HEADS = 8
HEAD_DIM = 64
HOPS = 3
TOKS = 4
BLK = 128
K = 12
SEND = 2
NB = 32
PARTS = 16
FEATS = 64
NODES = NB * BLK
TRAIN = 512
OWNERS = 128
QUAD = 4
QUAD_NODES = 256
NARROW = 8
DESTS = 32
GROUP = 16
UNROLL = 8
PICK_BLOCKS = 4
FF_CHUNK = 512
EPSILON = 1e-05

BF = jnp.bfloat16
F32 = jnp.float32
WIDE = ("z", "y")
NARROW_AXES = ("xh", "xl", "c")
QUADS = ("z", "y", "xh")


def params(limit_mib):
    return pltpu.CompilerParams(vmem_limit_bytes=limit_mib * 1024 * 1024)


def dot(left, right):
    return jnp.dot(left, right, preferred_element_type=F32)


def dot_rows(left, right):
    return lax.dot_general(left, right, (((1,), (1,)), ((), ())), preferred_element_type=F32)


def pack_kernel(sends, field, owners, outgoing, counts, sems):
    copies = []
    for slot in range(PARTS * SEND):
        start = pl.multiple_of(sends[0, slot // SEND, slot % SEND] * BLK, BLK)
        rows = (slot % SEND) * FEATS
        copies.append(
            pltpu.make_async_copy(
                field.at[:, pl.ds(start, BLK)],
                outgoing.at[slot // SEND, rows : rows + FEATS, :],
                sems.at[slot],
            )
        )
    for copy in copies:
        copy.start()
    named = lax.broadcasted_iota(jnp.int32, (OWNERS, TRAIN), 0) == owners[...]
    count = jnp.sum(jnp.where(named, 1.0, 0.0), axis=1, keepdims=True)
    counts[...] = jnp.broadcast_to(count, (OWNERS, OWNERS))
    for copy in copies:
        copy.wait()


def pack(sends, field, owners):
    return pl.pallas_call(
        pack_kernel,
        out_shape=[
            jax.ShapeDtypeStruct((PARTS, SEND * FEATS, BLK), BF),
            jax.ShapeDtypeStruct((OWNERS, OWNERS), F32),
        ],
        in_specs=[
            pl.BlockSpec(memory_space=pltpu.SMEM),
            pl.BlockSpec(memory_space=pltpu.HBM),
            pl.BlockSpec(memory_space=pltpu.VMEM),
        ],
        scratch_shapes=[pltpu.SemaphoreType.DMA((PARTS * SEND,))],
        compiler_params=params(4),
        name="pack",
    )(sends, in_hbm(field), owners)


def picked_columns(ids, fields):
    id_row = ids[...]

    def add_blocks(i, total):
        for j in range(PICK_BLOCKS):
            b = i * PICK_BLOCKS + j
            rows = lax.broadcasted_iota(jnp.int32, (BLK, TRAIN), 0) + b * BLK
            chosen = jnp.where(rows == id_row, 1.0, 0.0).astype(BF)
            cols = pl.ds(pl.multiple_of(b * BLK, BLK), BLK)
            block = jnp.concatenate([field[:, cols] for field in fields], axis=0)
            total = total + dot(block, chosen)
        return total

    start = jnp.zeros((FEATS * len(fields), TRAIN), F32)
    return lax.fori_loop(0, NB // PICK_BLOCKS, add_blocks, start).astype(BF)


def apply_kernel(*refs, second, first, last, picking, stage):
    refs = list(refs)
    lists, sends, tiles, field, incoming = refs[:5]
    refs = refs[5:]
    degree = None if first else refs.pop(0)
    previous = refs.pop(0) if second else None
    aliased = second and refs.pop(0)
    ids = refs.pop(0) if picking else None
    others = [refs.pop(0) for _ in range(picking - 1)] if picking else []
    result = refs.pop(0)
    hops = refs.pop(0) if second else None
    outgoing = None if last else refs.pop(0)
    rows_out = refs.pop(0) if picking else None
    degree_out = refs.pop(0) if first else None
    tiles_h, tiles = (tiles, refs.pop(0)) if stage else (None, tiles)
    pool, fresh, sems = refs

    def load(i):
        blocks = pl.ds(i * UNROLL, UNROLL)
        return pltpu.make_async_copy(tiles_h.at[blocks], tiles.at[blocks], sems.at[i])

    if stage:
        for i in range(NB // UNROLL):
            load(i).start()

    for j in range(NB):
        pool[j] = field[:, j * BLK : (j + 1) * BLK]
    for j in range(PARTS * SEND):
        rows = (j % SEND) * FEATS
        pool[NB + j] = incoming[j // SEND, rows : rows + FEATS, :]

    def one_block(b):
        picked = jnp.concatenate([pool[lists[b, k]] for k in range(K)], axis=1)
        if first:
            picked = jnp.concatenate([picked, jnp.ones((GROUP, K * BLK), BF)], axis=0)
        summed = dot(picked, tiles[b].reshape(K * BLK, BLK))
        if first:
            share = summed[FEATS : FEATS + 1, :]
            degree_out[pl.ds(b, 1), :] = share
            summed = summed[:FEATS, :]
        else:
            share = degree[pl.ds(b, 1), :]
        value = (summed / share).astype(BF)
        cols = pl.ds(pl.multiple_of(b * BLK, BLK), BLK)
        if second:
            value = (
                0.5 * previous[:, cols].astype(F32) + pool[b].astype(F32) + value.astype(F32)
            ).astype(BF)
        result[:, cols] = value
        fresh[b] = value

    def some_blocks(i, carry):
        if stage:
            load(i).wait()
        for j in range(UNROLL):
            one_block(i * UNROLL + j)
        return carry

    lax.fori_loop(0, NB // UNROLL, some_blocks, 0)
    if second:
        store = pltpu.make_async_copy(result, hops.at[second - 1], sems.at[0])
        store.start()
    if not last:
        for slot in range(PARTS * SEND):
            rows = (slot % SEND) * FEATS
            outgoing[slot // SEND, rows : rows + FEATS, :] = fresh[
                sends[0, slot // SEND, slot % SEND]
            ]
    if picking:
        picked = picked_columns(ids, [*others, result])
        if last:
            for n in range(NARROW):
                half = n // QUAD
                rows_out[n] = picked[:, half * QUAD_NODES : (half + 1) * QUAD_NODES]
        else:
            rows_out[...] = picked
    if second:
        store.wait()


def apply(lists, sends, tiles, field, incoming, degree=None, previous=None, hops=None, hop=0, ids=None, others=(), stage=False):
    second = previous is not None
    last = second and hop == HOPS - 1
    first = hop == 0 and not second
    smem = pl.BlockSpec(memory_space=pltpu.SMEM)
    vmem = pl.BlockSpec(memory_space=pltpu.VMEM)
    hbm = pl.BlockSpec(memory_space=pltpu.HBM)
    operands = [lists, sends, in_hbm(tiles) if stage else in_vmem(tiles), field, incoming]
    in_specs = [smem, smem, hbm if stage else vmem, vmem, vmem]
    if not first:
        operands.append(degree)
        in_specs.append(vmem)
    out_shape = [jax.ShapeDtypeStruct((FEATS, NODES), BF)]
    out_specs = [vmem]
    aliases = {}
    if second:
        operands.append(previous)
        in_specs.append(vmem)
        if hops is None:
            operands.append(sends)
            in_specs.append(smem)
        else:
            aliases = {len(operands): 1}
            operands.append(hops)
            in_specs.append(hbm)
        out_shape.append(jax.ShapeDtypeStruct((HOPS, FEATS, NODES), BF))
        out_specs.append(hbm)
    if ids is not None:
        operands += [ids, *others]
        in_specs += [vmem] * (1 + len(others))
    if not last:
        out_shape.append(jax.ShapeDtypeStruct((PARTS, SEND * FEATS, BLK), BF))
        out_specs.append(vmem)
    if ids is not None:
        rows = FEATS * (1 + len(others))
        shape = (NARROW, rows, QUAD_NODES) if last else (rows, TRAIN)
        out_shape.append(jax.ShapeDtypeStruct(shape, BF))
        out_specs.append(vmem)
    if first:
        out_shape.append(jax.ShapeDtypeStruct((NB, BLK), F32))
        out_specs.append(vmem)
    if stage:
        out_shape.append(pltpu.VMEM(tiles.shape, BF))
        out_specs.append(vmem)
    scratch = [
        pltpu.VMEM((2 * NB, FEATS, BLK), BF),
        pltpu.VMEM((NB, FEATS, BLK), BF),
        pltpu.SemaphoreType.DMA((NB // UNROLL,)),
    ]
    return pl.pallas_call(
        functools.partial(
            apply_kernel, second=second and hop + 1, first=first, last=last,
            picking=0 if ids is None else 1 + len(others), stage=stage,
        ),
        out_shape=out_shape,
        in_specs=in_specs,
        out_specs=out_specs,
        scratch_shapes=scratch,
        input_output_aliases=aliases,
        compiler_params=params(8),
        name=f"apply_{'second' if second else 'first'}_{hop}",
    )(*operands)


def layer_kernel(
    place, early_h, grads_h, final, counts, owners,
    query_h, key_h, value_h, out_h, out_th, up_h, up_th, down_h,
    result, query_s, key_s, value_s, mixed_s, probs_s, act_s, pre_s, gmix_s, gq_s, gk_s, gv_s, gr_s,
    query_w, key_w, value_w, out_w, out_t, up_w, up_t, down_w, early, grads, sems,
):
    own = place[0]
    mine = pl.ds(pl.multiple_of(place[1] * QUAD_NODES, QUAD_NODES), QUAD_NODES)
    pairs = (
        (query_h, query_w), (key_h, key_w), (value_h, value_w), (out_h, out_w),
        (up_h, up_w), (down_h, down_w), (up_th, up_t), (out_th, out_t),
        (early_h.at[:, :, mine], early), (grads_h.at[:, :, mine], grads),
    )
    loads = [
        pltpu.make_async_copy(source, target, sems.at[index])
        for index, (source, target) in enumerate(pairs)
    ]
    for index in (8, 0, 1, 2, 9, 3, 4, 5, 6, 7):
        loads[index].start()
    width = TOKS * QUAD_NODES
    loads[8].wait()
    tokens = jnp.concatenate(
        [early[:, t * FEATS : (t + 1) * FEATS, :].reshape(D, QUAD_NODES) for t in range(HOPS)]
        + [final[...].reshape(D, QUAD_NODES)],
        axis=1,
    )

    def normalize(hidden):
        center = hidden - jnp.mean(hidden, axis=0, keepdims=True)
        inverse = lax.rsqrt(jnp.mean(center * center, axis=0, keepdims=True) + EPSILON)
        return center * inverse, inverse

    normed_a = normalize(tokens.astype(F32))[0].astype(BF)
    loads[0].wait()
    query_s[...] = dot(query_w[...], normed_a).astype(BF)
    loads[1].wait()
    key_s[...] = dot(key_w[...], normed_a).astype(BF)
    loads[2].wait()
    value_s[...] = dot(value_w[...], normed_a).astype(BF)
    score_scale = 1.0 / math.sqrt(HEAD_DIM)

    def columns(half):
        return [
            pl.ds(pl.multiple_of(t * QUAD_NODES + half * BLK, BLK), BLK) for t in range(TOKS)
        ]

    def parts(ref, rows, cols):
        return [ref[rows, c].astype(F32) for c in cols]

    def forward_head(step, carry):
        h = step // 2
        cols = columns(step % 2)
        rows = pl.ds(pl.multiple_of(h * HEAD_DIM, HEAD_DIM), HEAD_DIM)
        query, key, value = [parts(ref, rows, cols) for ref in (query_s, key_s, value_s)]
        all_probs = []
        for t in range(TOKS):
            scores = [
                jnp.sum(query[t] * key[u], axis=0, keepdims=True) * score_scale
                for u in range(TOKS)
            ]
            top = jnp.maximum(
                jnp.maximum(scores[0], scores[1]), jnp.maximum(scores[2], scores[3])
            )
            raised = [jnp.exp(s - top) for s in scores]
            total = raised[0] + raised[1] + raised[2] + raised[3]
            probs = [r / total for r in raised]
            all_probs += probs
            low = [p.astype(BF).astype(F32) for p in probs]
            mixed_s[rows, cols[t]] = (
                low[0] * value[0] + low[1] * value[1] + low[2] * value[2] + low[3] * value[3]
            ).astype(BF)
        probs_s[step] = jnp.concatenate(all_probs, axis=0)
        return carry

    lax.fori_loop(0, 2 * HEADS, forward_head, 0)
    loads[3].wait()
    residual = (tokens.astype(F32) + dot(out_w[...], mixed_s[...])).astype(BF)
    second_norm, second_inv = normalize(residual.astype(F32))
    normed_b = second_norm.astype(BF)

    root = math.sqrt(2.0 / math.pi)
    groups = FF_CHUNK // (QUAD * GROUP)

    loads[9].wait()
    named = lax.broadcasted_iota(jnp.int32, (OWNERS, QUAD_NODES), 0) == owners[:, mine]
    by_owner = jnp.concatenate([1.0 / counts[...]] * (QUAD_NODES // OWNERS), axis=1)
    row_scale = jnp.sum(jnp.where(named, by_owner, 0.0), axis=0, keepdims=True)
    scaled = jnp.concatenate(
        [
            (
                grads[:, t * FEATS : (t + 1) * FEATS, :].reshape(D, QUAD_NODES).astype(F32)
                * row_scale
            ).astype(BF)
            for t in range(TOKS)
        ],
        axis=1,
    )

    def ffn_chunk(i, carry):
        rows = pl.ds(pl.multiple_of(i * FF_CHUNK, FF_CHUNK), FF_CHUNK)
        pre = dot(up_w[rows, :], normed_b)
        grad_act = dot(down_w[rows, :], scaled)
        square = pre * pre
        gate = 0.5 + 0.5 * jnp.tanh(pre * (root + (root * 0.044715) * square))
        activated = pre * gate
        slope = gate + activated * (1.0 - gate) * (
            2.0 * root + (6.0 * root * 0.044715) * square
        )
        at = pl.ds(i * groups, groups)
        act_s[at] = activated.astype(BF).reshape(groups, QUAD, GROUP, width)
        pre_s[at] = (grad_act * slope).astype(BF).reshape(groups, QUAD, GROUP, width)
        return carry

    loads[4].wait()
    loads[5].wait()
    lax.fori_loop(0, FF // FF_CHUNK, ffn_chunk, 0)

    share = FF // QUAD
    grad_down = dot_rows(act_s[:, own].reshape(share, width), scaled)
    result[:, 2 * GROUP : 3 * GROUP, :] = grad_down.astype(BF).reshape(DESTS, GROUP, D)
    grad_up = dot_rows(pre_s[:, own].reshape(share, width), normed_b)
    result[:, GROUP : 2 * GROUP, :] = grad_up.astype(BF).reshape(DESTS, GROUP, D)

    loads[6].wait()
    grad_normed = dot(up_t[...], pre_s[...].reshape(FF, width))
    grad_resid = (
        scaled.astype(F32)
        + second_inv
        * (
            grad_normed
            - jnp.mean(grad_normed, axis=0, keepdims=True)
            - second_norm * jnp.mean(grad_normed * second_norm, axis=0, keepdims=True)
        )
    ).astype(BF)
    gr_s[...] = grad_resid.reshape(HEADS, QUAD, GROUP, width)
    loads[7].wait()
    gmix_s[...] = dot(out_t[...], grad_resid).astype(BF)

    def backward_head(step, carry):
        h = step // 2
        cols = columns(step % 2)
        rows = pl.ds(pl.multiple_of(h * HEAD_DIM, HEAD_DIM), HEAD_DIM)
        query, key, value, grad_mixed = [
            parts(ref, rows, cols) for ref in (query_s, key_s, value_s, gmix_s)
        ]
        saved = probs_s[step]
        prob = lambda t, u: saved[t * TOKS + u : t * TOKS + u + 1, :]
        weights = []
        grad_query = []
        for t in range(TOKS):
            grad_probs = [
                jnp.sum(grad_mixed[t] * value[u], axis=0, keepdims=True) for u in range(TOKS)
            ]
            inner = sum(prob(t, u) * grad_probs[u] for u in range(TOKS))
            weight = [
                (prob(t, u) * (grad_probs[u] - inner) * score_scale).astype(BF).astype(F32)
                for u in range(TOKS)
            ]
            weights.append(weight)
            grad_query.append(sum(weight[u] * key[u] for u in range(TOKS)))
        grad_key = [sum(weights[t][u] * query[t] for t in range(TOKS)) for u in range(TOKS)]
        grad_value = [
            sum(prob(t, u).astype(BF).astype(F32) * grad_mixed[t] for t in range(TOKS))
            for u in range(TOKS)
        ]
        for ref, pieces in ((gq_s, grad_query), (gk_s, grad_key), (gv_s, grad_value)):
            for t in range(TOKS):
                ref[h, :, :, cols[t]] = pieces[t].astype(BF).reshape(QUAD, GROUP, BLK)
        return carry

    lax.fori_loop(0, 2 * HEADS, backward_head, 0)
    share = D // QUAD
    stacked = jnp.concatenate(
        [ref[:, own].reshape(share, width) for ref in (gq_s, gk_s, gv_s)], axis=0
    )
    count = HEADS * 3
    result[:count, 0:GROUP, :] = dot_rows(stacked, normed_a).astype(BF).reshape(count, GROUP, D)
    sum_out = dot_rows(gr_s[:, own].reshape(share, width), mixed_s[...])
    result[count:, 0:GROUP, :] = sum_out.astype(BF).reshape(HEADS, GROUP, D)


def in_vmem(array):
    return pltpu.with_memory_space_constraint(array, pltpu.VMEM)


def in_hbm(array):
    return pltpu.with_memory_space_constraint(array, pltpu.HBM)


def layer(place, early, grads, final, counts, owners, *weights):
    width = TOKS * QUAD_NODES
    square = pltpu.VMEM((D, width), BF)
    grouped = pltpu.VMEM((HEADS, QUAD, GROUP, width), BF)
    wide = pltpu.VMEM((DESTS, QUAD, GROUP, width), BF)
    vmem = pl.BlockSpec(memory_space=pltpu.VMEM)
    hbm = pl.BlockSpec(memory_space=pltpu.HBM)
    smem = pl.BlockSpec(memory_space=pltpu.SMEM)
    return pl.pallas_call(
        layer_kernel,
        out_shape=jax.ShapeDtypeStruct((DESTS, 3 * GROUP, D), BF),
        in_specs=[smem, hbm, hbm, vmem, vmem, vmem] + [hbm] * 8,
        out_specs=vmem,
        scratch_shapes=[
            square, square, square, square,
            pltpu.VMEM((2 * HEADS, TOKS * TOKS, BLK), F32),
            wide, wide, square, grouped, grouped, grouped, grouped,
            *[pltpu.VMEM(w.shape, BF) for w in weights],
            pltpu.VMEM((NARROW, HOPS * FEATS, QUAD_NODES), BF),
            pltpu.VMEM((NARROW, TOKS * FEATS, QUAD_NODES), BF),
            pltpu.SemaphoreType.DMA((len(weights) + 2,)),
        ],
        compiler_params=params(44),
        name="layer",
    )(
        place, in_hbm(early), in_hbm(grads), final, counts, owners,
        *[in_hbm(w) for w in weights],
    )


def exchange(array, axes):
    return lax.all_to_all(array, axes, split_axis=0, concat_axis=0, tiled=True)


def on_device(
    features, edge_tiles, block_lists, send_lists, train_ids, owners, cotangent,
    query_weight, key_weight, value_weight, out_weight, up_weight, down_weight,
):
    ids = train_ids.reshape(1, TRAIN)
    grads = lax.all_gather(cotangent.reshape(TOKS * FEATS, TRAIN), NARROW_AXES)
    owner_row = owners.reshape(1, TRAIN)
    outgoing, counts = pack(send_lists, features, owner_row)
    counts = lax.psum(counts, WIDE)
    incoming = exchange(outgoing, WIDE)
    incoming, up_t, out_t = lax.optimization_barrier((incoming, up_weight.T, out_weight.T))
    step = functools.partial(apply, block_lists, send_lists)
    current = features
    hops = None
    fields = [features]
    for hop in range(HOPS):
        if hop == 0:
            once, outgoing, degree, tiles = step(edge_tiles, current, incoming, stage=True)
        elif hop == HOPS - 1:
            once, outgoing, tiles = step(
                edge_tiles, current, incoming, degree, hop=hop, stage=True
            )
        else:
            once, outgoing = step(tiles, current, incoming, degree, hop=hop)
        incoming = exchange(outgoing, WIDE)
        results = step(
            tiles, once, incoming, degree, previous=current, hops=hops, hop=hop,
            ids=None if hop == 0 else ids,
            others=tuple(fields) if hop == HOPS - 2 else (),
        )
        current, hops = results[0], results[1]
        fields.append(current)
        if hop == HOPS - 2:
            early = lax.all_gather(results[3], NARROW_AXES)
        if hop < HOPS - 1:
            incoming = exchange(results[2], WIDE)
    final = exchange(results[2], NARROW_AXES)

    place = jnp.stack(
        [2 * lax.axis_index("xl") + lax.axis_index("c"), lax.axis_index("xh")]
    ).astype(jnp.int32)
    partial = layer(
        place, early, grads, final, counts, owner_row,
        query_weight, key_weight, value_weight, out_weight, out_t, up_weight, up_t, down_weight,
    )
    gathered = exchange(partial, QUADS)
    sums = jnp.sum(gathered.astype(F32), axis=0)
    return (hops, sums[:GROUP], sums[GROUP : 2 * GROUP], sums[2 * GROUP :])


def solution(mesh):
    split = Mesh(mesh.devices.reshape(4, 4, 2, 2, 2), ("z", "y", "xh", "xl", "c"))
    rows = P(WIDE + NARROW_AXES, None)
    in_specs = (
        P(NARROW_AXES, WIDE),
        P(WIDE, None, None, None),
        P(WIDE, None),
        P(WIDE, None, None),
        P(WIDE),
        P(WIDE, None),
        P(None, NARROW_AXES, WIDE),
        P(), P(), P(), P(), P(), P(),
    )
    out_specs = (P(None, NARROW_AXES, WIDE), rows, rows, rows)
    return jax.shard_map(
        on_device, mesh=split, in_specs=in_specs, out_specs=out_specs, check_vma=False
    )
```

```python
import functools
import math

import jax
import jax.numpy as jnp
from jax import lax
from jax.experimental import pallas as pl
from jax.experimental.pallas import tpu as pltpu
from jax.sharding import Mesh, PartitionSpec as P

D = 512
FF = 2048
HEADS = 8
HEAD_DIM = 64
HOPS = 3
TOKS = 4
BLK = 128
K = 12
SEND = 2
NB = 32
PARTS = 16
FEATS = 64
NODES = NB * BLK
TRAIN = 512
OWNERS = 128
QUAD = 4
QUAD_NODES = 256
NARROW = 8
DESTS = 32
GROUP = 16
UNROLL = 16
CHUNK = 4
IN_FLIGHT = 3
PICK_BLOCKS = 4
FF_CHUNK = 512
EPSILON = 1e-05

BF = jnp.bfloat16
F32 = jnp.float32
WIDE = ("z", "y")
NARROW_AXES = ("xh", "xl", "c")
QUADS = ("z", "y", "xh")


def params(limit_mib):
    return pltpu.CompilerParams(vmem_limit_bytes=limit_mib * 1024 * 1024)


def dot(left, right):
    return jnp.dot(left, right, preferred_element_type=F32)


def dot_rows(left, right):
    return lax.dot_general(left, right, (((1,), (1,)), ((), ())), preferred_element_type=F32)


def block_columns(b):
    return pl.ds(b * BLK if isinstance(b, int) else pl.multiple_of(b * BLK, BLK), BLK)


def pack_kernel(sends, field, owners_h, outgoing, counts, owners, sems):
    names = pltpu.make_async_copy(owners_h, owners, sems.at[PARTS * SEND])
    names.start()
    copies = []
    for slot in range(PARTS * SEND):
        start = pl.multiple_of(sends[0, slot // SEND, slot % SEND] * BLK, BLK)
        rows = (slot % SEND) * FEATS
        copies.append(
            pltpu.make_async_copy(
                field.at[:, pl.ds(start, BLK)],
                outgoing.at[slot // SEND, rows : rows + FEATS, :],
                sems.at[slot],
            )
        )
    for copy in copies:
        copy.start()
    names.wait()
    named = lax.broadcasted_iota(jnp.int32, (OWNERS, TRAIN), 0) == owners[...]
    count = jnp.sum(jnp.where(named, 1.0, 0.0), axis=1, keepdims=True)
    counts[...] = jnp.broadcast_to(count, (OWNERS, OWNERS))
    for copy in copies:
        copy.wait()


def pack(sends, field, owners):
    return pl.pallas_call(
        pack_kernel,
        out_shape=[
            jax.ShapeDtypeStruct((PARTS, SEND * FEATS, BLK), BF),
            jax.ShapeDtypeStruct((OWNERS, OWNERS), F32),
        ],
        in_specs=[
            pl.BlockSpec(memory_space=pltpu.SMEM),
            pl.BlockSpec(memory_space=pltpu.HBM),
            pl.BlockSpec(memory_space=pltpu.HBM),
        ],
        scratch_shapes=[
            pltpu.VMEM((1, TRAIN), jnp.int32),
            pltpu.SemaphoreType.DMA((PARTS * SEND + 1,)),
        ],
        compiler_params=params(4),
        name="pack",
    )(sends, in_hbm(field), in_hbm(owners))


def picked_columns(ids, fields):
    id_row = ids[...]
    span = PICK_BLOCKS * BLK
    total = None
    for start in range(0, NODES, span):
        rows = lax.broadcasted_iota(jnp.int32, (span, TRAIN), 0) + start
        chosen = jnp.where(rows == id_row, 1.0, 0.0).astype(BF)
        block = jnp.concatenate([field[:, start : start + span] for field in fields], axis=0)
        term = dot(block, chosen)
        total = term if total is None else total + term
    return total.astype(BF)


def apply_kernel(*refs, second, first, last, picking, stage):
    refs = list(refs)
    lists, sends, tiles, field, incoming = refs[:5]
    refs = refs[5:]
    degree = None if first else refs.pop(0)
    previous = refs.pop(0) if second else None
    aliased = second and refs.pop(0)
    ids = refs.pop(0) if picking else None
    others = [refs.pop(0) for _ in range(picking - 1)] if picking else []
    result = refs.pop(0)
    hops = refs.pop(0) if second else None
    outgoing = None if last else refs.pop(0)
    rows_out = refs.pop(0) if picking else None
    degree_out = refs.pop(0) if first else None
    tiles_h, tiles = (tiles, refs.pop(0)) if stage else (None, tiles)
    pool, fresh, sems = refs

    def load(i):
        blocks = pl.ds(i * CHUNK, CHUNK)
        return pltpu.make_async_copy(tiles_h.at[blocks], tiles.at[blocks], sems.at[i])

    def store(i):
        cols = pl.ds(pl.multiple_of(i * UNROLL * BLK, UNROLL * BLK), UNROLL * BLK)
        return pltpu.make_async_copy(
            result.at[:, cols], hops.at[second - 1, :, cols], sems.at[i]
        )

    if stage:
        for i in range(IN_FLIGHT):
            load(i).start()

    for j in range(NB):
        pool[j] = field[:, j * BLK : (j + 1) * BLK]
    for j in range(PARTS * SEND):
        rows = (j % SEND) * FEATS
        pool[NB + j] = incoming[j // SEND, rows : rows + FEATS, :]

    def one_block(b):
        picked = jnp.concatenate([pool[lists[b, k]] for k in range(K)], axis=1)
        if first:
            picked = jnp.concatenate([picked, jnp.ones((GROUP, K * BLK), BF)], axis=0)
        summed = dot(picked, tiles[b].reshape(K * BLK, BLK))
        if first:
            share = summed[FEATS : FEATS + 1, :]
            degree_out[pl.ds(b, 1), :] = share
            summed = summed[:FEATS, :]
        else:
            share = degree[pl.ds(b, 1), :]
        value = (summed / share).astype(BF)
        cols = block_columns(b)
        if second:
            value = (
                0.5 * previous[:, cols].astype(F32) + pool[b].astype(F32) + value.astype(F32)
            ).astype(BF)
        result[:, cols] = value
        fresh[b] = value

    def some_blocks(i, carry):
        for j in range(UNROLL):
            one_block(i * UNROLL + j)
        if second:
            store(i).start()
        return carry

    if stage:
        for i in range(NB // CHUNK):
            load(i).wait()
            if i + IN_FLIGHT < NB // CHUNK:
                load(i + IN_FLIGHT).start()
            for j in range(CHUNK):
                one_block(i * CHUNK + j)
    else:
        lax.fori_loop(0, NB // UNROLL, some_blocks, 0)
    if not last:
        for slot in range(PARTS * SEND):
            rows = (slot % SEND) * FEATS
            outgoing[slot // SEND, rows : rows + FEATS, :] = fresh[
                sends[0, slot // SEND, slot % SEND]
            ]
    if picking:
        picked = picked_columns(ids, [*others, result])
        if last:
            for n in range(NARROW):
                half = n // QUAD
                rows_out[n] = picked[:, half * QUAD_NODES : (half + 1) * QUAD_NODES]
        else:
            rows_out[...] = picked
    if second:
        for i in range(NB // UNROLL):
            store(i).wait()


def apply(lists, sends, tiles, field, incoming, degree=None, previous=None, hops=None, hop=0, ids=None, others=(), stage=False):
    second = previous is not None
    last = second and hop == HOPS - 1
    first = hop == 0 and not second
    smem = pl.BlockSpec(memory_space=pltpu.SMEM)
    vmem = pl.BlockSpec(memory_space=pltpu.VMEM)
    hbm = pl.BlockSpec(memory_space=pltpu.HBM)
    operands = [lists, sends, in_hbm(tiles) if stage else in_vmem(tiles), field, incoming]
    in_specs = [smem, smem, hbm if stage else vmem, vmem, vmem]
    if not first:
        operands.append(degree)
        in_specs.append(vmem)
    out_shape = [jax.ShapeDtypeStruct((FEATS, NODES), BF)]
    out_specs = [vmem]
    aliases = {}
    if second:
        operands.append(previous)
        in_specs.append(vmem)
        if hops is None:
            operands.append(sends)
            in_specs.append(smem)
        else:
            aliases = {len(operands): 1}
            operands.append(hops)
            in_specs.append(hbm)
        out_shape.append(jax.ShapeDtypeStruct((HOPS, FEATS, NODES), BF))
        out_specs.append(hbm)
    if ids is not None:
        operands += [ids, *others]
        in_specs += [vmem] * (1 + len(others))
    if not last:
        out_shape.append(jax.ShapeDtypeStruct((PARTS, SEND * FEATS, BLK), BF))
        out_specs.append(vmem)
    if ids is not None:
        rows = FEATS * (1 + len(others))
        shape = (NARROW, rows, QUAD_NODES) if last else (rows, TRAIN)
        out_shape.append(jax.ShapeDtypeStruct(shape, BF))
        out_specs.append(vmem)
    if first:
        out_shape.append(jax.ShapeDtypeStruct((NB, BLK), F32))
        out_specs.append(vmem)
    if stage:
        out_shape.append(pltpu.VMEM(tiles.shape, BF))
        out_specs.append(vmem)
    scratch = [
        pltpu.VMEM((2 * NB, FEATS, BLK), BF),
        pltpu.VMEM((NB, FEATS, BLK), BF),
        pltpu.SemaphoreType.DMA((NB // CHUNK,)),
    ]
    return pl.pallas_call(
        functools.partial(
            apply_kernel, second=second and hop + 1, first=first, last=last,
            picking=0 if ids is None else 1 + len(others), stage=stage,
        ),
        out_shape=out_shape,
        in_specs=in_specs,
        out_specs=out_specs,
        scratch_shapes=scratch,
        input_output_aliases=aliases,
        compiler_params=params(8),
        name=f"apply_{'second' if second else 'first'}_{hop}",
    )(*operands)


def layer_kernel(
    place, early_h, grads_h, final, counts_h, owners_h,
    query_h, key_h, value_h, out_h, out_th, up_h, up_th, down_h,
    result, query_s, key_s, value_s, mixed_s, probs_s, act_s, pre_s, gmix_s, gq_s, gk_s, gv_s, gr_s,
    query_w, key_w, value_w, out_w, out_t, up_w, up_t, down_w, early, grads, counts, owners, sems,
):
    own = place[0]
    mine = pl.ds(pl.multiple_of(place[1] * QUAD_NODES, QUAD_NODES), QUAD_NODES)
    pairs = (
        (query_h, query_w), (key_h, key_w), (value_h, value_w), (out_h, out_w),
        (up_h, up_w), (down_h, down_w), (up_th, up_t), (out_th, out_t),
        (early_h.at[:, :, mine], early), (grads_h.at[:, :, mine], grads),
        (counts_h, counts), (owners_h, owners),
    )
    loads = [
        pltpu.make_async_copy(source, target, sems.at[index])
        for index, (source, target) in enumerate(pairs)
    ]
    for index in (8, 0, 1, 2, 10, 11, 9, 3, 4, 5, 6, 7):
        loads[index].start()
    width = TOKS * QUAD_NODES
    loads[8].wait()
    tokens = jnp.concatenate(
        [early[:, t * FEATS : (t + 1) * FEATS, :].reshape(D, QUAD_NODES) for t in range(HOPS)]
        + [final[...].reshape(D, QUAD_NODES)],
        axis=1,
    )

    def normalize(hidden):
        center = hidden - jnp.mean(hidden, axis=0, keepdims=True)
        inverse = lax.rsqrt(jnp.mean(center * center, axis=0, keepdims=True) + EPSILON)
        return center * inverse, inverse

    normed_a = normalize(tokens.astype(F32))[0].astype(BF)
    loads[0].wait()
    query_s[...] = dot(query_w[...], normed_a).astype(BF)
    loads[1].wait()
    key_s[...] = dot(key_w[...], normed_a).astype(BF)
    loads[2].wait()
    value_s[...] = dot(value_w[...], normed_a).astype(BF)
    score_scale = 1.0 / math.sqrt(HEAD_DIM)

    def columns(half):
        return [
            pl.ds(pl.multiple_of(t * QUAD_NODES + half * BLK, BLK), BLK) for t in range(TOKS)
        ]

    def parts(ref, rows, cols):
        return [ref[rows, c].astype(F32) for c in cols]

    def forward_head(step, carry):
        h = step // 2
        cols = columns(step % 2)
        rows = pl.ds(pl.multiple_of(h * HEAD_DIM, HEAD_DIM), HEAD_DIM)
        query, key, value = [parts(ref, rows, cols) for ref in (query_s, key_s, value_s)]
        all_probs = []
        for t in range(TOKS):
            scores = [
                jnp.sum(query[t] * key[u], axis=0, keepdims=True) * score_scale
                for u in range(TOKS)
            ]
            top = jnp.maximum(
                jnp.maximum(scores[0], scores[1]), jnp.maximum(scores[2], scores[3])
            )
            raised = [jnp.exp(s - top) for s in scores]
            total = raised[0] + raised[1] + raised[2] + raised[3]
            probs = [r / total for r in raised]
            all_probs += probs
            low = [p.astype(BF).astype(F32) for p in probs]
            mixed_s[rows, cols[t]] = (
                low[0] * value[0] + low[1] * value[1] + low[2] * value[2] + low[3] * value[3]
            ).astype(BF)
        probs_s[step] = jnp.concatenate(all_probs, axis=0)
        return carry

    lax.fori_loop(0, 2 * HEADS, forward_head, 0)
    loads[3].wait()
    residual = (tokens.astype(F32) + dot(out_w[...], mixed_s[...])).astype(BF)
    second_norm, second_inv = normalize(residual.astype(F32))
    normed_b = second_norm.astype(BF)

    root = math.sqrt(2.0 / math.pi)
    groups = FF_CHUNK // (QUAD * GROUP)

    loads[9].wait()
    loads[10].wait()
    loads[11].wait()
    named = lax.broadcasted_iota(jnp.int32, (OWNERS, QUAD_NODES), 0) == owners[:, mine]
    by_owner = jnp.concatenate([1.0 / counts[...]] * (QUAD_NODES // OWNERS), axis=1)
    row_scale = jnp.sum(jnp.where(named, by_owner, 0.0), axis=0, keepdims=True)
    scaled = jnp.concatenate(
        [
            (
                grads[:, t * FEATS : (t + 1) * FEATS, :].reshape(D, QUAD_NODES).astype(F32)
                * row_scale
            ).astype(BF)
            for t in range(TOKS)
        ],
        axis=1,
    )

    def ffn_chunk(i, carry):
        rows = pl.ds(pl.multiple_of(i * FF_CHUNK, FF_CHUNK), FF_CHUNK)
        pre = dot(up_w[rows, :], normed_b)
        grad_act = dot(down_w[rows, :], scaled)
        square = pre * pre
        gate = 0.5 + 0.5 * jnp.tanh(pre * (root + (root * 0.044715) * square))
        activated = pre * gate
        slope = gate + activated * (1.0 - gate) * (
            2.0 * root + (6.0 * root * 0.044715) * square
        )
        at = pl.ds(i * groups, groups)
        act_s[at] = activated.astype(BF).reshape(groups, QUAD, GROUP, width)
        pre_s[at] = (grad_act * slope).astype(BF).reshape(groups, QUAD, GROUP, width)
        return carry

    loads[4].wait()
    loads[5].wait()
    lax.fori_loop(0, FF // FF_CHUNK, ffn_chunk, 0)

    share = FF // QUAD
    grad_down = dot_rows(act_s[:, own].reshape(share, width), scaled)
    result[:, 2 * GROUP : 3 * GROUP, :] = grad_down.astype(BF).reshape(DESTS, GROUP, D)
    grad_up = dot_rows(pre_s[:, own].reshape(share, width), normed_b)
    result[:, GROUP : 2 * GROUP, :] = grad_up.astype(BF).reshape(DESTS, GROUP, D)

    loads[6].wait()
    grad_normed = dot(up_t[...], pre_s[...].reshape(FF, width))
    grad_resid = (
        scaled.astype(F32)
        + second_inv
        * (
            grad_normed
            - jnp.mean(grad_normed, axis=0, keepdims=True)
            - second_norm * jnp.mean(grad_normed * second_norm, axis=0, keepdims=True)
        )
    ).astype(BF)
    gr_s[...] = grad_resid.reshape(HEADS, QUAD, GROUP, width)
    loads[7].wait()
    gmix_s[...] = dot(out_t[...], grad_resid).astype(BF)

    def backward_head(step, carry):
        h = step // 2
        cols = columns(step % 2)
        rows = pl.ds(pl.multiple_of(h * HEAD_DIM, HEAD_DIM), HEAD_DIM)
        query, key, value, grad_mixed = [
            parts(ref, rows, cols) for ref in (query_s, key_s, value_s, gmix_s)
        ]
        saved = probs_s[step]
        prob = lambda t, u: saved[t * TOKS + u : t * TOKS + u + 1, :]
        weights = []
        grad_query = []
        for t in range(TOKS):
            grad_probs = [
                jnp.sum(grad_mixed[t] * value[u], axis=0, keepdims=True) for u in range(TOKS)
            ]
            inner = sum(prob(t, u) * grad_probs[u] for u in range(TOKS))
            weight = [
                (prob(t, u) * (grad_probs[u] - inner) * score_scale).astype(BF).astype(F32)
                for u in range(TOKS)
            ]
            weights.append(weight)
            grad_query.append(sum(weight[u] * key[u] for u in range(TOKS)))
        grad_key = [sum(weights[t][u] * query[t] for t in range(TOKS)) for u in range(TOKS)]
        grad_value = [
            sum(prob(t, u).astype(BF).astype(F32) * grad_mixed[t] for t in range(TOKS))
            for u in range(TOKS)
        ]
        for ref, pieces in ((gq_s, grad_query), (gk_s, grad_key), (gv_s, grad_value)):
            for t in range(TOKS):
                ref[h, :, :, cols[t]] = pieces[t].astype(BF).reshape(QUAD, GROUP, BLK)
        return carry

    lax.fori_loop(0, 2 * HEADS, backward_head, 0)
    share = D // QUAD
    stacked = jnp.concatenate(
        [ref[:, own].reshape(share, width) for ref in (gq_s, gk_s, gv_s)], axis=0
    )
    count = HEADS * 3
    result[:count, 0:GROUP, :] = dot_rows(stacked, normed_a).astype(BF).reshape(count, GROUP, D)
    sum_out = dot_rows(gr_s[:, own].reshape(share, width), mixed_s[...])
    result[count:, 0:GROUP, :] = sum_out.astype(BF).reshape(HEADS, GROUP, D)


def in_vmem(array):
    return pltpu.with_memory_space_constraint(array, pltpu.VMEM)


def in_hbm(array):
    return pltpu.with_memory_space_constraint(array, pltpu.HBM)


def layer(place, early, grads, final, counts, owners, *weights):
    width = TOKS * QUAD_NODES
    square = pltpu.VMEM((D, width), BF)
    grouped = pltpu.VMEM((HEADS, QUAD, GROUP, width), BF)
    wide = pltpu.VMEM((DESTS, QUAD, GROUP, width), BF)
    vmem = pl.BlockSpec(memory_space=pltpu.VMEM)
    hbm = pl.BlockSpec(memory_space=pltpu.HBM)
    smem = pl.BlockSpec(memory_space=pltpu.SMEM)
    return pl.pallas_call(
        layer_kernel,
        out_shape=jax.ShapeDtypeStruct((DESTS, 3 * GROUP, D), BF),
        in_specs=[smem, hbm, hbm, vmem, hbm, hbm] + [hbm] * 8,
        out_specs=vmem,
        scratch_shapes=[
            square, square, square, square,
            pltpu.VMEM((2 * HEADS, TOKS * TOKS, BLK), F32),
            wide, wide, square, grouped, grouped, grouped, grouped,
            *[pltpu.VMEM(w.shape, BF) for w in weights],
            pltpu.VMEM((NARROW, HOPS * FEATS, QUAD_NODES), BF),
            pltpu.VMEM((NARROW, TOKS * FEATS, QUAD_NODES), BF),
            pltpu.VMEM((OWNERS, OWNERS), F32),
            pltpu.VMEM((1, TRAIN), jnp.int32),
            pltpu.SemaphoreType.DMA((len(weights) + 4,)),
        ],
        compiler_params=params(44),
        name="layer",
    )(
        place, in_hbm(early), in_hbm(grads), final, in_hbm(counts), in_hbm(owners),
        *[in_hbm(w) for w in weights],
    )


def sum_kernel(gathered, *outs):
    total = jnp.sum(gathered[...].astype(F32), axis=0)
    for index, out in enumerate(outs):
        out[...] = total[index * GROUP : (index + 1) * GROUP]


def sum_parts(gathered):
    return pl.pallas_call(
        sum_kernel,
        out_shape=[jax.ShapeDtypeStruct((GROUP, D), F32)] * 3,
        compiler_params=params(8),
        name="sum_parts",
    )(gathered)


def exchange(array, axes):
    return lax.all_to_all(array, axes, split_axis=0, concat_axis=0, tiled=True)


def on_device(
    features, edge_tiles, block_lists, send_lists, train_ids, owners, cotangent,
    query_weight, key_weight, value_weight, out_weight, up_weight, down_weight,
):
    ids = train_ids.reshape(1, TRAIN)
    grads = lax.all_gather(cotangent.reshape(TOKS * FEATS, TRAIN), NARROW_AXES)
    owner_row = owners.reshape(1, TRAIN)
    outgoing, counts = pack(send_lists, features, owner_row)
    counts = lax.psum(counts, WIDE)
    incoming = exchange(outgoing, WIDE)
    incoming, up_t, out_t = lax.optimization_barrier((incoming, up_weight.T, out_weight.T))
    step = functools.partial(apply, block_lists, send_lists)
    current = features
    hops = None
    fields = [features]
    for hop in range(HOPS):
        if hop == 0:
            once, outgoing, degree, tiles = step(edge_tiles, current, incoming, stage=True)
        elif hop == HOPS - 1:
            once, outgoing, tiles = step(
                edge_tiles, current, incoming, degree, hop=hop, stage=True
            )
        else:
            once, outgoing = step(tiles, current, incoming, degree, hop=hop)
        incoming = exchange(outgoing, WIDE)
        results = step(
            tiles, once, incoming, degree, previous=current, hops=hops, hop=hop,
            ids=None if hop == 0 else ids,
            others=tuple(fields) if hop == HOPS - 2 else (),
        )
        current, hops = results[0], results[1]
        fields.append(current)
        if hop == HOPS - 2:
            early = lax.all_gather(results[3], NARROW_AXES)
        if hop < HOPS - 1:
            incoming = exchange(results[2], WIDE)
    final = exchange(results[2], NARROW_AXES)

    place = jnp.stack(
        [2 * lax.axis_index("xl") + lax.axis_index("c"), lax.axis_index("xh")]
    ).astype(jnp.int32)
    partial = layer(
        place, early, grads, final, counts, owner_row,
        query_weight, key_weight, value_weight, out_weight, out_t, up_weight, up_t, down_weight,
    )
    gathered = exchange(partial, QUADS)
    return (hops, *sum_parts(gathered))


def solution(mesh):
    split = Mesh(mesh.devices.reshape(4, 4, 2, 2, 2), ("z", "y", "xh", "xl", "c"))
    rows = P(WIDE + NARROW_AXES, None)
    in_specs = (
        P(NARROW_AXES, WIDE),
        P(WIDE, None, None, None),
        P(WIDE, None),
        P(WIDE, None, None),
        P(WIDE),
        P(WIDE, None),
        P(None, NARROW_AXES, WIDE),
        P(), P(), P(), P(), P(), P(),
    )
    out_specs = (P(None, NARROW_AXES, WIDE), rows, rows, rows)
    return jax.shard_map(
        on_device, mesh=split, in_specs=in_specs, out_specs=out_specs, check_vma=False
    )
```

```python
import functools
import math

import jax
import jax.numpy as jnp
from jax import lax
from jax.experimental import pallas as pl
from jax.experimental.pallas import tpu as pltpu
from jax.sharding import Mesh, PartitionSpec as P

D = 512
FF = 2048
HEADS = 8
HEAD_DIM = 64
HOPS = 3
TOKS = 4
BLK = 128
K = 12
SEND = 2
NB = 32
PARTS = 16
FEATS = 64
NODES = NB * BLK
TRAIN = 512
OWNERS = 128
QUAD = 4
QUAD_NODES = 256
NARROW = 8
DESTS = 32
GROUP = 16
UNROLL = 16
CHUNK = 4
IN_FLIGHT = 3
PICK_BLOCKS = 4
FF_CHUNK = 512
EPSILON = 1e-05

BF = jnp.bfloat16
F32 = jnp.float32
WIDE = ("z", "y")
NARROW_AXES = ("xh", "xl", "c")
QUADS = ("z", "y", "xh")


def params(limit_mib):
    return pltpu.CompilerParams(vmem_limit_bytes=limit_mib * 1024 * 1024)


def dot(left, right):
    return jnp.dot(left, right, preferred_element_type=F32)


def dot_rows(left, right):
    return lax.dot_general(left, right, (((1,), (1,)), ((), ())), preferred_element_type=F32)


def block_columns(b):
    return pl.ds(b * BLK if isinstance(b, int) else pl.multiple_of(b * BLK, BLK), BLK)


def pack_kernel(sends, field, owners_h, outgoing, counts, owners, sems):
    names = pltpu.make_async_copy(owners_h, owners, sems.at[PARTS * SEND])
    names.start()
    copies = []
    for slot in range(PARTS * SEND):
        start = pl.multiple_of(sends[0, slot % SEND, slot // SEND] * BLK, BLK)
        rows = (slot % SEND) * FEATS
        copies.append(
            pltpu.make_async_copy(
                field.at[:, pl.ds(start, BLK)],
                outgoing.at[slot // SEND, rows : rows + FEATS, :],
                sems.at[slot],
            )
        )
    for copy in copies:
        copy.start()
    names.wait()
    named = lax.broadcasted_iota(jnp.int32, (OWNERS, TRAIN), 0) == owners[...]
    count = jnp.sum(jnp.where(named, 1.0, 0.0), axis=1, keepdims=True)
    counts[...] = jnp.broadcast_to(count, (OWNERS, OWNERS))
    for copy in copies:
        copy.wait()


def pack(sends, field, owners):
    return pl.pallas_call(
        pack_kernel,
        out_shape=[
            jax.ShapeDtypeStruct((PARTS, SEND * FEATS, BLK), BF),
            jax.ShapeDtypeStruct((OWNERS, OWNERS), F32),
        ],
        in_specs=[
            pl.BlockSpec(memory_space=pltpu.SMEM),
            pl.BlockSpec(memory_space=pltpu.HBM),
            pl.BlockSpec(memory_space=pltpu.HBM),
        ],
        scratch_shapes=[
            pltpu.VMEM((1, TRAIN), jnp.int32),
            pltpu.SemaphoreType.DMA((PARTS * SEND + 1,)),
        ],
        compiler_params=params(4),
        name="pack",
    )(in_hbm(sends), in_hbm(field), in_hbm(owners))


def picked_columns(ids, fields):
    id_row = ids[...]
    span = PICK_BLOCKS * BLK
    total = None
    for start in range(0, NODES, span):
        rows = lax.broadcasted_iota(jnp.int32, (span, TRAIN), 0) + start
        chosen = jnp.where(rows == id_row, 1.0, 0.0).astype(BF)
        block = jnp.concatenate([field[:, start : start + span] for field in fields], axis=0)
        term = dot(block, chosen)
        total = term if total is None else total + term
    return total.astype(BF)


def apply_kernel(*refs, second, first, last, picking, stage):
    refs = list(refs)
    lists, sends, tiles, field, incoming = refs[:5]
    refs = refs[5:]
    up_h, out_h = (refs.pop(0), refs.pop(0)) if first else (None, None)
    degree = None if first else refs.pop(0)
    previous = refs.pop(0) if second else None
    aliased = second and refs.pop(0)
    ids = refs.pop(0) if picking else None
    others = [refs.pop(0) for _ in range(picking - 1)] if picking else []
    result = refs.pop(0)
    hops = refs.pop(0) if second else None
    outgoing = None if last else refs.pop(0)
    rows_out = refs.pop(0) if picking else None
    degree_out = refs.pop(0) if first else None
    tiles_h, tiles = (tiles, refs.pop(0)) if stage else (None, tiles)
    up_t, out_t = (refs.pop(0), refs.pop(0)) if first else (None, None)
    pool, fresh, sems = refs[:3]
    if first:
        up_w, out_w = refs[3:]
        weights = [
            pltpu.make_async_copy(up_h, up_w, sems.at[NB // CHUNK]),
            pltpu.make_async_copy(out_h, out_w, sems.at[NB // CHUNK + 1]),
        ]
        for weight in weights:
            weight.start()

    def load(i):
        blocks = pl.ds(i * CHUNK, CHUNK)
        return pltpu.make_async_copy(tiles_h.at[blocks], tiles.at[blocks], sems.at[i])

    def store(i):
        cols = pl.ds(pl.multiple_of(i * UNROLL * BLK, UNROLL * BLK), UNROLL * BLK)
        return pltpu.make_async_copy(
            result.at[:, cols], hops.at[second - 1, :, cols], sems.at[i]
        )

    if stage:
        for i in range(IN_FLIGHT):
            load(i).start()

    if first:
        for weight in weights:
            weight.wait()
        for i in range(0, FF, D):
            up_t[:, i : i + D] = jnp.transpose(up_w[i : i + D, :])
        out_t[...] = jnp.transpose(out_w[...])
    for j in range(NB):
        pool[j] = field[:, j * BLK : (j + 1) * BLK]
    for j in range(PARTS * SEND):
        rows = (j % SEND) * FEATS
        pool[NB + j] = incoming[j // SEND, rows : rows + FEATS, :]

    def one_block(b):
        picked = jnp.concatenate([pool[lists[k, b]] for k in range(K)], axis=1)
        if first:
            picked = jnp.concatenate([picked, jnp.ones((GROUP, K * BLK), BF)], axis=0)
        summed = dot(picked, tiles[b].reshape(K * BLK, BLK))
        if first:
            share = summed[FEATS : FEATS + 1, :]
            degree_out[pl.ds(b, 1), :] = share
            summed = summed[:FEATS, :]
        else:
            share = degree[pl.ds(b, 1), :]
        value = (summed / share).astype(BF)
        cols = block_columns(b)
        if second:
            value = (
                0.5 * previous[:, cols].astype(F32) + pool[b].astype(F32) + value.astype(F32)
            ).astype(BF)
        result[:, cols] = value
        fresh[b] = value

    def some_blocks(i, carry):
        for j in range(UNROLL):
            one_block(i * UNROLL + j)
        if second:
            store(i).start()
        return carry

    if stage:
        for i in range(NB // CHUNK):
            load(i).wait()
            if i + IN_FLIGHT < NB // CHUNK:
                load(i + IN_FLIGHT).start()
            for j in range(CHUNK):
                one_block(i * CHUNK + j)
    else:
        lax.fori_loop(0, NB // UNROLL, some_blocks, 0)
    if not last:
        for slot in range(PARTS * SEND):
            rows = (slot % SEND) * FEATS
            outgoing[slot // SEND, rows : rows + FEATS, :] = fresh[
                sends[0, slot % SEND, slot // SEND]
            ]
    if picking:
        picked = picked_columns(ids, [*others, result])
        if last:
            for n in range(NARROW):
                half = n // QUAD
                rows_out[n] = picked[:, half * QUAD_NODES : (half + 1) * QUAD_NODES]
        else:
            rows_out[...] = picked
    if second:
        for i in range(NB // UNROLL):
            store(i).wait()


def apply(
    lists, sends, tiles, field, incoming, degree=None, previous=None, hops=None, hop=0, ids=None, others=(), stage=False,
    weights=(),
):
    second = previous is not None
    last = second and hop == HOPS - 1
    first = hop == 0 and not second
    smem = pl.BlockSpec(memory_space=pltpu.SMEM)
    vmem = pl.BlockSpec(memory_space=pltpu.VMEM)
    hbm = pl.BlockSpec(memory_space=pltpu.HBM)
    operands = [in_hbm(lists), in_hbm(sends), in_hbm(tiles) if stage else in_vmem(tiles), field, incoming]
    in_specs = [smem, smem, hbm if stage else vmem, vmem, vmem]
    if first:
        operands += [in_hbm(w) for w in weights]
        in_specs += [hbm, hbm]
    else:
        operands.append(degree)
        in_specs.append(vmem)
    out_shape = [jax.ShapeDtypeStruct((FEATS, NODES), BF)]
    out_specs = [vmem]
    aliases = {}
    if second:
        operands.append(previous)
        in_specs.append(vmem)
        if hops is None:
            operands.append(sends)
            in_specs.append(smem)
        else:
            aliases = {len(operands): 1}
            operands.append(hops)
            in_specs.append(hbm)
        out_shape.append(jax.ShapeDtypeStruct((HOPS, FEATS, NODES), BF))
        out_specs.append(hbm)
    if ids is not None:
        operands += [ids, *others]
        in_specs += [vmem] * (1 + len(others))
    if not last:
        out_shape.append(jax.ShapeDtypeStruct((PARTS, SEND * FEATS, BLK), BF))
        out_specs.append(vmem)
    if ids is not None:
        rows = FEATS * (1 + len(others))
        shape = (NARROW, rows, QUAD_NODES) if last else (rows, TRAIN)
        out_shape.append(jax.ShapeDtypeStruct(shape, BF))
        out_specs.append(vmem)
    if first:
        out_shape.append(jax.ShapeDtypeStruct((NB, BLK), F32))
        out_specs.append(vmem)
    if stage:
        out_shape.append(pltpu.VMEM(tiles.shape, BF))
        out_specs.append(vmem)
    if first:
        out_shape += [jax.ShapeDtypeStruct(w.shape[::-1], BF) for w in weights]
        out_specs += [vmem, vmem]
    scratch = [
        pltpu.VMEM((2 * NB, FEATS, BLK), BF),
        pltpu.VMEM((NB, FEATS, BLK), BF),
        pltpu.SemaphoreType.DMA((NB // CHUNK + 2,)),
        *[pltpu.VMEM(w.shape, BF) for w in weights],
    ]
    return pl.pallas_call(
        functools.partial(
            apply_kernel, second=second and hop + 1, first=first, last=last,
            picking=0 if ids is None else 1 + len(others), stage=stage,
        ),
        out_shape=out_shape,
        in_specs=in_specs,
        out_specs=out_specs,
        scratch_shapes=scratch,
        input_output_aliases=aliases,
        compiler_params=params(12 if first else 8),
        name=f"apply_{'second' if second else 'first'}_{hop}",
    )(*operands)


def normalize(hidden):
    center = hidden - jnp.mean(hidden, axis=0, keepdims=True)
    inverse = lax.rsqrt(jnp.mean(center * center, axis=0, keepdims=True) + EPSILON)
    return center * inverse, inverse


def copies_of(pairs, sems):
    return [
        pltpu.make_async_copy(source, target, sems.at[index])
        for index, (source, target) in enumerate(pairs)
    ]


def early_kernel(
    place, early_h, grads_h, counts_h, owners_h, query_h, key_h, value_h,
    tokens_h, normed_h, query_oh, key_oh, value_oh, scaled_h,
    early, grads, counts, owners, query_w, key_w, value_w,
    tokens_s, normed_s, query_s, key_s, value_s, scaled_s, sems,
):
    mine = pl.ds(pl.multiple_of(place[1] * QUAD_NODES, QUAD_NODES), QUAD_NODES)
    loads = copies_of(
        (
            (early_h.at[:, :, mine], early), (query_h, query_w), (key_h, key_w),
            (value_h, value_w), (counts_h, counts), (owners_h, owners),
            (grads_h.at[:, :, mine], grads),
        ),
        sems,
    )
    stores = copies_of(
        (
            (tokens_s, tokens_h), (normed_s, normed_h), (query_s, query_oh),
            (key_s, key_oh), (value_s, value_oh), (scaled_s, scaled_h),
        ),
        sems.at[pl.ds(len(loads), 6)],
    )
    for load in loads:
        load.start()
    loads[0].wait()
    for t in range(HOPS):
        cols = slice(t * QUAD_NODES, (t + 1) * QUAD_NODES)
        tokens = early[:, t * FEATS : (t + 1) * FEATS, :].reshape(D, QUAD_NODES)
        tokens_s[:, cols] = tokens
        normed_s[:, cols] = normalize(tokens.astype(F32))[0].astype(BF)
    stores[0].start()
    stores[1].start()
    for index, (weight, target) in enumerate(
        ((query_w, query_s), (key_w, key_s), (value_w, value_s))
    ):
        loads[1 + index].wait()
        target[...] = dot(weight[...], normed_s[...]).astype(BF)
        stores[2 + index].start()
    for load in loads[4:]:
        load.wait()
    named = lax.broadcasted_iota(jnp.int32, (OWNERS, QUAD_NODES), 0) == owners[:, mine]
    by_owner = jnp.concatenate([1.0 / counts[...]] * (QUAD_NODES // OWNERS), axis=1)
    row_scale = jnp.sum(jnp.where(named, by_owner, 0.0), axis=0, keepdims=True)
    for t in range(TOKS):
        rows = grads[:, t * FEATS : (t + 1) * FEATS, :].reshape(D, QUAD_NODES)
        scaled_s[:, t * QUAD_NODES : (t + 1) * QUAD_NODES] = (
            rows.astype(F32) * row_scale
        ).astype(BF)
    stores[5].start()
    for store in stores:
        store.wait()


def early_part(place, early, grads, counts, owners, *weights):
    hbm = pl.BlockSpec(memory_space=pltpu.HBM)
    smem = pl.BlockSpec(memory_space=pltpu.SMEM)
    shapes = [(D, HOPS * QUAD_NODES)] * 5 + [(D, TOKS * QUAD_NODES)]
    return pl.pallas_call(
        early_kernel,
        out_shape=[pltpu.HBM(shape, BF) for shape in shapes],
        in_specs=[smem] + [hbm] * 7,
        out_specs=[hbm] * 6,
        scratch_shapes=[
            pltpu.VMEM((NARROW, HOPS * FEATS, QUAD_NODES), BF),
            pltpu.VMEM((NARROW, TOKS * FEATS, QUAD_NODES), BF),
            pltpu.VMEM((OWNERS, OWNERS), F32),
            pltpu.VMEM((1, TRAIN), jnp.int32),
            *[pltpu.VMEM(w.shape, BF) for w in weights],
            *[pltpu.VMEM(shape, BF) for shape in shapes],
            pltpu.SemaphoreType.DMA((13,)),
        ],
        compiler_params=params(24),
        name="early",
    )(place, *[in_hbm(array) for array in (early, grads, counts, owners, *weights)])


def layer_kernel(
    final, tokens_h, normed_h, query_ih, key_ih, value_ih, scaled_h, place,
    query_h, key_h, value_h, out_h, out_th, up_h, up_th, down_h,
    result, query_s, key_s, value_s, mixed_s, probs_s, act_s, pre_s, gmix_s, gq_s, gk_s, gv_s, gr_s,
    query_w, key_w, value_w, out_w, out_t, up_w, up_t, down_w, tokens_s, normed_s, scaled_s, sems,
):
    own = place[0]
    width = TOKS * QUAD_NODES
    known = slice(0, HOPS * QUAD_NODES)
    added = slice(HOPS * QUAD_NODES, width)
    loads = copies_of(
        (
            (query_h, query_w), (key_h, key_w), (value_h, value_w),
            (query_ih, query_s.at[:, known]), (key_ih, key_s.at[:, known]),
            (value_ih, value_s.at[:, known]), (out_h, out_w), (tokens_h, tokens_s.at[:, known]),
            (up_h, up_w), (down_h, down_w), (scaled_h, scaled_s), (up_th, up_t),
            (out_th, out_t), (normed_h, normed_s.at[:, known]),
        ),
        sems,
    )
    for load in loads:
        load.start()
    last = final[...].reshape(D, QUAD_NODES)
    tokens_s[:, added] = last
    last = normalize(last.astype(F32))[0].astype(BF)
    normed_s[:, added] = last
    for index, (weight, target) in enumerate(
        ((query_w, query_s), (key_w, key_s), (value_w, value_s))
    ):
        loads[index].wait()
        target[:, added] = dot(weight[...], last).astype(BF)
    for load in loads[3:6]:
        load.wait()
    score_scale = 1.0 / math.sqrt(HEAD_DIM)

    def columns(half):
        return [
            pl.ds(pl.multiple_of(t * QUAD_NODES + half * BLK, BLK), BLK) for t in range(TOKS)
        ]

    def parts(ref, rows, cols):
        return [ref[rows, c].astype(F32) for c in cols]

    def forward_head(step, carry):
        h = step // 2
        cols = columns(step % 2)
        rows = pl.ds(pl.multiple_of(h * HEAD_DIM, HEAD_DIM), HEAD_DIM)
        query, key, value = [parts(ref, rows, cols) for ref in (query_s, key_s, value_s)]
        all_probs = []
        for t in range(TOKS):
            scores = [
                jnp.sum(query[t] * key[u], axis=0, keepdims=True) * score_scale
                for u in range(TOKS)
            ]
            top = jnp.maximum(
                jnp.maximum(scores[0], scores[1]), jnp.maximum(scores[2], scores[3])
            )
            raised = [jnp.exp(s - top) for s in scores]
            total = raised[0] + raised[1] + raised[2] + raised[3]
            probs = [r / total for r in raised]
            all_probs += probs
            low = [p.astype(BF).astype(F32) for p in probs]
            mixed_s[rows, cols[t]] = (
                low[0] * value[0] + low[1] * value[1] + low[2] * value[2] + low[3] * value[3]
            ).astype(BF)
        probs_s[step] = jnp.concatenate(all_probs, axis=0)
        return carry

    lax.fori_loop(0, 2 * HEADS, forward_head, 0)
    loads[6].wait()
    loads[7].wait()
    residual = (tokens_s[...].astype(F32) + dot(out_w[...], mixed_s[...])).astype(BF)
    second_norm, second_inv = normalize(residual.astype(F32))
    normed_b = second_norm.astype(BF)

    root = math.sqrt(2.0 / math.pi)
    groups = FF_CHUNK // (QUAD * GROUP)

    def ffn_chunk(i, carry):
        rows = pl.ds(pl.multiple_of(i * FF_CHUNK, FF_CHUNK), FF_CHUNK)
        pre = dot(up_w[rows, :], normed_b)
        grad_act = dot(down_w[rows, :], scaled_s[...])
        square = pre * pre
        gate = 0.5 + 0.5 * jnp.tanh(pre * (root + (root * 0.044715) * square))
        activated = pre * gate
        slope = gate + activated * (1.0 - gate) * (
            2.0 * root + (6.0 * root * 0.044715) * square
        )
        at = pl.ds(i * groups, groups)
        act_s[at] = activated.astype(BF).reshape(groups, QUAD, GROUP, width)
        pre_s[at] = (grad_act * slope).astype(BF).reshape(groups, QUAD, GROUP, width)
        return carry

    for load in loads[8:11]:
        load.wait()
    lax.fori_loop(0, FF // FF_CHUNK, ffn_chunk, 0)

    share = FF // QUAD
    grad_down = dot_rows(act_s[:, own].reshape(share, width), scaled_s[...])
    result[:, 2 * GROUP : 3 * GROUP, :] = grad_down.astype(BF).reshape(DESTS, GROUP, D)
    grad_up = dot_rows(pre_s[:, own].reshape(share, width), normed_b)
    result[:, GROUP : 2 * GROUP, :] = grad_up.astype(BF).reshape(DESTS, GROUP, D)

    loads[11].wait()
    grad_normed = dot(up_t[...], pre_s[...].reshape(FF, width))
    grad_resid = (
        scaled_s[...].astype(F32)
        + second_inv
        * (
            grad_normed
            - jnp.mean(grad_normed, axis=0, keepdims=True)
            - second_norm * jnp.mean(grad_normed * second_norm, axis=0, keepdims=True)
        )
    ).astype(BF)
    gr_s[...] = grad_resid.reshape(HEADS, QUAD, GROUP, width)
    loads[12].wait()
    gmix_s[...] = dot(out_t[...], grad_resid).astype(BF)

    def backward_head(step, carry):
        h = step // 2
        cols = columns(step % 2)
        rows = pl.ds(pl.multiple_of(h * HEAD_DIM, HEAD_DIM), HEAD_DIM)
        query, key, value, grad_mixed = [
            parts(ref, rows, cols) for ref in (query_s, key_s, value_s, gmix_s)
        ]
        saved = probs_s[step]
        prob = lambda t, u: saved[t * TOKS + u : t * TOKS + u + 1, :]
        weights = []
        grad_query = []
        for t in range(TOKS):
            grad_probs = [
                jnp.sum(grad_mixed[t] * value[u], axis=0, keepdims=True) for u in range(TOKS)
            ]
            inner = sum(prob(t, u) * grad_probs[u] for u in range(TOKS))
            weight = [
                (prob(t, u) * (grad_probs[u] - inner) * score_scale).astype(BF).astype(F32)
                for u in range(TOKS)
            ]
            weights.append(weight)
            grad_query.append(sum(weight[u] * key[u] for u in range(TOKS)))
        grad_key = [sum(weights[t][u] * query[t] for t in range(TOKS)) for u in range(TOKS)]
        grad_value = [
            sum(prob(t, u).astype(BF).astype(F32) * grad_mixed[t] for t in range(TOKS))
            for u in range(TOKS)
        ]
        for ref, pieces in ((gq_s, grad_query), (gk_s, grad_key), (gv_s, grad_value)):
            for t in range(TOKS):
                ref[h, :, :, cols[t]] = pieces[t].astype(BF).reshape(QUAD, GROUP, BLK)
        return carry

    lax.fori_loop(0, 2 * HEADS, backward_head, 0)
    share = D // QUAD
    stacked = jnp.concatenate(
        [ref[:, own].reshape(share, width) for ref in (gq_s, gk_s, gv_s)], axis=0
    )
    count = HEADS * 3
    loads[13].wait()
    result[:count, 0:GROUP, :] = dot_rows(stacked, normed_s[...]).astype(BF).reshape(count, GROUP, D)
    sum_out = dot_rows(gr_s[:, own].reshape(share, width), mixed_s[...])
    result[count:, 0:GROUP, :] = sum_out.astype(BF).reshape(HEADS, GROUP, D)


def in_vmem(array):
    return pltpu.with_memory_space_constraint(array, pltpu.VMEM)


def in_hbm(array):
    return pltpu.with_memory_space_constraint(array, pltpu.HBM)


def layer(final, known, place, *weights):
    width = TOKS * QUAD_NODES
    square = pltpu.VMEM((D, width), BF)
    grouped = pltpu.VMEM((HEADS, QUAD, GROUP, width), BF)
    wide = pltpu.VMEM((DESTS, QUAD, GROUP, width), BF)
    vmem = pl.BlockSpec(memory_space=pltpu.VMEM)
    hbm = pl.BlockSpec(memory_space=pltpu.HBM)
    smem = pl.BlockSpec(memory_space=pltpu.SMEM)
    return pl.pallas_call(
        layer_kernel,
        out_shape=jax.ShapeDtypeStruct((DESTS, 3 * GROUP, D), BF),
        in_specs=[vmem] + [hbm] * 6 + [smem] + [hbm] * 8,
        out_specs=vmem,
        scratch_shapes=[
            square, square, square, square,
            pltpu.VMEM((2 * HEADS, TOKS * TOKS, BLK), F32),
            wide, wide, square, grouped, grouped, grouped, grouped,
            *[pltpu.VMEM(w.shape, BF) for w in weights],
            square, square, square,
            pltpu.SemaphoreType.DMA((14,)),
        ],
        compiler_params=params(48),
        name="layer",
    )(final, *[in_hbm(k) for k in known], place, *[in_hbm(w) for w in weights])


def sum_kernel(gathered, *outs):
    total = jnp.sum(gathered[...].astype(F32), axis=0)
    for index, out in enumerate(outs):
        out[...] = total[index * GROUP : (index + 1) * GROUP]


def sum_parts(gathered):
    return pl.pallas_call(
        sum_kernel,
        out_shape=[jax.ShapeDtypeStruct((GROUP, D), F32)] * 3,
        compiler_params=params(8),
        name="sum_parts",
    )(gathered)


def exchange(array, axes):
    return lax.all_to_all(array, axes, split_axis=0, concat_axis=0, tiled=True)


def on_device(
    features, edge_tiles, block_lists, send_lists, train_ids, owners, cotangent,
    query_weight, key_weight, value_weight, out_weight, up_weight, down_weight,
):
    ids = train_ids.reshape(1, TRAIN)
    grads = lax.all_gather(cotangent.reshape(TOKS * FEATS, TRAIN), NARROW_AXES)
    owner_row = owners.reshape(1, TRAIN)
    send_slots = jnp.transpose(send_lists, (0, 2, 1))
    outgoing, counts = pack(send_slots, features, owner_row)
    counts = lax.psum(counts, WIDE)
    incoming = exchange(outgoing, WIDE)
    step = functools.partial(apply, jnp.transpose(block_lists), send_slots)
    current = features
    hops = None
    fields = [features]
    for hop in range(HOPS):
        if hop == 0:
            once, outgoing, degree, tiles, up_t, out_t = step(
                edge_tiles, current, incoming, stage=True, weights=(up_weight, out_weight)
            )
        elif hop == HOPS - 1:
            once, outgoing, tiles = step(
                edge_tiles, current, incoming, degree, hop=hop, stage=True
            )
        else:
            once, outgoing = step(tiles, current, incoming, degree, hop=hop)
        incoming = exchange(outgoing, WIDE)
        results = step(
            tiles, once, incoming, degree, previous=current, hops=hops, hop=hop,
            ids=None if hop == 0 else ids,
            others=tuple(fields) if hop == HOPS - 2 else (),
        )
        current, hops = results[0], results[1]
        fields.append(current)
        if hop == HOPS - 2:
            early = lax.all_gather(results[3], NARROW_AXES)
        if hop < HOPS - 1:
            incoming = exchange(results[2], WIDE)
    final = exchange(results[2], NARROW_AXES)
    place = jnp.stack(
        [2 * lax.axis_index("xl") + lax.axis_index("c"), lax.axis_index("xh")]
    ).astype(jnp.int32)
    known = early_part(
        place, early, grads, counts, owner_row, query_weight, key_weight, value_weight
    )
    partial = layer(
        final, known, place,
        query_weight, key_weight, value_weight, out_weight, out_t, up_weight, up_t, down_weight,
    )
    gathered = exchange(partial, QUADS)
    return (hops, *sum_parts(gathered))


def solution(mesh):
    split = Mesh(mesh.devices.reshape(4, 4, 2, 2, 2), ("z", "y", "xh", "xl", "c"))
    rows = P(WIDE + NARROW_AXES, None)
    in_specs = (
        P(NARROW_AXES, WIDE),
        P(WIDE, None, None, None),
        P(WIDE, None),
        P(WIDE, None, None),
        P(WIDE),
        P(WIDE, None),
        P(None, NARROW_AXES, WIDE),
        P(), P(), P(), P(), P(), P(),
    )
    out_specs = (P(None, NARROW_AXES, WIDE), rows, rows, rows)
    return jax.shard_map(
        on_device, mesh=split, in_specs=in_specs, out_specs=out_specs, check_vma=False
    )
```

```python
import functools
import math

import jax
import jax.numpy as jnp
from jax import lax
from jax.experimental import pallas as pl
from jax.experimental.pallas import tpu as pltpu
from jax.sharding import Mesh, PartitionSpec as P

D = 512
FF = 2048
HEADS = 8
HEAD_DIM = 64
HOPS = 3
TOKS = 4
BLK = 128
K = 12
SEND = 2
NB = 32
PARTS = 16
FEATS = 64
NODES = NB * BLK
TRAIN = 512
OWNERS = 128
QUAD = 4
QUAD_NODES = 256
NARROW = 8
DESTS = 32
GROUP = 16
UNROLL = 16
CHUNK = 4
IN_FLIGHT = 3
PICK_BLOCKS = 4
FF_CHUNK = 512
EPSILON = 1e-05

BF = jnp.bfloat16
F32 = jnp.float32
WIDE = ("z", "y")
NARROW_AXES = ("xh", "xl", "c")
QUADS = ("z", "y", "xh")


def params(limit_mib):
    return pltpu.CompilerParams(vmem_limit_bytes=limit_mib * 1024 * 1024)


def dot(left, right):
    return jnp.dot(left, right, preferred_element_type=F32)


def dot_rows(left, right):
    return lax.dot_general(left, right, (((1,), (1,)), ((), ())), preferred_element_type=F32)


def block_columns(b):
    return pl.ds(b * BLK if isinstance(b, int) else pl.multiple_of(b * BLK, BLK), BLK)


def pack_kernel(sends, field, owners_h, outgoing, counts, owners, sems):
    names = pltpu.make_async_copy(owners_h, owners, sems.at[PARTS * SEND])
    names.start()
    copies = []
    for slot in range(PARTS * SEND):
        start = pl.multiple_of(sends[0, slot % SEND, slot // SEND] * BLK, BLK)
        rows = (slot % SEND) * FEATS
        copies.append(
            pltpu.make_async_copy(
                field.at[:, pl.ds(start, BLK)],
                outgoing.at[slot // SEND, rows : rows + FEATS, :],
                sems.at[slot],
            )
        )
    for copy in copies:
        copy.start()
    names.wait()
    named = lax.broadcasted_iota(jnp.int32, (OWNERS, TRAIN), 0) == owners[...]
    count = jnp.sum(jnp.where(named, 1.0, 0.0), axis=1, keepdims=True)
    counts[...] = jnp.broadcast_to(count, (OWNERS, OWNERS))
    for copy in copies:
        copy.wait()


def pack(sends, field, owners):
    return pl.pallas_call(
        pack_kernel,
        out_shape=[
            jax.ShapeDtypeStruct((PARTS, SEND * FEATS, BLK), BF),
            jax.ShapeDtypeStruct((OWNERS, OWNERS), F32),
        ],
        in_specs=[
            pl.BlockSpec(memory_space=pltpu.SMEM),
            pl.BlockSpec(memory_space=pltpu.HBM),
            pl.BlockSpec(memory_space=pltpu.HBM),
        ],
        scratch_shapes=[
            pltpu.VMEM((1, TRAIN), jnp.int32),
            pltpu.SemaphoreType.DMA((PARTS * SEND + 1,)),
        ],
        compiler_params=params(4),
        name="pack",
    )(in_hbm(sends), in_hbm(field), in_hbm(owners))


def picked_columns(ids, fields):
    id_row = ids[...]
    span = PICK_BLOCKS * BLK
    total = None
    for start in range(0, NODES, span):
        rows = lax.broadcasted_iota(jnp.int32, (span, TRAIN), 0) + start
        chosen = jnp.where(rows == id_row, 1.0, 0.0).astype(BF)
        block = jnp.concatenate([field[:, start : start + span] for field in fields], axis=0)
        term = dot(block, chosen)
        total = term if total is None else total + term
    return total.astype(BF)


def apply_kernel(*refs, second, first, last, picking, stage):
    refs = list(refs)
    lists, sends, tiles, field, incoming = refs[:5]
    refs = refs[5:]
    up_h, out_h = (refs.pop(0), refs.pop(0)) if first else (None, None)
    degree = None if first else refs.pop(0)
    previous = refs.pop(0) if second else None
    aliased = second and refs.pop(0)
    ids = refs.pop(0) if picking else None
    others = [refs.pop(0) for _ in range(picking - 1)] if picking else []
    result = refs.pop(0)
    hops = refs.pop(0) if second else None
    outgoing = None if last else refs.pop(0)
    rows_out = refs.pop(0) if picking else None
    degree_out = refs.pop(0) if first else None
    tiles_h, tiles = (tiles, refs.pop(0)) if stage else (None, tiles)
    up_t, out_t = (refs.pop(0), refs.pop(0)) if first else (None, None)
    pool, fresh, sems = refs[:3]
    if first:
        up_w, out_w = refs[3:]
        weights = [
            pltpu.make_async_copy(up_h, up_w, sems.at[NB // CHUNK]),
            pltpu.make_async_copy(out_h, out_w, sems.at[NB // CHUNK + 1]),
        ]
        for weight in weights:
            weight.start()

    def load(i):
        blocks = pl.ds(i * CHUNK, CHUNK)
        return pltpu.make_async_copy(tiles_h.at[blocks], tiles.at[blocks], sems.at[i])

    def store(i):
        cols = pl.ds(pl.multiple_of(i * UNROLL * BLK, UNROLL * BLK), UNROLL * BLK)
        return pltpu.make_async_copy(
            result.at[:, cols], hops.at[second - 1, :, cols], sems.at[i]
        )

    if stage:
        for i in range(IN_FLIGHT):
            load(i).start()

    if first:
        for weight in weights:
            weight.wait()
        for i in range(0, FF, D):
            up_t[:, i : i + D] = jnp.transpose(up_w[i : i + D, :])
        out_t[...] = jnp.transpose(out_w[...])
    for j in range(NB):
        pool[j] = field[:, j * BLK : (j + 1) * BLK]
    for j in range(PARTS * SEND):
        rows = (j % SEND) * FEATS
        pool[NB + j] = incoming[j // SEND, rows : rows + FEATS, :]

    def one_block(b):
        picked = jnp.concatenate([pool[lists[k, b]] for k in range(K)], axis=1)
        if first:
            picked = jnp.concatenate([picked, jnp.ones((GROUP, K * BLK), BF)], axis=0)
        summed = dot(picked, tiles[b].reshape(K * BLK, BLK))
        if first:
            share = summed[FEATS : FEATS + 1, :]
            degree_out[pl.ds(b, 1), :] = share
            summed = summed[:FEATS, :]
        else:
            share = degree[pl.ds(b, 1), :]
        value = (summed / share).astype(BF)
        cols = block_columns(b)
        if second:
            value = (
                0.5 * previous[:, cols].astype(F32) + pool[b].astype(F32) + value.astype(F32)
            ).astype(BF)
        result[:, cols] = value
        fresh[b] = value

    def some_blocks(i, carry):
        for j in range(UNROLL):
            one_block(i * UNROLL + j)
        if second:
            store(i).start()
        return carry

    if stage:
        for i in range(NB // CHUNK):
            load(i).wait()
            if i + IN_FLIGHT < NB // CHUNK:
                load(i + IN_FLIGHT).start()
            for j in range(CHUNK):
                one_block(i * CHUNK + j)
    else:
        lax.fori_loop(0, NB // UNROLL, some_blocks, 0)
    if not last:
        for slot in range(PARTS * SEND):
            rows = (slot % SEND) * FEATS
            outgoing[slot // SEND, rows : rows + FEATS, :] = fresh[
                sends[0, slot % SEND, slot // SEND]
            ]
    if picking:
        picked = picked_columns(ids, [*others, result])
        if last:
            for n in range(NARROW):
                half = n // QUAD
                rows_out[n] = picked[:, half * QUAD_NODES : (half + 1) * QUAD_NODES]
        else:
            rows_out[...] = picked
    if second:
        for i in range(NB // UNROLL):
            store(i).wait()


def apply(
    lists, sends, tiles, field, incoming, degree=None, previous=None, hops=None, hop=0, ids=None, others=(), stage=False,
    weights=(),
):
    second = previous is not None
    last = second and hop == HOPS - 1
    first = hop == 0 and not second
    smem = pl.BlockSpec(memory_space=pltpu.SMEM)
    vmem = pl.BlockSpec(memory_space=pltpu.VMEM)
    hbm = pl.BlockSpec(memory_space=pltpu.HBM)
    operands = [in_hbm(lists), in_hbm(sends), in_hbm(tiles) if stage else in_vmem(tiles), field, incoming]
    in_specs = [smem, smem, hbm if stage else vmem, vmem, vmem]
    if first:
        operands += [in_hbm(w) for w in weights]
        in_specs += [hbm, hbm]
    else:
        operands.append(degree)
        in_specs.append(vmem)
    out_shape = [jax.ShapeDtypeStruct((FEATS, NODES), BF)]
    out_specs = [vmem]
    aliases = {}
    if second:
        operands.append(previous)
        in_specs.append(vmem)
        if hops is None:
            operands.append(sends)
            in_specs.append(smem)
        else:
            aliases = {len(operands): 1}
            operands.append(hops)
            in_specs.append(hbm)
        out_shape.append(jax.ShapeDtypeStruct((HOPS, FEATS, NODES), BF))
        out_specs.append(hbm)
    if ids is not None:
        operands += [ids, *others]
        in_specs += [vmem] * (1 + len(others))
    if not last:
        out_shape.append(jax.ShapeDtypeStruct((PARTS, SEND * FEATS, BLK), BF))
        out_specs.append(vmem)
    if ids is not None:
        rows = FEATS * (1 + len(others))
        shape = (NARROW, rows, QUAD_NODES) if last else (rows, TRAIN)
        out_shape.append(jax.ShapeDtypeStruct(shape, BF))
        out_specs.append(vmem)
    if first:
        out_shape.append(jax.ShapeDtypeStruct((NB, BLK), F32))
        out_specs.append(vmem)
    if stage:
        out_shape.append(pltpu.VMEM(tiles.shape, BF))
        out_specs.append(vmem)
    if first:
        out_shape += [jax.ShapeDtypeStruct(w.shape[::-1], BF) for w in weights]
        out_specs += [vmem, vmem]
    scratch = [
        pltpu.VMEM((2 * NB, FEATS, BLK), BF),
        pltpu.VMEM((NB, FEATS, BLK), BF),
        pltpu.SemaphoreType.DMA((NB // CHUNK + 2,)),
        *[pltpu.VMEM(w.shape, BF) for w in weights],
    ]
    return pl.pallas_call(
        functools.partial(
            apply_kernel, second=second and hop + 1, first=first, last=last,
            picking=0 if ids is None else 1 + len(others), stage=stage,
        ),
        out_shape=out_shape,
        in_specs=in_specs,
        out_specs=out_specs,
        scratch_shapes=scratch,
        input_output_aliases=aliases,
        compiler_params=params(12 if first else 8),
        name=f"apply_{'second' if second else 'first'}_{hop}",
    )(*operands)


def normalize(hidden):
    center = hidden - jnp.mean(hidden, axis=0, keepdims=True)
    inverse = lax.rsqrt(jnp.mean(center * center, axis=0, keepdims=True) + EPSILON)
    return center * inverse, inverse


def copies_of(pairs, sems):
    return [
        pltpu.make_async_copy(source, target, sems.at[index])
        for index, (source, target) in enumerate(pairs)
    ]


def early_kernel(
    place, early_h, grads_h, counts_h, owners_h, query_h, key_h, value_h,
    tokens_h, normed_h, query_oh, key_oh, value_oh, scaled_h,
    early, grads, counts, owners, query_w, key_w, value_w,
    tokens_s, normed_s, query_s, key_s, value_s, scaled_s, sems,
):
    mine = pl.ds(pl.multiple_of(place[1] * QUAD_NODES, QUAD_NODES), QUAD_NODES)
    loads = copies_of(
        (
            (early_h.at[:, :, mine], early), (query_h, query_w), (key_h, key_w),
            (value_h, value_w), (counts_h, counts), (owners_h, owners),
            (grads_h.at[:, :, mine], grads),
        ),
        sems,
    )
    stores = copies_of(
        (
            (tokens_s, tokens_h), (normed_s, normed_h), (query_s, query_oh),
            (key_s, key_oh), (value_s, value_oh), (scaled_s, scaled_h),
        ),
        sems.at[pl.ds(len(loads), 6)],
    )
    for load in loads:
        load.start()
    loads[0].wait()
    for t in range(HOPS):
        cols = slice(t * QUAD_NODES, (t + 1) * QUAD_NODES)
        tokens = early[:, t * FEATS : (t + 1) * FEATS, :].reshape(D, QUAD_NODES)
        tokens_s[:, cols] = tokens
        normed_s[:, cols] = normalize(tokens.astype(F32))[0].astype(BF)
    stores[0].start()
    stores[1].start()
    for index, (weight, target) in enumerate(
        ((query_w, query_s), (key_w, key_s), (value_w, value_s))
    ):
        loads[1 + index].wait()
        target[...] = dot(weight[...], normed_s[...]).astype(BF)
        stores[2 + index].start()
    for load in loads[4:]:
        load.wait()
    named = lax.broadcasted_iota(jnp.int32, (OWNERS, QUAD_NODES), 0) == owners[:, mine]
    totals = jnp.sum(counts[...], axis=0)
    by_owner = jnp.concatenate([1.0 / totals] * (QUAD_NODES // OWNERS), axis=1)
    row_scale = jnp.sum(jnp.where(named, by_owner, 0.0), axis=0, keepdims=True)
    for t in range(TOKS):
        rows = grads[:, t * FEATS : (t + 1) * FEATS, :].reshape(D, QUAD_NODES)
        scaled_s[:, t * QUAD_NODES : (t + 1) * QUAD_NODES] = (
            rows.astype(F32) * row_scale
        ).astype(BF)
    stores[5].start()
    for store in stores:
        store.wait()


def early_part(place, early, grads, counts, owners, *weights):
    hbm = pl.BlockSpec(memory_space=pltpu.HBM)
    smem = pl.BlockSpec(memory_space=pltpu.SMEM)
    shapes = [(D, HOPS * QUAD_NODES)] * 5 + [(D, TOKS * QUAD_NODES)]
    return pl.pallas_call(
        early_kernel,
        out_shape=[pltpu.HBM(shape, BF) for shape in shapes],
        in_specs=[smem] + [hbm] * 7,
        out_specs=[hbm] * 6,
        scratch_shapes=[
            pltpu.VMEM((NARROW, HOPS * FEATS, QUAD_NODES), BF),
            pltpu.VMEM((NARROW, TOKS * FEATS, QUAD_NODES), BF),
            pltpu.VMEM((PARTS, OWNERS, OWNERS), F32),
            pltpu.VMEM((1, TRAIN), jnp.int32),
            *[pltpu.VMEM(w.shape, BF) for w in weights],
            *[pltpu.VMEM(shape, BF) for shape in shapes],
            pltpu.SemaphoreType.DMA((13,)),
        ],
        compiler_params=params(24),
        name="early",
    )(place, *[in_hbm(array) for array in (early, grads, counts, owners, *weights)])


def layer_kernel(
    final, tokens_h, normed_h, query_ih, key_ih, value_ih, scaled_h, place,
    query_h, key_h, value_h, out_h, out_th, up_h, up_th, down_h,
    result, query_s, key_s, value_s, mixed_s, probs_s, act_s, pre_s, gmix_s, gq_s, gk_s, gv_s, gr_s,
    query_w, key_w, value_w, out_w, out_t, up_w, up_t, down_w, tokens_s, normed_s, scaled_s, sems,
):
    own = place[0]
    width = TOKS * QUAD_NODES
    known = slice(0, HOPS * QUAD_NODES)
    added = slice(HOPS * QUAD_NODES, width)
    loads = copies_of(
        (
            (query_h, query_w), (key_h, key_w), (value_h, value_w),
            (query_ih, query_s.at[:, known]), (key_ih, key_s.at[:, known]),
            (value_ih, value_s.at[:, known]), (out_h, out_w), (tokens_h, tokens_s.at[:, known]),
            (up_h, up_w), (down_h, down_w), (scaled_h, scaled_s), (up_th, up_t),
            (out_th, out_t), (normed_h, normed_s.at[:, known]),
        ),
        sems,
    )
    for load in loads:
        load.start()
    last = final[...].reshape(D, QUAD_NODES)
    tokens_s[:, added] = last
    last = normalize(last.astype(F32))[0].astype(BF)
    normed_s[:, added] = last
    for index, (weight, target) in enumerate(
        ((query_w, query_s), (key_w, key_s), (value_w, value_s))
    ):
        loads[index].wait()
        target[:, added] = dot(weight[...], last).astype(BF)
    for load in loads[3:6]:
        load.wait()
    score_scale = 1.0 / math.sqrt(HEAD_DIM)

    def columns(half):
        return [
            pl.ds(pl.multiple_of(t * QUAD_NODES + half * BLK, BLK), BLK) for t in range(TOKS)
        ]

    def parts(ref, rows, cols):
        return [ref[rows, c].astype(F32) for c in cols]

    def forward_head(step, carry):
        h = step // 2
        cols = columns(step % 2)
        rows = pl.ds(pl.multiple_of(h * HEAD_DIM, HEAD_DIM), HEAD_DIM)
        query, key, value = [parts(ref, rows, cols) for ref in (query_s, key_s, value_s)]
        all_probs = []
        for t in range(TOKS):
            scores = [
                jnp.sum(query[t] * key[u], axis=0, keepdims=True) * score_scale
                for u in range(TOKS)
            ]
            top = jnp.maximum(
                jnp.maximum(scores[0], scores[1]), jnp.maximum(scores[2], scores[3])
            )
            raised = [jnp.exp(s - top) for s in scores]
            total = raised[0] + raised[1] + raised[2] + raised[3]
            probs = [r / total for r in raised]
            all_probs += probs
            low = [p.astype(BF).astype(F32) for p in probs]
            mixed_s[rows, cols[t]] = (
                low[0] * value[0] + low[1] * value[1] + low[2] * value[2] + low[3] * value[3]
            ).astype(BF)
        probs_s[step] = jnp.concatenate(all_probs, axis=0)
        return carry

    lax.fori_loop(0, 2 * HEADS, forward_head, 0)
    loads[6].wait()
    loads[7].wait()
    residual = (tokens_s[...].astype(F32) + dot(out_w[...], mixed_s[...])).astype(BF)
    second_norm, second_inv = normalize(residual.astype(F32))
    normed_b = second_norm.astype(BF)

    root = math.sqrt(2.0 / math.pi)
    groups = FF_CHUNK // (QUAD * GROUP)

    def ffn_chunk(i, carry):
        rows = pl.ds(pl.multiple_of(i * FF_CHUNK, FF_CHUNK), FF_CHUNK)
        pre = dot(up_w[rows, :], normed_b)
        grad_act = dot(down_w[rows, :], scaled_s[...])
        square = pre * pre
        gate = 0.5 + 0.5 * jnp.tanh(pre * (root + (root * 0.044715) * square))
        activated = pre * gate
        slope = gate + activated * (1.0 - gate) * (
            2.0 * root + (6.0 * root * 0.044715) * square
        )
        at = pl.ds(i * groups, groups)
        act_s[at] = activated.astype(BF).reshape(groups, QUAD, GROUP, width)
        pre_s[at] = (grad_act * slope).astype(BF).reshape(groups, QUAD, GROUP, width)
        return carry

    for load in loads[8:11]:
        load.wait()
    lax.fori_loop(0, FF // FF_CHUNK, ffn_chunk, 0)

    share = FF // QUAD
    grad_down = dot_rows(act_s[:, own].reshape(share, width), scaled_s[...])
    result[:, 2 * GROUP : 3 * GROUP, :] = grad_down.astype(BF).reshape(DESTS, GROUP, D)
    grad_up = dot_rows(pre_s[:, own].reshape(share, width), normed_b)
    result[:, GROUP : 2 * GROUP, :] = grad_up.astype(BF).reshape(DESTS, GROUP, D)

    loads[11].wait()
    grad_normed = dot(up_t[...], pre_s[...].reshape(FF, width))
    grad_resid = (
        scaled_s[...].astype(F32)
        + second_inv
        * (
            grad_normed
            - jnp.mean(grad_normed, axis=0, keepdims=True)
            - second_norm * jnp.mean(grad_normed * second_norm, axis=0, keepdims=True)
        )
    ).astype(BF)
    gr_s[...] = grad_resid.reshape(HEADS, QUAD, GROUP, width)
    loads[12].wait()
    gmix_s[...] = dot(out_t[...], grad_resid).astype(BF)

    def backward_head(step, carry):
        h = step // 2
        cols = columns(step % 2)
        rows = pl.ds(pl.multiple_of(h * HEAD_DIM, HEAD_DIM), HEAD_DIM)
        query, key, value, grad_mixed = [
            parts(ref, rows, cols) for ref in (query_s, key_s, value_s, gmix_s)
        ]
        saved = probs_s[step]
        prob = lambda t, u: saved[t * TOKS + u : t * TOKS + u + 1, :]
        weights = []
        grad_query = []
        for t in range(TOKS):
            grad_probs = [
                jnp.sum(grad_mixed[t] * value[u], axis=0, keepdims=True) for u in range(TOKS)
            ]
            inner = sum(prob(t, u) * grad_probs[u] for u in range(TOKS))
            weight = [
                (prob(t, u) * (grad_probs[u] - inner) * score_scale).astype(BF).astype(F32)
                for u in range(TOKS)
            ]
            weights.append(weight)
            grad_query.append(sum(weight[u] * key[u] for u in range(TOKS)))
        grad_key = [sum(weights[t][u] * query[t] for t in range(TOKS)) for u in range(TOKS)]
        grad_value = [
            sum(prob(t, u).astype(BF).astype(F32) * grad_mixed[t] for t in range(TOKS))
            for u in range(TOKS)
        ]
        for ref, pieces in ((gq_s, grad_query), (gk_s, grad_key), (gv_s, grad_value)):
            for t in range(TOKS):
                ref[h, :, :, cols[t]] = pieces[t].astype(BF).reshape(QUAD, GROUP, BLK)
        return carry

    lax.fori_loop(0, 2 * HEADS, backward_head, 0)
    share = D // QUAD
    stacked = jnp.concatenate(
        [ref[:, own].reshape(share, width) for ref in (gq_s, gk_s, gv_s)], axis=0
    )
    count = HEADS * 3
    loads[13].wait()
    result[:count, 0:GROUP, :] = dot_rows(stacked, normed_s[...]).astype(BF).reshape(count, GROUP, D)
    sum_out = dot_rows(gr_s[:, own].reshape(share, width), mixed_s[...])
    result[count:, 0:GROUP, :] = sum_out.astype(BF).reshape(HEADS, GROUP, D)


def in_vmem(array):
    return pltpu.with_memory_space_constraint(array, pltpu.VMEM)


def in_hbm(array):
    return pltpu.with_memory_space_constraint(array, pltpu.HBM)


def layer(final, known, place, *weights):
    width = TOKS * QUAD_NODES
    square = pltpu.VMEM((D, width), BF)
    grouped = pltpu.VMEM((HEADS, QUAD, GROUP, width), BF)
    wide = pltpu.VMEM((DESTS, QUAD, GROUP, width), BF)
    vmem = pl.BlockSpec(memory_space=pltpu.VMEM)
    hbm = pl.BlockSpec(memory_space=pltpu.HBM)
    smem = pl.BlockSpec(memory_space=pltpu.SMEM)
    return pl.pallas_call(
        layer_kernel,
        out_shape=jax.ShapeDtypeStruct((DESTS, 3 * GROUP, D), BF),
        in_specs=[vmem] + [hbm] * 6 + [smem] + [hbm] * 8,
        out_specs=vmem,
        scratch_shapes=[
            square, square, square, square,
            pltpu.VMEM((2 * HEADS, TOKS * TOKS, BLK), F32),
            wide, wide, square, grouped, grouped, grouped, grouped,
            *[pltpu.VMEM(w.shape, BF) for w in weights],
            square, square, square,
            pltpu.SemaphoreType.DMA((14,)),
        ],
        compiler_params=params(48),
        name="layer",
    )(final, *[in_hbm(k) for k in known], place, *[in_hbm(w) for w in weights])


def sum_kernel(gathered, *outs):
    total = jnp.sum(gathered[...].astype(F32), axis=0)
    for index, out in enumerate(outs):
        out[...] = total[index * GROUP : (index + 1) * GROUP]


def sum_parts(gathered):
    return pl.pallas_call(
        sum_kernel,
        out_shape=[jax.ShapeDtypeStruct((GROUP, D), F32)] * 3,
        compiler_params=params(8),
        name="sum_parts",
    )(gathered)


def exchange(array, axes):
    return lax.all_to_all(array, axes, split_axis=0, concat_axis=0, tiled=True)


def on_device(
    features, edge_tiles, block_lists, send_lists, train_ids, owners, cotangent,
    query_weight, key_weight, value_weight, out_weight, up_weight, down_weight,
):
    ids = train_ids.reshape(1, TRAIN)
    grads = lax.all_gather(cotangent.reshape(TOKS * FEATS, TRAIN), NARROW_AXES)
    owner_row = owners.reshape(1, TRAIN)
    send_slots = jnp.transpose(send_lists, (0, 2, 1))
    outgoing, counts = pack(send_slots, features, owner_row)
    counts = lax.all_gather(counts, WIDE)
    incoming = exchange(outgoing, WIDE)
    step = functools.partial(apply, jnp.transpose(block_lists), send_slots)
    current = features
    hops = None
    fields = [features]
    for hop in range(HOPS):
        if hop == 0:
            once, outgoing, degree, tiles, up_t, out_t = step(
                edge_tiles, current, incoming, stage=True, weights=(up_weight, out_weight)
            )
        elif hop == HOPS - 1:
            once, outgoing, tiles = step(
                edge_tiles, current, incoming, degree, hop=hop, stage=True
            )
        else:
            once, outgoing = step(tiles, current, incoming, degree, hop=hop)
        incoming = exchange(outgoing, WIDE)
        results = step(
            tiles, once, incoming, degree, previous=current, hops=hops, hop=hop,
            ids=None if hop == 0 else ids,
            others=tuple(fields) if hop == HOPS - 2 else (),
        )
        current, hops = results[0], results[1]
        fields.append(current)
        if hop == HOPS - 2:
            early = lax.all_gather(results[3], NARROW_AXES)
        if hop < HOPS - 1:
            incoming = exchange(results[2], WIDE)
    final = exchange(results[2], NARROW_AXES)
    place = jnp.stack(
        [2 * lax.axis_index("xl") + lax.axis_index("c"), lax.axis_index("xh")]
    ).astype(jnp.int32)
    known = early_part(
        place, early, grads, counts, owner_row, query_weight, key_weight, value_weight
    )
    partial = layer(
        final, known, place,
        query_weight, key_weight, value_weight, out_weight, out_t, up_weight, up_t, down_weight,
    )
    gathered = exchange(partial, QUADS)
    return (hops, *sum_parts(gathered))


def solution(mesh):
    split = Mesh(mesh.devices.reshape(4, 4, 2, 2, 2), ("z", "y", "xh", "xl", "c"))
    rows = P(WIDE + NARROW_AXES, None)
    in_specs = (
        P(NARROW_AXES, WIDE),
        P(WIDE, None, None, None),
        P(WIDE, None),
        P(WIDE, None, None),
        P(WIDE),
        P(WIDE, None),
        P(None, NARROW_AXES, WIDE),
        P(), P(), P(), P(), P(), P(),
    )
    out_specs = (P(None, NARROW_AXES, WIDE), rows, rows, rows)
    return jax.shard_map(
        on_device, mesh=split, in_specs=in_specs, out_specs=out_specs, check_vma=False
    )
```

```python
import functools
import math

import jax
import jax.numpy as jnp
from jax import lax
from jax.experimental import pallas as pl
from jax.experimental.pallas import tpu as pltpu
from jax.sharding import Mesh, PartitionSpec as P

D = 512
FF = 2048
HEADS = 8
HEAD_DIM = 64
HOPS = 3
TOKS = 4
BLK = 128
K = 12
SEND = 2
NB = 32
PARTS = 16
FEATS = 64
NODES = NB * BLK
TRAIN = 512
OWNERS = 128
QUAD = 4
QUAD_NODES = 256
NARROW = 8
DESTS = 32
GROUP = 16
UNROLL = 16
CHUNK = 4
IN_FLIGHT = 8
PICK_BLOCKS = 4
FF_CHUNK = 512
OUT_CHUNK = 128
EPSILON = 1e-05

BF = jnp.bfloat16
F32 = jnp.float32
WIDE = ("z", "y")
NARROW_AXES = ("xh", "xl", "c")
QUADS = ("z", "y", "xh")


def params(limit_mib):
    return pltpu.CompilerParams(vmem_limit_bytes=limit_mib * 1024 * 1024)


def dot(left, right):
    return jnp.dot(left, right, preferred_element_type=F32)


def dot_rows(left, right):
    return lax.dot_general(left, right, (((1,), (1,)), ((), ())), preferred_element_type=F32)


def block_columns(b):
    return pl.ds(b * BLK if isinstance(b, int) else pl.multiple_of(b * BLK, BLK), BLK)


def pack_kernel(sends, field, owners_h, outgoing, counts, owners, sems):
    names = pltpu.make_async_copy(owners_h, owners, sems.at[PARTS * SEND])
    names.start()
    copies = []
    for slot in range(PARTS * SEND):
        start = pl.multiple_of(sends[0, slot % SEND, slot // SEND] * BLK, BLK)
        rows = (slot % SEND) * FEATS
        copies.append(
            pltpu.make_async_copy(
                field.at[:, pl.ds(start, BLK)],
                outgoing.at[slot // SEND, rows : rows + FEATS, :],
                sems.at[slot],
            )
        )
    for copy in copies:
        copy.start()
    names.wait()
    named = lax.broadcasted_iota(jnp.int32, (OWNERS, TRAIN), 0) == owners[...]
    count = jnp.sum(jnp.where(named, 1.0, 0.0), axis=1, keepdims=True)
    counts[...] = jnp.broadcast_to(count, (OWNERS, OWNERS))
    for copy in copies:
        copy.wait()


def pack(sends, field, owners):
    return pl.pallas_call(
        pack_kernel,
        out_shape=[
            jax.ShapeDtypeStruct((PARTS, SEND * FEATS, BLK), BF),
            jax.ShapeDtypeStruct((OWNERS, OWNERS), F32),
        ],
        in_specs=[
            pl.BlockSpec(memory_space=pltpu.SMEM),
            pl.BlockSpec(memory_space=pltpu.HBM),
            pl.BlockSpec(memory_space=pltpu.HBM),
        ],
        scratch_shapes=[
            pltpu.VMEM((1, TRAIN), jnp.int32),
            pltpu.SemaphoreType.DMA((PARTS * SEND + 1,)),
        ],
        compiler_params=params(4),
        name="pack",
    )(in_hbm(sends), in_hbm(field), in_hbm(owners))


def picked_columns(ids, fields):
    id_row = ids[...]
    span = PICK_BLOCKS * BLK
    total = None
    for start in range(0, NODES, span):
        rows = lax.broadcasted_iota(jnp.int32, (span, TRAIN), 0) + start
        chosen = jnp.where(rows == id_row, 1.0, 0.0).astype(BF)
        block = jnp.concatenate([field[:, start : start + span] for field in fields], axis=0)
        term = dot(block, chosen)
        total = term if total is None else total + term
    return total.astype(BF)


def apply_kernel(*refs, second, first, last, picking, stage):
    refs = list(refs)
    lists, sends, tiles, field, incoming = refs[:5]
    refs = refs[5:]
    degree = None if first else refs.pop(0)
    previous = refs.pop(0) if second else None
    aliased = second and refs.pop(0)
    ids = refs.pop(0) if picking else None
    others = [refs.pop(0) for _ in range(picking - 1)] if picking else []
    result = refs.pop(0)
    hops = refs.pop(0) if second else None
    outgoing = None if last else refs.pop(0)
    rows_out = refs.pop(0) if picking else None
    degree_out = refs.pop(0) if first else None
    tiles_h, tiles = (tiles, refs.pop(0)) if stage else (None, tiles)
    pool, fresh, sems = refs

    def load(i):
        blocks = pl.ds(i * CHUNK, CHUNK)
        return pltpu.make_async_copy(tiles_h.at[blocks], tiles.at[blocks], sems.at[i])

    def store(i):
        cols = pl.ds(pl.multiple_of(i * UNROLL * BLK, UNROLL * BLK), UNROLL * BLK)
        return pltpu.make_async_copy(
            result.at[:, cols], hops.at[second - 1, :, cols], sems.at[i]
        )

    if stage:
        for i in range(IN_FLIGHT):
            load(i).start()

    for j in range(NB):
        pool[j] = field[:, j * BLK : (j + 1) * BLK]
    for j in range(PARTS * SEND):
        rows = (j % SEND) * FEATS
        pool[NB + j] = incoming[j // SEND, rows : rows + FEATS, :]

    def one_block(b):
        picked = jnp.concatenate([pool[lists[k, b]] for k in range(K)], axis=1)
        if first:
            picked = jnp.concatenate([picked, jnp.ones((GROUP, K * BLK), BF)], axis=0)
        summed = dot(picked, tiles[b].reshape(K * BLK, BLK))
        if first:
            share = summed[FEATS : FEATS + 1, :]
            degree_out[pl.ds(b, 1), :] = share
            summed = summed[:FEATS, :]
        else:
            share = degree[pl.ds(b, 1), :]
        value = (summed / share).astype(BF)
        cols = block_columns(b)
        if second:
            value = (
                0.5 * previous[:, cols].astype(F32) + pool[b].astype(F32) + value.astype(F32)
            ).astype(BF)
        result[:, cols] = value
        fresh[b] = value

    def some_blocks(i, carry):
        for j in range(UNROLL):
            one_block(i * UNROLL + j)
        if second:
            store(i).start()
        return carry

    if stage:
        for i in range(NB // CHUNK):
            load(i).wait()
            if i + IN_FLIGHT < NB // CHUNK:
                load(i + IN_FLIGHT).start()
            for j in range(CHUNK):
                one_block(i * CHUNK + j)
    else:
        lax.fori_loop(0, NB // UNROLL, some_blocks, 0)
    if not last:
        for slot in range(PARTS * SEND):
            rows = (slot % SEND) * FEATS
            outgoing[slot // SEND, rows : rows + FEATS, :] = fresh[
                sends[0, slot % SEND, slot // SEND]
            ]
    if picking:
        picked = picked_columns(ids, [*others, result])
        if last:
            for n in range(NARROW):
                half = n // QUAD
                rows_out[n] = picked[:, half * QUAD_NODES : (half + 1) * QUAD_NODES]
        else:
            rows_out[...] = picked
    if second:
        for i in range(NB // UNROLL):
            store(i).wait()


def apply(
    lists, sends, tiles, field, incoming, degree=None, previous=None, hops=None, hop=0, ids=None, others=(), stage=False,
):
    second = previous is not None
    last = second and hop == HOPS - 1
    first = hop == 0 and not second
    smem = pl.BlockSpec(memory_space=pltpu.SMEM)
    vmem = pl.BlockSpec(memory_space=pltpu.VMEM)
    hbm = pl.BlockSpec(memory_space=pltpu.HBM)
    operands = [in_hbm(lists), in_hbm(sends), in_hbm(tiles) if stage else in_vmem(tiles), field, incoming]
    in_specs = [smem, smem, hbm if stage else vmem, vmem, vmem]
    if not first:
        operands.append(degree)
        in_specs.append(vmem)
    out_shape = [jax.ShapeDtypeStruct((FEATS, NODES), BF)]
    out_specs = [vmem]
    aliases = {}
    if second:
        operands.append(previous)
        in_specs.append(vmem)
        if hops is None:
            operands.append(sends)
            in_specs.append(smem)
        else:
            aliases = {len(operands): 1}
            operands.append(hops)
            in_specs.append(hbm)
        out_shape.append(jax.ShapeDtypeStruct((HOPS, FEATS, NODES), BF))
        out_specs.append(hbm)
    if ids is not None:
        operands += [ids, *others]
        in_specs += [vmem] * (1 + len(others))
    if not last:
        out_shape.append(jax.ShapeDtypeStruct((PARTS, SEND * FEATS, BLK), BF))
        out_specs.append(vmem)
    if ids is not None:
        rows = FEATS * (1 + len(others))
        shape = (NARROW, rows, QUAD_NODES) if last else (rows, TRAIN)
        out_shape.append(jax.ShapeDtypeStruct(shape, BF))
        out_specs.append(vmem)
    if first:
        out_shape.append(jax.ShapeDtypeStruct((NB, BLK), F32))
        out_specs.append(vmem)
    if stage:
        out_shape.append(pltpu.VMEM(tiles.shape, BF))
        out_specs.append(vmem)
    scratch = [
        pltpu.VMEM((2 * NB, FEATS, BLK), BF),
        pltpu.VMEM((NB, FEATS, BLK), BF),
        pltpu.SemaphoreType.DMA((NB // CHUNK,)),
    ]
    return pl.pallas_call(
        functools.partial(
            apply_kernel, second=second and hop + 1, first=first, last=last,
            picking=0 if ids is None else 1 + len(others), stage=stage,
        ),
        out_shape=out_shape,
        in_specs=in_specs,
        out_specs=out_specs,
        scratch_shapes=scratch,
        input_output_aliases=aliases,
        compiler_params=params(8),
        name=f"apply_{'second' if second else 'first'}_{hop}",
    )(*operands)


def normalize(hidden):
    center = hidden - jnp.mean(hidden, axis=0, keepdims=True)
    inverse = lax.rsqrt(jnp.mean(center * center, axis=0, keepdims=True) + EPSILON)
    return center * inverse, inverse


def copies_of(pairs, sems):
    return [
        pltpu.make_async_copy(source, target, sems.at[index])
        for index, (source, target) in enumerate(pairs)
    ]


def early_kernel(
    place, early_h, grads_h, counts_h, owners_h, query_h, key_h, value_h,
    tokens_h, normed_h, query_oh, key_oh, value_oh, scaled_h,
    early, grads, counts, owners, query_w, key_w, value_w,
    tokens_s, normed_s, query_s, key_s, value_s, scaled_s, sems,
):
    mine = pl.ds(pl.multiple_of(place[1] * QUAD_NODES, QUAD_NODES), QUAD_NODES)
    loads = copies_of(
        (
            (early_h.at[:, :, mine], early), (query_h, query_w), (key_h, key_w),
            (value_h, value_w), (counts_h, counts), (owners_h, owners),
            (grads_h.at[:, :, mine], grads),
        ),
        sems,
    )
    stores = copies_of(
        (
            (tokens_s, tokens_h), (normed_s, normed_h), (query_s, query_oh),
            (key_s, key_oh), (value_s, value_oh), (scaled_s, scaled_h),
        ),
        sems.at[pl.ds(len(loads), 6)],
    )
    for load in loads:
        load.start()
    loads[0].wait()
    for t in range(HOPS):
        cols = slice(t * QUAD_NODES, (t + 1) * QUAD_NODES)
        tokens = early[:, t * FEATS : (t + 1) * FEATS, :].reshape(D, QUAD_NODES)
        tokens_s[:, cols] = tokens
        normed_s[:, cols] = normalize(tokens.astype(F32))[0].astype(BF)
    stores[0].start()
    stores[1].start()
    for index, (weight, target) in enumerate(
        ((query_w, query_s), (key_w, key_s), (value_w, value_s))
    ):
        loads[1 + index].wait()
        target[...] = dot(weight[...], normed_s[...]).astype(BF)
        stores[2 + index].start()
    for load in loads[4:]:
        load.wait()
    named = lax.broadcasted_iota(jnp.int32, (OWNERS, QUAD_NODES), 0) == owners[:, mine]
    totals = jnp.sum(counts[...], axis=0)
    by_owner = jnp.concatenate([1.0 / totals] * (QUAD_NODES // OWNERS), axis=1)
    row_scale = jnp.sum(jnp.where(named, by_owner, 0.0), axis=0, keepdims=True)
    for t in range(TOKS):
        rows = grads[:, t * FEATS : (t + 1) * FEATS, :].reshape(D, QUAD_NODES)
        scaled_s[:, t * QUAD_NODES : (t + 1) * QUAD_NODES] = (
            rows.astype(F32) * row_scale
        ).astype(BF)
    stores[5].start()
    for store in stores:
        store.wait()


def early_part(place, early, grads, counts, owners, *weights):
    hbm = pl.BlockSpec(memory_space=pltpu.HBM)
    smem = pl.BlockSpec(memory_space=pltpu.SMEM)
    shapes = [(D, HOPS * QUAD_NODES)] * 5 + [(D, TOKS * QUAD_NODES)]
    return pl.pallas_call(
        early_kernel,
        out_shape=[pltpu.HBM(shape, BF) for shape in shapes],
        in_specs=[smem] + [hbm] * 7,
        out_specs=[hbm] * 6,
        scratch_shapes=[
            pltpu.VMEM((NARROW, HOPS * FEATS, QUAD_NODES), BF),
            pltpu.VMEM((NARROW, TOKS * FEATS, QUAD_NODES), BF),
            pltpu.VMEM((PARTS, OWNERS, OWNERS), F32),
            pltpu.VMEM((1, TRAIN), jnp.int32),
            *[pltpu.VMEM(w.shape, BF) for w in weights],
            *[pltpu.VMEM(shape, BF) for shape in shapes],
            pltpu.SemaphoreType.DMA((13,)),
        ],
        compiler_params=params(24),
        name="early",
    )(place, *[in_hbm(array) for array in (early, grads, counts, owners, *weights)])


def layer_kernel(
    final, tokens_h, normed_h, query_ih, key_ih, value_ih, scaled_h, place,
    query_h, key_h, value_h, out_h, up_h, down_h,
    result, query_s, key_s, value_s, mixed_s, probs_s, act_s, pre_s, gmix_s, gq_s, gk_s, gv_s, gr_s,
    query_w, key_w, value_w, out_w, up_w, down_w, out_t, up_t, tokens_s, normed_s, scaled_s, sems,
):
    own = place[0]
    width = TOKS * QUAD_NODES
    known = slice(0, HOPS * QUAD_NODES)
    added = slice(HOPS * QUAD_NODES, width)
    loads = copies_of(
        (
            (query_h, query_w), (key_h, key_w), (value_h, value_w),
            (query_ih, query_s.at[:, known]), (key_ih, key_s.at[:, known]),
            (value_ih, value_s.at[:, known]), (out_h, out_w), (tokens_h, tokens_s.at[:, known]),
            (up_h, up_w), (down_h, down_w), (scaled_h, scaled_s),
            (normed_h, normed_s.at[:, known]),
        ),
        sems,
    )
    for load in loads:
        load.start()
    last = final[...].reshape(D, QUAD_NODES)
    tokens_s[:, added] = last
    last = normalize(last.astype(F32))[0].astype(BF)
    normed_s[:, added] = last
    for index, (weight, target) in enumerate(
        ((query_w, query_s), (key_w, key_s), (value_w, value_s))
    ):
        loads[index].wait()
        target[:, added] = dot(weight[...], last).astype(BF)
    for load in loads[3:6]:
        load.wait()
    score_scale = 1.0 / math.sqrt(HEAD_DIM)

    def columns(half):
        return [
            pl.ds(pl.multiple_of(t * QUAD_NODES + half * BLK, BLK), BLK) for t in range(TOKS)
        ]

    def parts(ref, rows, cols):
        return [ref[rows, c].astype(F32) for c in cols]

    def forward_head(step, carry):
        h = step // 2
        cols = columns(step % 2)
        rows = pl.ds(pl.multiple_of(h * HEAD_DIM, HEAD_DIM), HEAD_DIM)
        query, key, value = [parts(ref, rows, cols) for ref in (query_s, key_s, value_s)]
        all_probs = []
        for t in range(TOKS):
            scores = [
                jnp.sum(query[t] * key[u], axis=0, keepdims=True) * score_scale
                for u in range(TOKS)
            ]
            top = jnp.maximum(
                jnp.maximum(scores[0], scores[1]), jnp.maximum(scores[2], scores[3])
            )
            raised = [jnp.exp(s - top) for s in scores]
            total = raised[0] + raised[1] + raised[2] + raised[3]
            probs = [r / total for r in raised]
            all_probs += probs
            low = [p.astype(BF).astype(F32) for p in probs]
            mixed_s[rows, cols[t]] = (
                low[0] * value[0] + low[1] * value[1] + low[2] * value[2] + low[3] * value[3]
            ).astype(BF)
        probs_s[step] = jnp.concatenate(all_probs, axis=0)
        return carry

    lax.fori_loop(0, 2 * HEADS, forward_head, 0)
    loads[6].wait()
    loads[7].wait()
    residual = (tokens_s[...].astype(F32) + dot(out_w[...], mixed_s[...])).astype(BF)
    second_norm, second_inv = normalize(residual.astype(F32))
    normed_b = second_norm.astype(BF)

    root = math.sqrt(2.0 / math.pi)
    groups = FF_CHUNK // (QUAD * GROUP)

    def ffn_chunk(i, carry):
        rows = pl.ds(pl.multiple_of(i * FF_CHUNK, FF_CHUNK), FF_CHUNK)
        up_t[:, rows] = jnp.transpose(up_w[rows, :])
        share = pl.ds(pl.multiple_of(i * OUT_CHUNK, OUT_CHUNK), OUT_CHUNK)
        out_t[:, share] = jnp.transpose(out_w[share, :])
        pre = dot(up_w[rows, :], normed_b)
        grad_act = dot(down_w[rows, :], scaled_s[...])
        square = pre * pre
        gate = 0.5 + 0.5 * jnp.tanh(pre * (root + (root * 0.044715) * square))
        activated = pre * gate
        slope = gate + activated * (1.0 - gate) * (
            2.0 * root + (6.0 * root * 0.044715) * square
        )
        at = pl.ds(i * groups, groups)
        act_s[at] = activated.astype(BF).reshape(groups, QUAD, GROUP, width)
        pre_s[at] = (grad_act * slope).astype(BF).reshape(groups, QUAD, GROUP, width)
        return carry

    for load in loads[8:11]:
        load.wait()
    lax.fori_loop(0, FF // FF_CHUNK, ffn_chunk, 0)

    share = FF // QUAD
    grad_down = dot_rows(act_s[:, own].reshape(share, width), scaled_s[...])
    result[:, 2 * GROUP : 3 * GROUP, :] = grad_down.astype(BF).reshape(DESTS, GROUP, D)
    grad_up = dot_rows(pre_s[:, own].reshape(share, width), normed_b)
    result[:, GROUP : 2 * GROUP, :] = grad_up.astype(BF).reshape(DESTS, GROUP, D)

    grad_normed = dot(up_t[...], pre_s[...].reshape(FF, width))
    grad_resid = (
        scaled_s[...].astype(F32)
        + second_inv
        * (
            grad_normed
            - jnp.mean(grad_normed, axis=0, keepdims=True)
            - second_norm * jnp.mean(grad_normed * second_norm, axis=0, keepdims=True)
        )
    ).astype(BF)
    gr_s[...] = grad_resid.reshape(HEADS, QUAD, GROUP, width)
    gmix_s[...] = dot(out_t[...], grad_resid).astype(BF)

    def backward_head(step, carry):
        h = step // 2
        cols = columns(step % 2)
        rows = pl.ds(pl.multiple_of(h * HEAD_DIM, HEAD_DIM), HEAD_DIM)
        query, key, value, grad_mixed = [
            parts(ref, rows, cols) for ref in (query_s, key_s, value_s, gmix_s)
        ]
        saved = probs_s[step]
        prob = lambda t, u: saved[t * TOKS + u : t * TOKS + u + 1, :]
        weights = []
        grad_query = []
        for t in range(TOKS):
            grad_probs = [
                jnp.sum(grad_mixed[t] * value[u], axis=0, keepdims=True) for u in range(TOKS)
            ]
            inner = sum(prob(t, u) * grad_probs[u] for u in range(TOKS))
            weight = [
                (prob(t, u) * (grad_probs[u] - inner) * score_scale).astype(BF).astype(F32)
                for u in range(TOKS)
            ]
            weights.append(weight)
            grad_query.append(sum(weight[u] * key[u] for u in range(TOKS)))
        grad_key = [sum(weights[t][u] * query[t] for t in range(TOKS)) for u in range(TOKS)]
        grad_value = [
            sum(prob(t, u).astype(BF).astype(F32) * grad_mixed[t] for t in range(TOKS))
            for u in range(TOKS)
        ]
        for ref, pieces in ((gq_s, grad_query), (gk_s, grad_key), (gv_s, grad_value)):
            for t in range(TOKS):
                ref[h, :, :, cols[t]] = pieces[t].astype(BF).reshape(QUAD, GROUP, BLK)
        return carry

    lax.fori_loop(0, 2 * HEADS, backward_head, 0)
    share = D // QUAD
    stacked = jnp.concatenate(
        [ref[:, own].reshape(share, width) for ref in (gq_s, gk_s, gv_s)], axis=0
    )
    count = HEADS * 3
    loads[11].wait()
    result[:count, 0:GROUP, :] = dot_rows(stacked, normed_s[...]).astype(BF).reshape(count, GROUP, D)
    sum_out = dot_rows(gr_s[:, own].reshape(share, width), mixed_s[...])
    result[count:, 0:GROUP, :] = sum_out.astype(BF).reshape(HEADS, GROUP, D)


def in_vmem(array):
    return pltpu.with_memory_space_constraint(array, pltpu.VMEM)


def in_hbm(array):
    return pltpu.with_memory_space_constraint(array, pltpu.HBM)


def layer(final, known, place, *weights):
    width = TOKS * QUAD_NODES
    square = pltpu.VMEM((D, width), BF)
    grouped = pltpu.VMEM((HEADS, QUAD, GROUP, width), BF)
    wide = pltpu.VMEM((DESTS, QUAD, GROUP, width), BF)
    vmem = pl.BlockSpec(memory_space=pltpu.VMEM)
    hbm = pl.BlockSpec(memory_space=pltpu.HBM)
    smem = pl.BlockSpec(memory_space=pltpu.SMEM)
    return pl.pallas_call(
        layer_kernel,
        out_shape=jax.ShapeDtypeStruct((DESTS, 3 * GROUP, D), BF),
        in_specs=[vmem] + [hbm] * 6 + [smem] + [hbm] * 6,
        out_specs=vmem,
        scratch_shapes=[
            square, square, square, square,
            pltpu.VMEM((2 * HEADS, TOKS * TOKS, BLK), F32),
            wide, wide, square, grouped, grouped, grouped, grouped,
            *[pltpu.VMEM(w.shape, BF) for w in weights],
            pltpu.VMEM((D, D), BF),
            pltpu.VMEM((D, FF), BF),
            square, square, square,
            pltpu.SemaphoreType.DMA((12,)),
        ],
        compiler_params=params(48),
        name="layer",
    )(final, *[in_hbm(k) for k in known], place, *[in_hbm(w) for w in weights])


def sum_kernel(gathered, *outs):
    total = jnp.sum(gathered[...].astype(F32), axis=0)
    for index, out in enumerate(outs):
        out[...] = total[index * GROUP : (index + 1) * GROUP]


def sum_parts(gathered):
    return pl.pallas_call(
        sum_kernel,
        out_shape=[jax.ShapeDtypeStruct((GROUP, D), F32)] * 3,
        compiler_params=params(8),
        name="sum_parts",
    )(gathered)


def exchange(array, axes):
    return lax.all_to_all(array, axes, split_axis=0, concat_axis=0, tiled=True)


def on_device(
    features, edge_tiles, block_lists, send_lists, train_ids, owners, cotangent,
    query_weight, key_weight, value_weight, out_weight, up_weight, down_weight,
):
    ids = train_ids.reshape(1, TRAIN)
    grads = lax.all_gather(cotangent.reshape(TOKS * FEATS, TRAIN), NARROW_AXES)
    owner_row = owners.reshape(1, TRAIN)
    send_slots = jnp.transpose(send_lists, (0, 2, 1))
    outgoing, counts = pack(send_slots, features, owner_row)
    counts = lax.all_gather(counts, WIDE)
    incoming = exchange(outgoing, WIDE)
    step = functools.partial(apply, jnp.transpose(block_lists), send_slots)
    current = features
    hops = None
    fields = [features]
    for hop in range(HOPS):
        if hop == 0:
            once, outgoing, degree, tiles = step(edge_tiles, current, incoming, stage=True)
        elif hop == HOPS - 1:
            once, outgoing, tiles = step(
                edge_tiles, current, incoming, degree, hop=hop, stage=True
            )
        else:
            once, outgoing = step(tiles, current, incoming, degree, hop=hop)
        incoming = exchange(outgoing, WIDE)
        results = step(
            tiles, once, incoming, degree, previous=current, hops=hops, hop=hop,
            ids=None if hop == 0 else ids,
            others=tuple(fields) if hop == HOPS - 2 else (),
        )
        current, hops = results[0], results[1]
        fields.append(current)
        if hop == HOPS - 2:
            early = lax.all_gather(results[3], NARROW_AXES)
        if hop < HOPS - 1:
            incoming = exchange(results[2], WIDE)
    final = exchange(results[2], NARROW_AXES)
    place = jnp.stack(
        [2 * lax.axis_index("xl") + lax.axis_index("c"), lax.axis_index("xh")]
    ).astype(jnp.int32)
    known = early_part(
        place, early, grads, counts, owner_row, query_weight, key_weight, value_weight
    )
    partial = layer(
        final, known, place,
        query_weight, key_weight, value_weight, out_weight, up_weight, down_weight,
    )
    gathered = exchange(partial, QUADS)
    return (hops, *sum_parts(gathered))


def solution(mesh):
    split = Mesh(mesh.devices.reshape(4, 4, 2, 2, 2), ("z", "y", "xh", "xl", "c"))
    rows = P(WIDE + NARROW_AXES, None)
    in_specs = (
        P(NARROW_AXES, WIDE),
        P(WIDE, None, None, None),
        P(WIDE, None),
        P(WIDE, None, None),
        P(WIDE),
        P(WIDE, None),
        P(None, NARROW_AXES, WIDE),
        P(), P(), P(), P(), P(), P(),
    )
    out_specs = (P(None, NARROW_AXES, WIDE), rows, rows, rows)
    return jax.shard_map(
        on_device, mesh=split, in_specs=in_specs, out_specs=out_specs, check_vma=False
    )
```

```python
import functools
import math

import jax
import jax.numpy as jnp
from jax import lax
from jax.experimental import pallas as pl
from jax.experimental.pallas import tpu as pltpu
from jax.sharding import Mesh, PartitionSpec as P

D = 512
FF = 2048
HEADS = 8
HEAD_DIM = 64
HOPS = 3
TOKS = 4
BLK = 128
K = 12
SEND = 2
NB = 32
PARTS = 16
FEATS = 64
NODES = NB * BLK
TRAIN = 512
OWNERS = 128
QUAD = 4
QUAD_NODES = 256
NARROW = 8
DESTS = 32
GROUP = 16
UNROLL = 16
CHUNK = 4
IN_FLIGHT = 8
PICK_BLOCKS = 4
FF_CHUNK = 512
OUT_CHUNK = 128
EPSILON = 1e-05

BF = jnp.bfloat16
F32 = jnp.float32
WIDE = ("z", "y")
NARROW_AXES = ("xh", "xl", "c")
QUADS = ("z", "y", "xh")


def params(limit_mib):
    return pltpu.CompilerParams(vmem_limit_bytes=limit_mib * 1024 * 1024)


def dot(left, right):
    return jnp.dot(left, right, preferred_element_type=F32)


def dot_rows(left, right):
    return lax.dot_general(left, right, (((1,), (1,)), ((), ())), preferred_element_type=F32)


def block_columns(b):
    return pl.ds(b * BLK if isinstance(b, int) else pl.multiple_of(b * BLK, BLK), BLK)


def pack_kernel(sends, field, owners_h, outgoing, counts, owners, sems):
    names = pltpu.make_async_copy(owners_h, owners, sems.at[PARTS * SEND])
    names.start()
    copies = []
    for slot in range(PARTS * SEND):
        start = pl.multiple_of(sends[0, slot % SEND, slot // SEND] * BLK, BLK)
        rows = (slot % SEND) * FEATS
        copies.append(
            pltpu.make_async_copy(
                field.at[:, pl.ds(start, BLK)],
                outgoing.at[slot // SEND, rows : rows + FEATS, :],
                sems.at[slot],
            )
        )
    for copy in copies:
        copy.start()
    names.wait()
    named = lax.broadcasted_iota(jnp.int32, (OWNERS, TRAIN), 0) == owners[...]
    count = jnp.sum(jnp.where(named, 1.0, 0.0), axis=1, keepdims=True)
    counts[...] = jnp.broadcast_to(count, (OWNERS, OWNERS))
    for copy in copies:
        copy.wait()


def pack(sends, field, owners):
    return pl.pallas_call(
        pack_kernel,
        out_shape=[
            jax.ShapeDtypeStruct((PARTS, SEND * FEATS, BLK), BF),
            jax.ShapeDtypeStruct((OWNERS, OWNERS), F32),
        ],
        in_specs=[
            pl.BlockSpec(memory_space=pltpu.SMEM),
            pl.BlockSpec(memory_space=pltpu.HBM),
            pl.BlockSpec(memory_space=pltpu.HBM),
        ],
        scratch_shapes=[
            pltpu.VMEM((1, TRAIN), jnp.int32),
            pltpu.SemaphoreType.DMA((PARTS * SEND + 1,)),
        ],
        compiler_params=params(4),
        name="pack",
    )(in_hbm(sends), in_hbm(field), in_hbm(owners))


def picked_columns(ids, fields):
    id_row = ids[...]
    span = PICK_BLOCKS * BLK
    total = None
    for start in range(0, NODES, span):
        rows = lax.broadcasted_iota(jnp.int32, (span, TRAIN), 0) + start
        chosen = jnp.where(rows == id_row, 1.0, 0.0).astype(BF)
        block = jnp.concatenate([field[:, start : start + span] for field in fields], axis=0)
        term = dot(block, chosen)
        total = term if total is None else total + term
    return total.astype(BF)


def apply_kernel(*refs, second, first, last, picking, stage):
    refs = list(refs)
    lists, sends, tiles, field, incoming = refs[:5]
    refs = refs[5:]
    degree = None if first else refs.pop(0)
    previous = refs.pop(0) if second else None
    aliased = second and refs.pop(0)
    ids = refs.pop(0) if picking else None
    others = [refs.pop(0) for _ in range(picking - 1)] if picking else []
    result = refs.pop(0)
    hops = refs.pop(0) if second else None
    outgoing = None if last else refs.pop(0)
    rows_out = refs.pop(0) if picking else None
    degree_out = refs.pop(0) if first else None
    tiles_h, tiles = (tiles, refs.pop(0)) if stage else (None, tiles)
    pool, fresh, sems = refs

    def load(i):
        blocks = pl.ds(i * CHUNK, CHUNK)
        return pltpu.make_async_copy(tiles_h.at[blocks], tiles.at[blocks], sems.at[i])

    def store(i):
        cols = pl.ds(pl.multiple_of(i * UNROLL * BLK, UNROLL * BLK), UNROLL * BLK)
        return pltpu.make_async_copy(
            result.at[:, cols], hops.at[second - 1, :, cols], sems.at[i]
        )

    if stage:
        for i in range(IN_FLIGHT):
            load(i).start()

    for j in range(NB):
        pool[j] = field[:, j * BLK : (j + 1) * BLK]
    for j in range(PARTS * SEND):
        rows = (j % SEND) * FEATS
        pool[NB + j] = incoming[j // SEND, rows : rows + FEATS, :]

    def one_block(b):
        picked = jnp.concatenate([pool[lists[k, b]] for k in range(K)], axis=1)
        if first:
            picked = jnp.concatenate([picked, jnp.ones((GROUP, K * BLK), BF)], axis=0)
        summed = dot(picked, tiles[b].reshape(K * BLK, BLK))
        if first:
            share = summed[FEATS : FEATS + 1, :]
            degree_out[pl.ds(b, 1), :] = share
            summed = summed[:FEATS, :]
        else:
            share = degree[pl.ds(b, 1), :]
        value = (summed / share).astype(BF)
        cols = block_columns(b)
        if second:
            value = (
                0.5 * previous[:, cols].astype(F32) + pool[b].astype(F32) + value.astype(F32)
            ).astype(BF)
        result[:, cols] = value
        fresh[b] = value

    def some_blocks(i, carry):
        for j in range(UNROLL):
            one_block(i * UNROLL + j)
        if second:
            store(i).start()
        return carry

    if stage:
        for i in range(NB // CHUNK):
            load(i).wait()
            if i + IN_FLIGHT < NB // CHUNK:
                load(i + IN_FLIGHT).start()
            for j in range(CHUNK):
                one_block(i * CHUNK + j)
    else:
        lax.fori_loop(0, NB // UNROLL, some_blocks, 0)
    if not last:
        for slot in range(PARTS * SEND):
            rows = (slot % SEND) * FEATS
            outgoing[slot // SEND, rows : rows + FEATS, :] = fresh[
                sends[0, slot % SEND, slot // SEND]
            ]
    if picking:
        picked = picked_columns(ids, [*others, result])
        if last:
            for n in range(NARROW):
                half = n // QUAD
                rows_out[n] = picked[:, half * QUAD_NODES : (half + 1) * QUAD_NODES]
        else:
            rows_out[...] = picked
    if second:
        for i in range(NB // UNROLL):
            store(i).wait()


def apply(
    lists, sends, tiles, field, incoming, degree=None, previous=None, hops=None, hop=0, ids=None, others=(), stage=False,
):
    second = previous is not None
    last = second and hop == HOPS - 1
    first = hop == 0 and not second
    smem = pl.BlockSpec(memory_space=pltpu.SMEM)
    vmem = pl.BlockSpec(memory_space=pltpu.VMEM)
    hbm = pl.BlockSpec(memory_space=pltpu.HBM)
    operands = [in_hbm(lists), in_hbm(sends), in_hbm(tiles) if stage else in_vmem(tiles), field, incoming]
    in_specs = [smem, smem, hbm if stage else vmem, vmem, vmem]
    if not first:
        operands.append(degree)
        in_specs.append(vmem)
    out_shape = [jax.ShapeDtypeStruct((FEATS, NODES), BF)]
    out_specs = [vmem]
    aliases = {}
    if second:
        operands.append(previous)
        in_specs.append(vmem)
        if hops is None:
            operands.append(sends)
            in_specs.append(smem)
        else:
            aliases = {len(operands): 1}
            operands.append(hops)
            in_specs.append(hbm)
        out_shape.append(jax.ShapeDtypeStruct((HOPS, FEATS, NODES), BF))
        out_specs.append(hbm)
    if ids is not None:
        operands += [ids, *others]
        in_specs += [vmem] * (1 + len(others))
    if not last:
        out_shape.append(jax.ShapeDtypeStruct((PARTS, SEND * FEATS, BLK), BF))
        out_specs.append(vmem)
    if ids is not None:
        rows = FEATS * (1 + len(others))
        shape = (NARROW, rows, QUAD_NODES) if last else (rows, TRAIN)
        out_shape.append(jax.ShapeDtypeStruct(shape, BF))
        out_specs.append(vmem)
    if first:
        out_shape.append(jax.ShapeDtypeStruct((NB, BLK), F32))
        out_specs.append(vmem)
    if stage:
        out_shape.append(pltpu.VMEM(tiles.shape, BF))
        out_specs.append(vmem)
    scratch = [
        pltpu.VMEM((2 * NB, FEATS, BLK), BF),
        pltpu.VMEM((NB, FEATS, BLK), BF),
        pltpu.SemaphoreType.DMA((NB // CHUNK,)),
    ]
    return pl.pallas_call(
        functools.partial(
            apply_kernel, second=second and hop + 1, first=first, last=last,
            picking=0 if ids is None else 1 + len(others), stage=stage,
        ),
        out_shape=out_shape,
        in_specs=in_specs,
        out_specs=out_specs,
        scratch_shapes=scratch,
        input_output_aliases=aliases,
        compiler_params=params(8),
        name=f"apply_{'second' if second else 'first'}_{hop}",
    )(*operands)


def normalize(hidden):
    center = hidden - jnp.mean(hidden, axis=0, keepdims=True)
    inverse = lax.rsqrt(jnp.mean(center * center, axis=0, keepdims=True) + EPSILON)
    return center * inverse, inverse


def copies_of(pairs, sems):
    return [
        pltpu.make_async_copy(source, target, sems.at[index])
        for index, (source, target) in enumerate(pairs)
    ]


def early_kernel(
    place, early_h, grads_h, counts_h, owners_h, query_h, key_h, value_h,
    tokens_h, normed_h, query_oh, key_oh, value_oh, scaled_h,
    early, grads, counts, owners, query_w, key_w, value_w,
    tokens_s, normed_s, query_s, key_s, value_s, scaled_s, sems,
):
    mine = pl.ds(pl.multiple_of(place[1] * QUAD_NODES, QUAD_NODES), QUAD_NODES)
    loads = copies_of(
        (
            (early_h.at[:, :, mine], early), (query_h, query_w), (key_h, key_w),
            (value_h, value_w), (counts_h, counts), (owners_h, owners),
            (grads_h.at[:, :, mine], grads),
        ),
        sems,
    )
    stores = copies_of(
        (
            (tokens_s, tokens_h), (normed_s, normed_h), (query_s, query_oh),
            (key_s, key_oh), (value_s, value_oh), (scaled_s, scaled_h),
        ),
        sems.at[pl.ds(len(loads), 6)],
    )
    for load in loads:
        load.start()
    loads[0].wait()
    for t in range(HOPS):
        cols = slice(t * QUAD_NODES, (t + 1) * QUAD_NODES)
        tokens = early[:, t * FEATS : (t + 1) * FEATS, :].reshape(D, QUAD_NODES)
        tokens_s[:, cols] = tokens
        normed_s[:, cols] = normalize(tokens.astype(F32))[0].astype(BF)
    stores[0].start()
    stores[1].start()
    for index, (weight, target) in enumerate(
        ((query_w, query_s), (key_w, key_s), (value_w, value_s))
    ):
        loads[1 + index].wait()
        target[...] = dot(weight[...], normed_s[...]).astype(BF)
        stores[2 + index].start()
    for load in loads[4:]:
        load.wait()
    named = lax.broadcasted_iota(jnp.int32, (OWNERS, QUAD_NODES), 0) == owners[:, mine]
    totals = jnp.sum(counts[...], axis=0)
    by_owner = jnp.concatenate([1.0 / totals] * (QUAD_NODES // OWNERS), axis=1)
    row_scale = jnp.sum(jnp.where(named, by_owner, 0.0), axis=0, keepdims=True)
    for t in range(TOKS):
        rows = grads[:, t * FEATS : (t + 1) * FEATS, :].reshape(D, QUAD_NODES)
        scaled_s[:, t * QUAD_NODES : (t + 1) * QUAD_NODES] = (
            rows.astype(F32) * row_scale
        ).astype(BF)
    stores[5].start()
    for store in stores:
        store.wait()


def early_part(place, early, grads, counts, owners, *weights):
    hbm = pl.BlockSpec(memory_space=pltpu.HBM)
    smem = pl.BlockSpec(memory_space=pltpu.SMEM)
    shapes = [(D, HOPS * QUAD_NODES)] * 5 + [(D, TOKS * QUAD_NODES)]
    return pl.pallas_call(
        early_kernel,
        out_shape=[pltpu.HBM(shape, BF) for shape in shapes],
        in_specs=[smem] + [hbm] * 7,
        out_specs=[hbm] * 6,
        scratch_shapes=[
            pltpu.VMEM((NARROW, HOPS * FEATS, QUAD_NODES), BF),
            pltpu.VMEM((NARROW, TOKS * FEATS, QUAD_NODES), BF),
            pltpu.VMEM((PARTS, OWNERS, OWNERS), F32),
            pltpu.VMEM((1, TRAIN), jnp.int32),
            *[pltpu.VMEM(w.shape, BF) for w in weights],
            *[pltpu.VMEM(shape, BF) for shape in shapes],
            pltpu.SemaphoreType.DMA((13,)),
        ],
        compiler_params=params(24),
        name="early",
    )(place, *[in_hbm(array) for array in (early, grads, counts, owners, *weights)])


def layer_kernel(
    final, tokens_h, normed_h, query_ih, key_ih, value_ih, scaled_h, place,
    query_h, key_h, value_h, out_h, up_h, down_h,
    result, query_s, key_s, value_s, mixed_s, probs_s, act_s, pre_s, gmix_s, gq_s, gk_s, gv_s, gr_s,
    query_w, key_w, value_w, out_w, up_w, down_w, out_t, up_t, tokens_s, normed_s, scaled_s, sems,
):
    own = place[0]
    width = TOKS * QUAD_NODES
    known = slice(0, HOPS * QUAD_NODES)
    added = slice(HOPS * QUAD_NODES, width)
    loads = copies_of(
        (
            (query_h, query_w), (key_h, key_w), (value_h, value_w),
            (query_ih, query_s.at[:, known]), (key_ih, key_s.at[:, known]),
            (value_ih, value_s.at[:, known]), (out_h, out_w), (tokens_h, tokens_s.at[:, known]),
            (up_h, up_w), (down_h, down_w), (scaled_h, scaled_s),
            (normed_h, normed_s.at[:, known]),
        ),
        sems,
    )
    for load in loads[:6]:
        load.start()
    last = final[...].reshape(D, QUAD_NODES)
    tokens_s[:, added] = last
    last = normalize(last.astype(F32))[0].astype(BF)
    normed_s[:, added] = last
    for index, (weight, target) in enumerate(
        ((query_w, query_s), (key_w, key_s), (value_w, value_s))
    ):
        loads[index].wait()
        target[:, added] = dot(weight[...], last).astype(BF)
    for load in loads[3:6]:
        load.wait()
    for load in loads[6:]:
        load.start()
    score_scale = 1.0 / math.sqrt(HEAD_DIM)

    def columns(half):
        return [
            pl.ds(pl.multiple_of(t * QUAD_NODES + half * BLK, BLK), BLK) for t in range(TOKS)
        ]

    def parts(ref, rows, cols):
        return [ref[rows, c].astype(F32) for c in cols]

    def forward_head(step, carry):
        h = step // 2
        cols = columns(step % 2)
        rows = pl.ds(pl.multiple_of(h * HEAD_DIM, HEAD_DIM), HEAD_DIM)
        query, key, value = [parts(ref, rows, cols) for ref in (query_s, key_s, value_s)]
        all_probs = []
        for t in range(TOKS):
            scores = [
                jnp.sum(query[t] * key[u], axis=0, keepdims=True) * score_scale
                for u in range(TOKS)
            ]
            top = jnp.maximum(
                jnp.maximum(scores[0], scores[1]), jnp.maximum(scores[2], scores[3])
            )
            raised = [jnp.exp(s - top) for s in scores]
            total = raised[0] + raised[1] + raised[2] + raised[3]
            probs = [r / total for r in raised]
            all_probs += probs
            low = [p.astype(BF).astype(F32) for p in probs]
            mixed_s[rows, cols[t]] = (
                low[0] * value[0] + low[1] * value[1] + low[2] * value[2] + low[3] * value[3]
            ).astype(BF)
        probs_s[step] = jnp.concatenate(all_probs, axis=0)
        return carry

    lax.fori_loop(0, 2 * HEADS, forward_head, 0)
    loads[6].wait()
    loads[7].wait()
    residual = (tokens_s[...].astype(F32) + dot(out_w[...], mixed_s[...])).astype(BF)
    second_norm, second_inv = normalize(residual.astype(F32))
    normed_b = second_norm.astype(BF)

    root = math.sqrt(2.0 / math.pi)
    groups = FF_CHUNK // (QUAD * GROUP)

    def ffn_chunk(i, carry):
        rows = pl.ds(pl.multiple_of(i * FF_CHUNK, FF_CHUNK), FF_CHUNK)
        up_t[:, rows] = jnp.transpose(up_w[rows, :])
        share = pl.ds(pl.multiple_of(i * OUT_CHUNK, OUT_CHUNK), OUT_CHUNK)
        out_t[:, share] = jnp.transpose(out_w[share, :])
        pre = dot(up_w[rows, :], normed_b)
        grad_act = dot(down_w[rows, :], scaled_s[...])
        square = pre * pre
        gate = 0.5 + 0.5 * jnp.tanh(pre * (root + (root * 0.044715) * square))
        activated = pre * gate
        slope = gate + activated * (1.0 - gate) * (
            2.0 * root + (6.0 * root * 0.044715) * square
        )
        at = pl.ds(i * groups, groups)
        act_s[at] = activated.astype(BF).reshape(groups, QUAD, GROUP, width)
        pre_s[at] = (grad_act * slope).astype(BF).reshape(groups, QUAD, GROUP, width)
        return carry

    for load in loads[8:11]:
        load.wait()
    lax.fori_loop(0, FF // FF_CHUNK, ffn_chunk, 0)

    share = FF // QUAD
    grad_down = dot_rows(act_s[:, own].reshape(share, width), scaled_s[...])
    result[:, 2 * GROUP : 3 * GROUP, :] = grad_down.astype(BF).reshape(DESTS, GROUP, D)
    grad_up = dot_rows(pre_s[:, own].reshape(share, width), normed_b)
    result[:, GROUP : 2 * GROUP, :] = grad_up.astype(BF).reshape(DESTS, GROUP, D)

    grad_normed = dot(up_t[...], pre_s[...].reshape(FF, width))
    grad_resid = (
        scaled_s[...].astype(F32)
        + second_inv
        * (
            grad_normed
            - jnp.mean(grad_normed, axis=0, keepdims=True)
            - second_norm * jnp.mean(grad_normed * second_norm, axis=0, keepdims=True)
        )
    ).astype(BF)
    gr_s[...] = grad_resid.reshape(HEADS, QUAD, GROUP, width)
    gmix_s[...] = dot(out_t[...], grad_resid).astype(BF)

    def backward_head(step, carry):
        h = step // 2
        cols = columns(step % 2)
        rows = pl.ds(pl.multiple_of(h * HEAD_DIM, HEAD_DIM), HEAD_DIM)
        query, key, value, grad_mixed = [
            parts(ref, rows, cols) for ref in (query_s, key_s, value_s, gmix_s)
        ]
        saved = probs_s[step]
        prob = lambda t, u: saved[t * TOKS + u : t * TOKS + u + 1, :]
        weights = []
        grad_query = []
        for t in range(TOKS):
            grad_probs = [
                jnp.sum(grad_mixed[t] * value[u], axis=0, keepdims=True) for u in range(TOKS)
            ]
            inner = sum(prob(t, u) * grad_probs[u] for u in range(TOKS))
            weight = [
                (prob(t, u) * (grad_probs[u] - inner) * score_scale).astype(BF).astype(F32)
                for u in range(TOKS)
            ]
            weights.append(weight)
            grad_query.append(sum(weight[u] * key[u] for u in range(TOKS)))
        grad_key = [sum(weights[t][u] * query[t] for t in range(TOKS)) for u in range(TOKS)]
        grad_value = [
            sum(prob(t, u).astype(BF).astype(F32) * grad_mixed[t] for t in range(TOKS))
            for u in range(TOKS)
        ]
        for ref, pieces in ((gq_s, grad_query), (gk_s, grad_key), (gv_s, grad_value)):
            for t in range(TOKS):
                ref[h, :, :, cols[t]] = pieces[t].astype(BF).reshape(QUAD, GROUP, BLK)
        return carry

    lax.fori_loop(0, 2 * HEADS, backward_head, 0)
    share = D // QUAD
    stacked = jnp.concatenate(
        [ref[:, own].reshape(share, width) for ref in (gq_s, gk_s, gv_s)], axis=0
    )
    count = HEADS * 3
    loads[11].wait()
    result[:count, 0:GROUP, :] = dot_rows(stacked, normed_s[...]).astype(BF).reshape(count, GROUP, D)
    sum_out = dot_rows(gr_s[:, own].reshape(share, width), mixed_s[...])
    result[count:, 0:GROUP, :] = sum_out.astype(BF).reshape(HEADS, GROUP, D)


def in_vmem(array):
    return pltpu.with_memory_space_constraint(array, pltpu.VMEM)


def in_hbm(array):
    return pltpu.with_memory_space_constraint(array, pltpu.HBM)


def layer(final, known, place, *weights):
    width = TOKS * QUAD_NODES
    square = pltpu.VMEM((D, width), BF)
    grouped = pltpu.VMEM((HEADS, QUAD, GROUP, width), BF)
    wide = pltpu.VMEM((DESTS, QUAD, GROUP, width), BF)
    vmem = pl.BlockSpec(memory_space=pltpu.VMEM)
    hbm = pl.BlockSpec(memory_space=pltpu.HBM)
    smem = pl.BlockSpec(memory_space=pltpu.SMEM)
    return pl.pallas_call(
        layer_kernel,
        out_shape=jax.ShapeDtypeStruct((DESTS, 3 * GROUP, D), BF),
        in_specs=[vmem] + [hbm] * 6 + [smem] + [hbm] * 6,
        out_specs=vmem,
        scratch_shapes=[
            square, square, square, square,
            pltpu.VMEM((2 * HEADS, TOKS * TOKS, BLK), F32),
            wide, wide, square, grouped, grouped, grouped, grouped,
            *[pltpu.VMEM(w.shape, BF) for w in weights],
            pltpu.VMEM((D, D), BF),
            pltpu.VMEM((D, FF), BF),
            square, square, square,
            pltpu.SemaphoreType.DMA((12,)),
        ],
        compiler_params=params(48),
        name="layer",
    )(final, *[in_hbm(k) for k in known], place, *[in_hbm(w) for w in weights])


def sum_kernel(gathered, *outs):
    total = jnp.sum(gathered[...].astype(F32), axis=0)
    for index, out in enumerate(outs):
        out[...] = total[index * GROUP : (index + 1) * GROUP]


def sum_parts(gathered):
    return pl.pallas_call(
        sum_kernel,
        out_shape=[jax.ShapeDtypeStruct((GROUP, D), F32)] * 3,
        compiler_params=params(8),
        name="sum_parts",
    )(gathered)


def exchange(array, axes):
    return lax.all_to_all(array, axes, split_axis=0, concat_axis=0, tiled=True)


def on_device(
    features, edge_tiles, block_lists, send_lists, train_ids, owners, cotangent,
    query_weight, key_weight, value_weight, out_weight, up_weight, down_weight,
):
    ids = train_ids.reshape(1, TRAIN)
    grads = lax.all_gather(cotangent.reshape(TOKS * FEATS, TRAIN), NARROW_AXES)
    owner_row = owners.reshape(1, TRAIN)
    send_slots = jnp.transpose(send_lists, (0, 2, 1))
    outgoing, counts = pack(send_slots, features, owner_row)
    counts = lax.all_gather(counts, WIDE)
    incoming = exchange(outgoing, WIDE)
    step = functools.partial(apply, jnp.transpose(block_lists), send_slots)
    current = features
    hops = None
    fields = [features]
    for hop in range(HOPS):
        if hop == 0:
            once, outgoing, degree, tiles = step(edge_tiles, current, incoming, stage=True)
        elif hop == HOPS - 1:
            once, outgoing, tiles = step(
                edge_tiles, current, incoming, degree, hop=hop, stage=True
            )
        else:
            once, outgoing = step(tiles, current, incoming, degree, hop=hop)
        incoming = exchange(outgoing, WIDE)
        results = step(
            tiles, once, incoming, degree, previous=current, hops=hops, hop=hop,
            ids=None if hop == 0 else ids,
            others=tuple(fields) if hop == HOPS - 2 else (),
        )
        current, hops = results[0], results[1]
        fields.append(current)
        if hop == HOPS - 2:
            early = lax.all_gather(results[3], NARROW_AXES)
        if hop < HOPS - 1:
            incoming = exchange(results[2], WIDE)
    final = exchange(results[2], NARROW_AXES)
    place = jnp.stack(
        [2 * lax.axis_index("xl") + lax.axis_index("c"), lax.axis_index("xh")]
    ).astype(jnp.int32)
    known = early_part(
        place, early, grads, counts, owner_row, query_weight, key_weight, value_weight
    )
    partial = layer(
        final, known, place,
        query_weight, key_weight, value_weight, out_weight, up_weight, down_weight,
    )
    gathered = exchange(partial, QUADS)
    return (hops, *sum_parts(gathered))


def solution(mesh):
    split = Mesh(mesh.devices.reshape(4, 4, 2, 2, 2), ("z", "y", "xh", "xl", "c"))
    rows = P(WIDE + NARROW_AXES, None)
    in_specs = (
        P(NARROW_AXES, WIDE),
        P(WIDE, None, None, None),
        P(WIDE, None),
        P(WIDE, None, None),
        P(WIDE),
        P(WIDE, None),
        P(None, NARROW_AXES, WIDE),
        P(), P(), P(), P(), P(), P(),
    )
    out_specs = (P(None, NARROW_AXES, WIDE), rows, rows, rows)
    return jax.shard_map(
        on_device, mesh=split, in_specs=in_specs, out_specs=out_specs, check_vma=False
    )
```
